256 devices in a mesh: gx: 4 (over y), gy: 8 (over z), gz: 8 (over x, core).
Axes of the slice: x: 4, y: 4, z: 8, core: 2. Of those that a mesh axis runs over, the one named last changes fastest.
Arguments:
- boxes: bfloat16 [4, 8, 8, 16, 16, 256], P('gx', 'gy', 'gz'), may hold values from 0 to 2
- anchors: int32 [4, 8, 8, 16, 3], P('gx', 'gy', 'gz'), may hold values from 0 to 4, as said below
- potential: float32 [160, 320, 320], P('gx', 'gy', 'gz'), may hold values from 0.5 to 2
Outputs:
- relaxed: bfloat16 [4, 8, 8, 16, 16, 256], P('gx', 'gy', 'gz')
The draws below stay inside these ranges and needn't reach their ends.
Inputs may be any that keep to these rules, and one draw needn't show every extreme that they name: `anchors`: in every region exactly 8 of the 16 functions are border functions, and every coordinate of theirs is 0 or 4; all coordinates of the others lie within 1 to 3.
All inputs are finite; a program needn't handle non-finite values.
Results may differ from the reference program's by a relative error of at most 0.0041.
Values may be sent and summed in bfloat16 or wider, within the bound.
No kernel may reach another device: no remote copies, remote signals or barrier semaphores. Data moves between devices by JAX's collectives and lax.ppermute only.
A program may use at most 128 MiB of HBM per device.

```python
import math
import jax
import jax.numpy as jnp
from jax import lax

FUNCS = 16
EXPORT = 8
REGION = 5
BOX = 16
SWEEPS = 2
RCELLS = 40
GRIDX = 4
GRIDY = 8
GRIDZ = 8
CELLSX = 160
CELLSY = 320
CELLSZ = 320


def draw_anchors(key, part):
    key_inside, key_value, key_order = jax.random.split(key, 3)
    grid_shape = (GRIDX, GRIDY, GRIDZ, FUNCS)
    inside_pos = jax.random.randint(key_inside, grid_shape + (3,), 1, REGION - 1)
    touching_pos = jax.random.randint(key_value, grid_shape + (3,), 0, 2) * (REGION - 1)
    scores = jax.random.randint(key_order, grid_shape, 0, 1 << 20) * FUNCS + jnp.arange(FUNCS, dtype=jnp.int32)
    ranking = jnp.argsort(jnp.argsort(scores, axis=-1, stable=True), axis=-1, stable=True)
    return jnp.where((ranking < EXPORT)[..., None], touching_pos, inside_pos).astype(jnp.int32)


def block_scale(key, dims, pieces, low, top_value):
    gain = 1.0
    for dim, shards_of in pieces:
        draws = jax.random.uniform(jax.random.fold_in(jax.random.fold_in(key, 6), dim), (shards_of,), jnp.float32, low / len(pieces), top_value / len(pieces))
        gain = gain * jnp.repeat(jnp.exp(draws), dims[dim] // shards_of).reshape((-1,) + (1,) * (len(dims) - 1 - dim))
    return gain


def setup_inputs(seed: int = 0) -> dict:
    key_list = jax.random.split(jax.random.key(seed), 4)
    return {
        "boxes": jnp.clip(2.0 * jax.random.uniform(key_list[0], (GRIDX, GRIDY, GRIDZ, FUNCS, BOX, BOX * BOX), jnp.float32) ** block_scale(key_list[0], (GRIDX, GRIDY, GRIDZ, FUNCS, BOX, BOX * BOX), ((0, 4), (1, 8), (2, 8)), -0.2, 0.2), 0.0, 2.0).astype(jnp.bfloat16),
        "anchors": draw_anchors(jax.random.fold_in(key_list[3], 71), 0),
        "potential": jnp.clip(jnp.exp(math.log(2.0) - 1.3862944 * jax.random.uniform(key_list[2], (CELLSX, CELLSY, CELLSZ), jnp.float32) ** block_scale(key_list[2], (CELLSX, CELLSY, CELLSZ), ((0, 4), (1, 8), (2, 8)), -0.2, 0.2)), 0.5, 2.0),
    }


MAGIC = [8.4334247333529341e-7, -1.2905572013420610e-5, 8.7629844762105596e-5, -3.0158038132690463e-4, 1.7472371367299390e-3, -9.4204703020108039e-3, 2.3738214637249424e-2, 6.1262589583120798e-2, 0.9940415697834004, -6.0489528919698352e-2, -2.1030251609303814e-2, 1.3372634148547948e-2, -3.4412814449349386e-3, 4.9443227688689919e-4, -5.1859868811734329e-5, 2.7273449291197966e-6]
KINETIC = [-3.5536922899131902, 2.2191465938911164, -0.6156141465570069, 0.2371780582153806, -0.0822663999742123, 0.0220702918848226, -4.0976568934263382e-3, 4.5167920287502235e-4, -2.3982285245075997e-5, 2.0904234952920366e-6, -3.7230763047369276e-7, -1.0585705549674147e-8, -5.8138798302825405e-11, 2.7080049362631944e-13, -6.9244749406392002e-18]
CELL = 1.0 / 4096.0
STEP = 0.1
PENALTY = 3.0


def magic_table(amount):
    row_ids = jnp.arange(amount)[:, None]
    col_ids = jnp.arange(amount)[None, :]
    offset = col_ids - row_ids + 8
    coeffs = jnp.array(MAGIC, dtype=jnp.float32)
    picked = coeffs[jnp.clip(offset, 0, 15)]
    return jnp.where((offset >= 0) & (offset < 16), picked, jnp.zeros_like(picked))


def kinetic_table(amount):
    row_ids = jnp.arange(amount)[:, None]
    col_ids = jnp.arange(amount)[None, :]
    distance = jnp.abs(col_ids - row_ids)
    coeffs = jnp.array(KINETIC, dtype=jnp.float32)
    picked = coeffs[jnp.clip(distance, 0, 14)]
    return jnp.where(distance < 15, picked, jnp.zeros_like(picked))


def apply_hamiltonian(values, potential_box):
    highest = lax.Precision.HIGHEST
    amount = values.shape[1]
    magic = magic_table(amount)
    second = kinetic_table(amount)
    identity_small = jnp.eye(amount, dtype=jnp.float32)
    magic_pair = jnp.kron(magic, magic)
    second_pair = jnp.kron(second, identity_small) + jnp.kron(identity_small, second)
    on_grid = jnp.einsum("xw,fwc->fxc", magic, values, precision=highest)
    on_grid = jnp.einsum("dc,fxc->fxd", magic_pair, on_grid, precision=highest)
    weighted = potential_box * on_grid
    returned = jnp.einsum("wx,fwc->fxc", magic, weighted, precision=highest)
    returned = jnp.einsum("cd,fxc->fxd", magic_pair, returned, precision=highest)
    kinetic = jnp.einsum("xw,fwc->fxc", second, values, precision=highest)
    kinetic = kinetic + jnp.einsum("dc,fxc->fxd", second_pair, values, precision=highest)
    return returned - 0.5 * kinetic


def border_rows(anchor_rows):
    amount = anchor_rows.shape[0]
    touching = jnp.any((anchor_rows == 0) | (anchor_rows == REGION - 1), axis=1).astype(jnp.int32)
    ranking = jnp.cumsum(touching) - touching
    places = jnp.arange(EXPORT, dtype=jnp.int32)
    matched = (touching[None, :] == 1) & (ranking[None, :] == places[:, None])
    numbers = jnp.arange(amount, dtype=jnp.int32)[None, :]
    return jnp.sum(jnp.where(matched, numbers, 0), axis=1).astype(jnp.int32)


def octants(values):
    amount = values.shape[0]
    half_width = values.shape[1] // 2
    split_up = values.reshape(amount, 2, half_width, 2, half_width, 2, half_width)
    return split_up.transpose(0, 1, 3, 5, 2, 4, 6).reshape(amount * 8, half_width ** 3)


def from_octants(values, amount, width):
    half_width = width // 2
    split_up = values.reshape(amount, 2, 2, 2, half_width, half_width, half_width)
    return split_up.transpose(0, 1, 4, 2, 5, 3, 6).reshape(amount, width, width * width)


def octant_mask(left_anchor, right_anchor):
    labels = jnp.arange(8, dtype=jnp.int32)
    corner_bits = jnp.stack([labels // 4, (labels // 2) % 2, labels % 2], axis=1)
    left_place = left_anchor[:, None, :] + corner_bits[None]
    right_place = right_anchor[:, None, :] + corner_bits[None]
    result = jnp.ones((left_anchor.shape[0], 8, right_anchor.shape[0], 8), jnp.float32)
    for dimension in range(3):
        equal = left_place[:, :, None, None, dimension] == right_place[None, None, :, :, dimension]
        result = result * equal.astype(jnp.float32)
    return result


def combine(current, own_anchor, applied, cand_boxes, cand_anchor):
    func_count = current.shape[0]
    cand_count = cand_boxes.shape[0]
    width = current.shape[1]
    stacked = octants(jnp.concatenate([current, applied.astype(jnp.bfloat16)], axis=0))
    columns = octants(cand_boxes)
    products = jnp.einsum("ak,bk->ab", stacked.astype(jnp.float32), columns.astype(jnp.float32), precision=lax.Precision.HIGHEST)
    products = products.reshape(2, func_count, 8, cand_count, 8)
    geometry = octant_mask(own_anchor, cand_anchor)
    intersection = CELL * jnp.sum(products * geometry[None], axis=(2, 4))
    identity = (jnp.arange(func_count)[:, None] == jnp.arange(cand_count)[None, :]).astype(jnp.float32)
    coupling = intersection[1] - PENALTY * (intersection[0] - identity)
    weights = (coupling[:, None, :, None] * geometry).astype(jnp.bfloat16).reshape(func_count * 8, cand_count * 8)
    correction = jnp.dot(weights, columns, preferred_element_type=jnp.float32)
    correction = from_octants(correction, func_count, width)
    return (current.astype(jnp.float32) - STEP * (applied - correction)).astype(jnp.bfloat16)


def reference(boxes, anchors, potential):
    width = boxes.shape[4]
    half_width = width // 2
    func_count = boxes.shape[3]
    region_count = GRIDX * GRIDY * GRIDZ
    padded = jnp.concatenate([potential, potential[:half_width]], axis=0)
    padded = jnp.concatenate([padded, padded[:, :half_width]], axis=1)
    padded = jnp.concatenate([padded, padded[:, :, :half_width]], axis=2)
    flat_anchor = anchors.reshape(region_count, func_count, 3)
    chosen_all = jax.vmap(border_rows)(flat_anchor)
    exported_anchor = jnp.take_along_axis(flat_anchor, chosen_all[:, :, None], axis=1).reshape(GRIDX, GRIDY, GRIDZ, EXPORT, 3)
    current_all = boxes
    for sweep_index in range(SWEEPS):
        exported = jnp.take_along_axis(current_all.reshape(region_count, func_count, width, width * width), chosen_all[:, :, None, None], axis=1)
        exported = exported.reshape(GRIDX, GRIDY, GRIDZ, EXPORT, width, width * width)
        previous = current_all

        def one_region(region):
            place_x = region // (GRIDY * GRIDZ)
            place_y = (region // GRIDZ) % GRIDY
            place_z = region % GRIDZ
            current = previous[place_x, place_y, place_z]
            own_anchor = anchors[place_x, place_y, place_z]
            corner = jnp.stack([place_x, place_y, place_z]).astype(jnp.int32) * RCELLS

            def cut_box(anchor_row):
                start = corner + half_width * anchor_row
                return lax.dynamic_slice(padded, (start[0], start[1], start[2]), (width, width, width))

            potential_box = jax.vmap(cut_box)(own_anchor).reshape(func_count, width, width * width)
            applied = apply_hamiltonian(current.astype(jnp.float32), potential_box)
            piece_boxes = [current]
            piece_anchor = [own_anchor]
            for step_x in (-1, 0, 1):
                for step_y in (-1, 0, 1):
                    for step_z in (-1, 0, 1):
                        if (step_x, step_y, step_z) != (0, 0, 0):
                            near_x = (place_x + step_x) % GRIDX
                            near_y = (place_y + step_y) % GRIDY
                            near_z = (place_z + step_z) % GRIDZ
                            piece_boxes.append(exported[near_x, near_y, near_z])
                            moved = REGION * jnp.array([step_x, step_y, step_z], dtype=jnp.int32)
                            piece_anchor.append(exported_anchor[near_x, near_y, near_z] + moved[None, :])
            cand_boxes = jnp.concatenate(piece_boxes, axis=0)
            cand_anchor = jnp.concatenate(piece_anchor, axis=0)
            return combine(current, own_anchor, applied, cand_boxes, cand_anchor)

        current_all = lax.map(one_region, jnp.arange(region_count, dtype=jnp.int32)).reshape(boxes.shape)
    return current_all
```

```python
import functools

import jax
import jax.numpy as jnp
import ml_dtypes
import numpy as np
from jax import lax
from jax.experimental import pallas as pl
from jax.experimental.pallas import tpu as pltpu
from jax.sharding import PartitionSpec as P

F32 = jnp.float32
BF16 = jnp.bfloat16

MAGIC = [
    8.433424733352934e-07,
    -1.290557201342061e-05,
    8.76298447621056e-05,
    -0.00030158038132690465,
    0.001747237136729939,
    -0.009420470302010804,
    0.023738214637249424,
    0.0612625895831208,
    0.9940415697834004,
    -0.06048952891969835,
    -0.021030251609303816,
    0.013372634148547948,
    -0.0034412814449349387,
    0.0004944322768868992,
    -5.185986881173433e-05,
    2.7273449291197967e-06,
]
KINETIC = [
    -3.55369228991319,
    2.2191465938911166,
    -0.6156141465570069,
    0.2371780582153806,
    -0.0822663999742123,
    0.0220702918848226,
    -0.004097656893426338,
    0.00045167920287502236,
    -2.3982285245075998e-05,
    2.0904234952920368e-06,
    -3.7230763047369276e-07,
    -1.0585705549674146e-08,
    -5.8138798302825405e-11,
    2.7080049362631943e-13,
    -6.9244749406392e-18,
]
CELL = 1.0 / 4096.0
STEP = 0.1
PENALTY = 3.0

META = 128
VBLOCK = 16
VEDGE = (0, 1, 4)


def split_parts(values):
    high = values.astype(ml_dtypes.bfloat16)
    low = (values - high.astype(np.float64)).astype(ml_dtypes.bfloat16)
    return high, low


@functools.cache
def tables():
    out = {}
    magic = np.zeros((16, 16))
    kinetic = np.zeros((16, 16))
    for r in range(16):
        for c in range(16):
            if 0 <= c - r + 8 < 16:
                magic[r, c] = MAGIC[c - r + 8]
            if abs(c - r) < 15:
                kinetic[r, c] = KINETIC[abs(c - r)]
    eye = np.eye(16)
    row_of = np.array(
        [f * 16 + px * 8 + x8 for x8 in range(8) for f in range(16) for px in range(2)]
    )
    lane_of = np.array(
        [
            (py * 8 + y8) * 16 + pz * 8 + z8
            for py in range(2)
            for pz in range(2)
            for y8 in range(8)
            for z8 in range(8)
        ]
    )
    full = np.eye(256)
    prow = full[row_of]
    pcol = full[:, lane_of]
    out["prow"], out["prow_t"] = prow, prow.T
    out["pcol"], out["pcol_t"] = pcol, pcol.T
    pair = np.kron(magic, magic)[np.ix_(lane_of, lane_of)]
    out["yz_h"], out["yz_l"] = split_parts(pair.T.copy())
    out["yzt_h"], out["yzt_l"] = split_parts(pair)
    along = np.kron(eye, magic)[np.ix_(row_of, row_of)]
    out["x_h"], out["x_l"] = split_parts(along)
    out["xt_h"], out["xt_l"] = split_parts(along.T.copy())
    second = (np.kron(kinetic, eye) + np.kron(eye, kinetic))[np.ix_(lane_of, lane_of)]
    out["kyz_h"], out["kyz_l"] = split_parts(-0.5 * second)
    along = np.kron(eye, kinetic)[np.ix_(row_of, row_of)]
    out["kx_h"], out["kx_l"] = split_parts(-0.5 * along)

    octs = [(py, pz, f, px) for py in range(2) for pz in range(2) for f in range(16) for px in range(2)]
    func = np.array([o[2] for o in octs])
    spread = np.zeros((128, 128))
    spread[np.arange(128), func] = 1
    out["spread"], out["spread_t"] = spread, spread.T
    corner = np.zeros((128, 128))
    corner[:, 0] = [o[3] for o in octs]
    corner[:, 1] = [o[0] for o in octs]
    corner[:, 2] = [o[1] for o in octs]
    out["corner"], out["corner_t"] = corner, corner.T[:8]
    before = np.zeros((128, 128))
    for r in range(128):
        if octs[r][0] == octs[r][1] == octs[r][3] == 0:
            before[r] = func > func[r]
    out["before"] = before
    same = func[:, None] == func[None, :]
    out["same"] = same
    exported = [(qx, qy, qz, k) for qx in range(2) for qy in range(2) for qz in range(2) for k in range(8)]
    out["octant_eq"] = [[e[:3] == (o[3], o[0], o[1]) for o in octs] for e in exported]
    slot = np.array([e[3] for e in exported])
    out["same_slot"] = slot[:, None] == slot[None, :]
    d_rows = {}
    xm = [((-1, 0, 0), q, k) for q in range(4) for k in range(8)]
    xp = [((1, 0, 0), q, k) for q in range(4) for k in range(8)]

    def moved(rows, axis, step, groups, keep):
        size = len(rows) // groups
        kept = []
        for g in range(keep, groups, 2):
            kept += rows[g * size : (g + 1) * size]
        done = []
        for d, q, k in kept:
            d = list(d)
            d[axis] += step
            done.append((tuple(d), q, k))
        return done

    own = [((0, 0, 0), q, k) for q in range(8) for k in range(8)]

    def y_rows(step):
        keep = 1 if step < 0 else 0
        return (
            moved(own, 1, step, 4, keep)
            + moved(xm, 1, step, 2, keep)
            + moved(xp, 1, step, 2, keep)
        )

    ym, yp = y_rows(-1), y_rows(1)

    def z_rows(step):
        keep = 1 if step < 0 else 0
        rows = []
        for part in (own, xm, xp, ym, yp):
            rows += moved(part, 2, step, len(part) // 8, keep)
        return rows

    cand = xm + xp + ym + yp + z_rows(-1) + z_rows(1)
    count = len(cand)
    away = np.zeros((count, META))
    away[:, :3] = [[5 * c for c in d] for d, q, k in cand]
    out["away"] = away
    names = [(d, k) for d, q, k in cand]
    out["same_cand"] = [[a == b for b in names] for a in names]
    out["eye8"] = np.eye(8, META)
    lift = np.zeros((8, 40, 384))
    for y8 in range(8):
        for z in range(40):
            lift[y8, z, (z // 8) * 64 + y8 * 8 + z % 8] = 1
    out["lift"] = lift
    regroup = np.zeros((320, 200))
    for x8 in range(8):
        for x in range(5):
            for y in range(5):
                regroup[x8 * 40 + x * 8 + y, (x * 8 + x8) * 5 + y] = 1
    out["regroup"] = regroup
    faces = np.zeros((3 * VBLOCK, 200))
    codes = np.full(200 + VBLOCK + 2 * VBLOCK + 4 * VBLOCK, -1.0)
    places = {}
    for z in range(5):
        for x in range(5):
            for y in range(5):
                codes[z * 40 + x * 8 + y] = 36 * x + 6 * y + z
                places[x, y, z] = z * 40 + x * 8 + y
    blocks = []
    for axis in range(3):
        block = []
        for a in VEDGE:
            for b in VEDGE:
                place = [a, b]
                place.insert(axis, 0)
                faces[axis * VBLOCK + len(block), places[tuple(place)]] = 1
                block.append(tuple(place))
        blocks.append(block + [None] * (VBLOCK - len(block)))

    def carried(block, axis):
        done = []
        for place in block:
            if place is None or place[axis] != 0:
                done.append(None)
            else:
                done.append(place[:axis] + (5,) + place[axis + 1 :])
        return done

    vx = carried(blocks[0], 0)
    vy = carried(blocks[1], 1) + carried(vx, 1)
    vz = carried(blocks[2], 2) + carried(vx, 2) + carried(vy, 2)
    for number, place in enumerate(vx + vy + vz):
        if place is not None:
            codes[200 + number] = 36 * place[0] + 6 * place[1] + place[2]
    assert sorted(c for c in codes if c >= 0) == sorted(set(codes[codes >= 0]))
    out["faces"] = faces
    out["v_codes"] = np.broadcast_to(codes, (8, codes.size))
    keep32 = ("v_codes",)
    return {
        k: np.ascontiguousarray(v, dtype=np.float32 if k in keep32 else ml_dtypes.bfloat16)
        for k, v in out.items()
    }


def dot(a, b):
    return lax.dot_general(a, b, (((1,), (0,)), ((), ())), preferred_element_type=F32)


def dot_nt(a, b):
    return lax.dot_general(a, b, (((1,), (1,)), ((), ())), preferred_element_type=F32)


def halves(values):
    high = values.astype(BF16)
    low = (values - high.astype(F32)).astype(BF16)
    return high, low


def rolled(values):
    return pltpu.roll(values, 64, 1)


def low_lanes(values):
    return lax.broadcasted_iota(jnp.int32, values.shape, 1) < 64


def to_octants(split, roll=rolled):
    rows = split.shape[0] // 8
    blocks = []
    for py in range(split.shape[1] // 128):
        here = split[:, py * 128 : (py + 1) * 128]
        other = roll(here)
        for pz in range(2):
            pieces = []
            for x8 in range(0, 8, 2):
                one = slice(x8 * rows, (x8 + 1) * rows)
                two = slice((x8 + 1) * rows, (x8 + 2) * rows)
                if pz == 0:
                    left, right = here[one], other[two]
                else:
                    left, right = other[one], here[two]
                pieces.append(jnp.where(low_lanes(left), left, right))
            blocks.append(jnp.concatenate(pieces, axis=1))
    return blocks


def to_split(octant, roll=rolled):
    columns = []
    for py in range(2):
        first = octant[(2 * py) * 32 : (2 * py + 1) * 32]
        second = octant[(2 * py + 1) * 32 : (2 * py + 2) * 32]
        pieces = []
        for pair in range(4):
            lanes = slice(pair * 128, (pair + 1) * 128)
            one, two = first[:, lanes], second[:, lanes]
            pieces.append(jnp.where(low_lanes(one), one, roll(two)))
            pieces.append(jnp.where(low_lanes(one), roll(one), two))
        columns.append(jnp.concatenate(pieces, axis=0))
    return jnp.concatenate(columns, axis=1)


def mix(high_low, values):
    high, low = halves(values)
    return dot(high_low[0], high) + (dot(high_low[0], low) + dot(high_low[1], high))


def mix_right(values, high_low):
    high, low = halves(values)
    return dot(high, high_low[0]) + (dot(low, high_low[0]) + dot(high, high_low[1]))


def octant_places(anc, anc_t, t):
    by_row = dot(t["spread"], anc) + t["corner"].astype(F32)
    base = dot(anc_t, t["spread_t"])
    by_lane = base + t["corner_t"].astype(F32)
    return by_row, base, by_lane


def code_of(x, y, z):
    return 36.0 * x + 6.0 * y + z


def export_table(base, t):
    edge = (base == 0.0) | (base == 4.0)
    edge = edge[0:1] | edge[1:2] | edge[2:3]
    edge = edge.astype(F32)
    rank = dot(jnp.broadcast_to(edge, (8, 128)).astype(BF16), t["before"])[0:1]
    slot = lax.broadcasted_iota(jnp.int32, (64, 128), 0) % 8
    chosen = (rank == slot.astype(F32)) & (edge > 0.5)
    return jnp.where(chosen, t["octant_eq"].astype(F32), 0.0).astype(BF16)


PACK = ("prow", "pcol", "spread", "corner", "spread_t", "corner_t", "before", "octant_eq", "lift", "regroup", "faces")


def pack_body(boxes, anc, anc_t, potential_rows, t, roll=rolled):
    split = dot(dot(t["prow"], boxes).astype(BF16), t["pcol"])
    octant = jnp.concatenate(to_octants(split, roll), axis=0).astype(BF16)
    by_row, base, _ = octant_places(anc, anc_t, t)
    table = export_table(base, t)
    exported = dot(table, octant).astype(BF16)
    meta = dot(table, by_row.astype(BF16)).astype(BF16)
    exported = jnp.concatenate([exported, meta], axis=1)
    lifted = None
    for y8 in range(8):
        part = dot(potential_rows(y8).astype(BF16), t["lift"][y8])
        lifted = part if lifted is None else lifted + part
    regrouped = dot(t["regroup"], lifted.astype(BF16))
    v_rows = jnp.concatenate(to_octants(regrouped, roll)[:5], axis=0).astype(BF16)
    v_faces = dot(t["faces"], v_rows).astype(BF16)
    v_faces = jnp.concatenate([v_faces, jnp.zeros((3 * VBLOCK, META), BF16)], axis=1)
    return split.astype(BF16), octant, exported, v_rows, v_faces


OPERATE = ("yz_h", "yz_l", "yzt_h", "yzt_l", "x_h", "x_l", "xt_h", "xt_l", "kyz_h", "kyz_l", "kx_h", "kx_l")


def operate(split, v_box, t, roll=rolled):
    inner = dot(split, t["yz_h"]) + dot(split, t["yz_l"])
    grid = mix((t["x_h"], t["x_l"]), inner)
    octant = jnp.concatenate(to_octants(grid, roll), axis=0) * v_box
    weighted = to_split(octant, roll)
    returned = mix((t["xt_h"], t["xt_l"]), mix_right(weighted, (t["yzt_h"], t["yzt_l"])))
    kinetic = (dot(split, t["kyz_h"]) + dot(split, t["kyz_l"])) + (
        dot(t["kx_h"], split) + dot(t["kx_l"], split)
    )
    return jnp.concatenate(to_octants(returned + kinetic, roll), axis=0)


def own_weights(octant, applied_bf, geometry, t):
    products = dot_nt(applied_bf, octant) - PENALTY * dot_nt(octant, octant)
    high, low = halves(products * (geometry * CELL))
    rows = dot(t["same"], high) + dot(t["same"], low)
    high, low = halves(rows)
    coupling = dot(high, t["same"]) + dot(low, t["same"])
    coupling = coupling + PENALTY * t["same"].astype(F32)
    return (coupling * geometry).astype(BF16)


def near_weights(table, exported, applied_bf, cand, geometry, t):
    applied_rows = dot(table, applied_bf).astype(BF16)
    products = dot_nt(applied_rows, cand) - PENALTY * dot_nt(exported, cand)
    high, low = halves(products * (geometry * CELL))
    rows = dot(t["same_slot"], high) + dot(t["same_slot"], low)
    high, low = halves(rows)
    coupling = dot(high, t["same_cand"]) + dot(low, t["same_cand"])
    return (coupling * geometry).astype(BF16)


FIRST = OPERATE + (
    "spread", "corner", "spread_t", "corner_t", "before", "octant_eq",
    "same", "same_slot", "same_cand", "away", "eye8", "v_codes",
)


def first_body(split, octant, exported, anc, anc_t, cand, v_rows, t, roll=rolled):
    by_row, base, by_lane = octant_places(anc, anc_t, t)
    row_code = code_of(by_row[:, 0:1], by_row[:, 1:2], by_row[:, 2:3])
    lane_code = code_of(by_lane[0:1], by_lane[1:2], by_lane[2:3])
    geometry = (row_code == lane_code).astype(F32)
    picks = (row_code == t["v_codes"][0:1]).astype(BF16)
    v_box = dot(picks, v_rows)
    applied = operate(split, v_box, t, roll)
    applied_bf = applied.astype(BF16)
    weights = own_weights(octant, applied_bf, geometry, t)
    correction = dot(weights, octant)
    table = export_table(base, t)
    places = dot_nt(t["eye8"], cand[:, 512:] + t["away"])
    mine = exported[:, 512:].astype(F32)
    near = (
        (mine[:, 0:1] == places[0:1])
        & (mine[:, 1:2] == places[1:2])
        & (mine[:, 2:3] == places[2:3])
    ).astype(F32)
    cand = cand[:, :512]
    near_w = near_weights(table, exported[:, :512], applied_bf, cand, near, t)
    spread_w = dot(table_t(table), near_w).astype(BF16)
    correction = correction + dot(spread_w, cand)
    current = octant.astype(F32) - STEP * (applied - correction)
    current = current.astype(BF16)
    sent = dot(table, current).astype(BF16)
    return current, sent, v_box.astype(BF16), geometry.astype(BF16), near.astype(BF16), table


def table_t(table):
    return table.astype(F32).T.astype(BF16)


SECOND = OPERATE + ("same",)


def second_body(octant, v_box, geometry, t, roll=rolled):
    split = to_split(octant.astype(F32), roll).astype(BF16)
    applied = operate(split, v_box.astype(F32), t, roll)
    applied_bf = applied.astype(BF16)
    weights = own_weights(octant, applied_bf, geometry.astype(F32), t)
    done = octant.astype(F32) - STEP * (applied - dot(weights, octant))
    return done, applied_bf


LAST = ("same_slot", "same_cand", "prow_t", "pcol_t")


def last_body(done, applied_bf, exported, table, cand, near, t, roll=rolled):
    near_w = near_weights(table, exported, applied_bf, cand, near.astype(F32), t)
    spread_w = dot(table_t(table), near_w).astype(BF16)
    current = (done + STEP * dot(spread_w, cand)).astype(BF16)
    split = to_split(current.astype(F32), roll).astype(BF16)
    return dot(dot(t["prow_t"], split).astype(BF16), t["pcol_t"]).astype(BF16)


def shape(dims, dtype=BF16):
    return jax.ShapeDtypeStruct(dims, dtype)


def call(body, names, out_shape, inputs, cost, name):
    consts = [tables()[k] for k in names]
    count = len(inputs)

    def kernel(*refs):
        ins = refs[:count]
        t = {k: r for k, r in zip(names, refs[count : count + len(names)])}
        body(ins, {k: Loaded(r) for k, r in t.items()}, refs[count + len(names) :])

    return pl.pallas_call(
        kernel,
        out_shape=out_shape,
        in_specs=[pl.BlockSpec(memory_space=pltpu.VMEM)] * (count + len(names)),
        out_specs=jax.tree.map(lambda _: pl.BlockSpec(memory_space=pltpu.VMEM), out_shape),
        compiler_params=pltpu.CompilerParams(vmem_limit_bytes=32 << 20),
        cost_estimate=pl.CostEstimate(flops=cost, bytes_accessed=cost // 100, transcendentals=0),
        name=name,
    )(*inputs, *consts)


def Loaded(ref):
    return ref[...]


def pack_kernel(ins, t, outs):
    boxes, anc, anc_t, potential = ins
    got = pack_body(
        boxes[...],
        anc[...],
        anc_t[...],
        lambda y8: potential[pl.ds(y8, 200, stride=8), :],
        t,
    )
    split, octant, exported, v_rows, v_faces = got
    outs[0][...] = split
    outs[1][...] = octant
    outs[2][...] = exported
    outs[3][...] = v_rows
    outs[4][...] = jnp.concatenate([exported[0:32], v_faces[0:VBLOCK]], axis=0)
    outs[5][...] = exported[32:64]
    outs[6][...] = v_faces[VBLOCK:]


def first_kernel(ins, t, outs):
    got = first_body(*[r[...] for r in ins], t)
    for ref, value in zip(outs, got):
        ref[...] = value
    outs[6][...] = got[1][0:32]
    outs[7][...] = got[1][32:64]


def second_kernel(ins, t, outs):
    for ref, value in zip(outs, second_body(*[r[...] for r in ins], t)):
        ref[...] = value


def last_kernel(ins, t, outs):
    outs[0][...] = last_body(*[r[...] for r in ins], t)


def passed_along(value, axis, step):
    count = lax.axis_size(axis)
    return lax.ppermute(value, axis, [(i, (i + step) % count) for i in range(count)])


def half_of(rows, groups, keep):
    return rows.reshape(groups // 2, 2, rows.shape[0] // groups, rows.shape[1])[:, keep].reshape(
        rows.shape[0] // 2, rows.shape[1]
    )


def exchange(exported, to_low, to_high, v_faces, send=passed_along):
    xp = send(to_low, "gx", -1)
    xm = send(to_high, "gx", 1)
    x_rows = [xm, xp[:32]]
    v_x = [xp[32:]] if v_faces is not None else []
    v_y = [v_faces[:VBLOCK]] if v_faces is not None else []
    v_z = [v_faces[VBLOCK:]] if v_faces is not None else []

    def y_part(keep):
        return [half_of(exported, 4, keep)] + [half_of(r, 2, keep) for r in x_rows]

    yp = send(jnp.concatenate(y_part(0) + v_y + v_x, axis=0), "gy", -1)
    ym = send(jnp.concatenate(y_part(1), axis=0), "gy", 1)
    y_rows = [ym, yp[:64]]
    v_y = [yp[64:]] if v_faces is not None else []

    def z_part(keep):
        return [half_of(r, r.shape[0] // 8, keep) for r in [exported] + x_rows + y_rows]

    zp = send(jnp.concatenate(z_part(0) + v_z + v_x + v_y, axis=0), "gz", -1)
    zm = send(jnp.concatenate(z_part(1), axis=0), "gz", 1)
    v_z = [zp[128:]] if v_faces is not None else []
    cand = jnp.concatenate(x_rows + y_rows + [zm, zp[:128]], axis=0)
    if v_faces is None:
        return cand
    return cand, jnp.concatenate(v_x + v_y + v_z, axis=0)[:, :512]


def local(boxes, anchors, potential):
    own = boxes.reshape(256, 256)
    anchor = anchors.reshape(16, 3).astype(BF16)
    anc = jnp.pad(anchor, ((0, 112), (0, 125)))
    anc_t = jnp.pad(anchor.T, ((0, 5), (0, 112)))
    wide = 512 + META
    split, octant, exported, v_own, to_low, to_high, v_faces = call(
        pack_kernel,
        PACK,
        (
            shape((256, 256)),
            shape((128, 512)),
            shape((64, wide)),
            shape((200, 512)),
            shape((32 + VBLOCK, wide)),
            shape((32, wide)),
            shape((2 * VBLOCK, wide)),
        ),
        (own, anc, anc_t, potential.reshape(1600, 40)),
        10**8,
        "pack",
    )
    cand, v_far = exchange(exported, to_low, to_high, v_faces)
    v_rows = jnp.concatenate([v_own, v_far], axis=0)
    current, sent, v_box, geometry, near, table, to_low, to_high = call(
        first_kernel,
        FIRST,
        (
            shape((128, 512)),
            shape((64, 512)),
            shape((128, 512)),
            shape((128, 128)),
            shape((64, 448)),
            shape((64, 128)),
            shape((32, 512)),
            shape((32, 512)),
        ),
        (split, octant, exported, anc, anc_t, cand, v_rows),
        10**9,
        "first",
    )
    cand = exchange(sent, to_low, to_high, None)
    done, applied_bf = call(
        second_kernel,
        SECOND,
        (shape((128, 512), F32), shape((128, 512))),
        (current, v_box, geometry),
        10**9,
        "second",
    )
    (relaxed,) = call(
        last_kernel,
        LAST,
        (shape((256, 256)),),
        (done, applied_bf, sent, table, cand, near),
        10**9,
        "last",
    )
    return relaxed.reshape(boxes.shape)


def solution(mesh):
    placed = (
        P("gx", "gy", "gz", None, None, None),
        P("gx", "gy", "gz", None, None),
        P("gx", "gy", "gz"),
    )
    return jax.shard_map(
        local,
        mesh=mesh,
        in_specs=placed,
        out_specs=P("gx", "gy", "gz", None, None, None),
        check_vma=False,
    )
```

```python
import functools

import jax
import jax.numpy as jnp
import ml_dtypes
import numpy as np
from jax import lax
from jax.experimental import pallas as pl
from jax.experimental.pallas import tpu as pltpu
from jax.sharding import PartitionSpec as P

F32 = jnp.float32
BF16 = jnp.bfloat16

MAGIC = [
    8.433424733352934e-07,
    -1.290557201342061e-05,
    8.76298447621056e-05,
    -0.00030158038132690465,
    0.001747237136729939,
    -0.009420470302010804,
    0.023738214637249424,
    0.0612625895831208,
    0.9940415697834004,
    -0.06048952891969835,
    -0.021030251609303816,
    0.013372634148547948,
    -0.0034412814449349387,
    0.0004944322768868992,
    -5.185986881173433e-05,
    2.7273449291197967e-06,
]
KINETIC = [
    -3.55369228991319,
    2.2191465938911166,
    -0.6156141465570069,
    0.2371780582153806,
    -0.0822663999742123,
    0.0220702918848226,
    -0.004097656893426338,
    0.00045167920287502236,
    -2.3982285245075998e-05,
    2.0904234952920368e-06,
    -3.7230763047369276e-07,
    -1.0585705549674146e-08,
    -5.8138798302825405e-11,
    2.7080049362631943e-13,
    -6.9244749406392e-18,
]
CELL = 1.0 / 4096.0
STEP = 0.1
PENALTY = 3.0

META = 128
VEDGE = (0, 1, 4)
VFACE = 16


def split_parts(values):
    high = values.astype(ml_dtypes.bfloat16)
    low = (values - high.astype(np.float64)).astype(ml_dtypes.bfloat16)
    return high, low


def candidate_rows():
    own = [((0, 0, 0), k) for q in range(8) for k in range(8)]

    def moved(rows, axis, step, groups):
        size = len(rows) // groups
        kept = []
        for g in range(1 if step < 0 else 0, groups, 2):
            kept += rows[g * size : (g + 1) * size]
        return [(d[:axis] + (d[axis] + step,) + d[axis + 1 :], k) for d, k in kept]

    parts = [own]
    for axis, groups in ((0, lambda n: 2), (1, lambda n: n // 16), (2, lambda n: n // 8)):
        here = list(parts)
        for step in (-1, 1):
            parts.append(sum((moved(p, axis, step, groups(len(p))) for p in here), []))
    return sum(parts[1:], [])


def face_places(axis):
    groups = ([], [])
    for a in VEDGE:
        for b in VEDGE:
            place = [a, b]
            place.insert(axis, 0)
            groups[0 if 0 in (a, b) else 1].append(tuple(place))
    return sum((g + [None] * (8 - len(g)) for g in groups), [])


def carried(block, axis):
    return [
        None if p is None or p[axis] != 0 else p[:axis] + (5,) + p[axis + 1 :] for p in block
    ]


@functools.cache
def tables():
    out = {}
    magic = np.zeros((16, 16))
    kinetic = np.zeros((16, 16))
    for r in range(16):
        for c in range(16):
            if 0 <= c - r + 8 < 16:
                magic[r, c] = MAGIC[c - r + 8]
            if abs(c - r) < 15:
                kinetic[r, c] = KINETIC[abs(c - r)]
    eye = np.eye(16)
    full = np.eye(256)
    row_of = np.array(
        [f * 16 + px * 8 + x8 for x8 in range(8) for px in range(2) for f in range(16)]
    )
    lane_of = np.array(
        [
            (py * 8 + y8) * 16 + pz * 8 + z8
            for py in range(2)
            for pz in range(2)
            for y8 in range(8)
            for z8 in range(8)
        ]
    )
    prow = full[row_of]
    pcol = full[:, lane_of]
    out["prow"], out["prow_t"] = prow, prow.T
    out["pcol"], out["pcol_t"] = pcol, pcol.T
    pair = np.kron(magic, magic)[np.ix_(lane_of, lane_of)] - full
    out["yz"], out["yz_t"] = pair.T, pair
    along = np.kron(eye, magic)[np.ix_(row_of, row_of)] - full
    out["x"], out["x_t"] = along, along.T
    second = (np.kron(kinetic, eye) + np.kron(eye, kinetic))[np.ix_(lane_of, lane_of)]
    out["kyz_h"], out["kyz_l"] = split_parts(-0.5 * second)
    along = np.kron(eye, kinetic)[np.ix_(row_of, row_of)]
    out["kx_h"], out["kx_l"] = split_parts(-0.5 * along)

    cand = candidate_rows()
    away = np.zeros((len(cand), META))
    away[:, :3] = [[5 * c for c in d] for d, k in cand]
    out["away"] = away
    out["same_cand"] = [[a == b for b in cand] for a in cand]
    lift = np.zeros((8, 40, 384))
    for y8 in range(8):
        for z in range(40):
            lift[y8, z, (z // 8) * 64 + y8 * 8 + z % 8] = 1
    out["lift"] = lift
    regroup = np.zeros((320, 200))
    for x8 in range(8):
        for x in range(5):
            for y in range(5):
                regroup[x8 * 40 + x * 8 + y, (x * 8 + x8) * 5 + y] = 1
    out["regroup"] = regroup
    own = [None] * 200
    for z in range(5):
        for x in range(5):
            for y in range(5):
                own[z * 40 + x * 8 + y] = (x, y, z)
    blocks = [face_places(axis) for axis in range(3)]
    faces = np.zeros((3 * VFACE, 200))
    for row, place in enumerate(sum(blocks, [])):
        if place is not None:
            faces[row, own.index(place)] = 1
    out["faces"] = faces
    vx = carried(blocks[0], 0)
    vy = carried(blocks[1] + vx[:8], 1)
    vz = carried(blocks[2] + vx[:8] + vy[:8] + vy[16:], 2)

    def coded(places):
        codes = [-1.0 if p is None else 36 * p[0] + 6 * p[1] + p[2] for p in places]
        return np.broadcast_to(np.array(codes), (8, len(codes)))

    out["codes_own"] = coded(own)
    out["codes_far"] = coded(vx + vy + vz)
    return {
        k: np.ascontiguousarray(
            v, dtype=np.float32 if k.startswith("codes") else ml_dtypes.bfloat16
        )
        for k, v in out.items()
    }


def dot(a, b):
    return lax.dot_general(a, b, (((1,), (0,)), ((), ())), preferred_element_type=F32)


def dot_nt(a, b):
    return lax.dot_general(a, b, (((1,), (1,)), ((), ())), preferred_element_type=F32)


def rolled(values):
    return pltpu.roll(values, 64, 1)


def iota(dims, axis):
    return lax.broadcasted_iota(jnp.int32, dims, axis)


def low_lanes(values):
    return iota(values.shape, 1) < 64


def to_octants(split, roll):
    rows = split.shape[0] // 8
    blocks = []
    for py in range(split.shape[1] // 128):
        here = split[:, py * 128 : (py + 1) * 128]
        other = roll(here)
        for pz in range(2):
            pieces = []
            for x8 in range(0, 8, 2):
                one = slice(x8 * rows, (x8 + 1) * rows)
                two = slice((x8 + 1) * rows, (x8 + 2) * rows)
                if pz == 0:
                    left, right = here[one], other[two]
                else:
                    left, right = other[one], here[two]
                pieces.append(jnp.where(low_lanes(left), left, right))
            blocks.append(jnp.concatenate(pieces, axis=1))
    return blocks


def to_octant(split, roll):
    return jnp.concatenate(to_octants(split, roll), axis=0)


def to_split(octant, roll):
    columns = []
    for py in range(2):
        first = octant[(2 * py) * 32 : (2 * py + 1) * 32]
        second = octant[(2 * py + 1) * 32 : (2 * py + 2) * 32]
        pieces = []
        for pair in range(4):
            lanes = slice(pair * 128, (pair + 1) * 128)
            one, two = first[:, lanes], second[:, lanes]
            pieces.append(jnp.where(low_lanes(one), one, roll(two)))
            pieces.append(jnp.where(low_lanes(one), roll(one), two))
        columns.append(jnp.concatenate(pieces, axis=0))
    return jnp.concatenate(columns, axis=1)


def octant_places(anchor):
    lane = iota((16, 128), 1)
    base = jnp.zeros((16, 128), F32)
    for c in range(3):
        base = jnp.where(lane == c, anchor[:, c : c + 1], base)
    base = jnp.concatenate([base] * 8, axis=0)
    row, lane = iota((128, 128), 0), iota((128, 128), 1)
    bit = jnp.where(lane == 0, row // 16, jnp.where(lane == 1, row // 64, row // 32)) % 2
    return base + jnp.where(lane < 3, bit, 0).astype(F32), base


def across(values):
    eye = (iota((8, 128), 0) == iota((8, 128), 1)).astype(F32).astype(BF16)
    return dot_nt(eye, values.astype(BF16))


def export_table(base):
    edge = across(base)
    edge = ((edge == 0.0) | (edge == 4.0)).astype(F32)
    edge = jnp.maximum(jnp.maximum(edge[0:1], edge[1:2]), edge[2:3])
    row, lane = iota((128, 128), 0), iota((128, 128), 1)
    before = (row < lane % 16).astype(F32).astype(BF16)
    before = jnp.where(row < 16, before, jnp.zeros_like(before))
    rank = dot(jnp.broadcast_to(edge, (8, 128)).astype(BF16), before)[0:1]
    row, lane = iota((64, 128), 0), iota((64, 128), 1)
    match = (
        (row // 32 == (lane // 16) % 2)
        & ((row // 16) % 2 == lane // 64)
        & ((row // 8) % 2 == (lane // 32) % 2)
    )
    chosen = (rank == (row % 8).astype(F32)) & (edge > 0.5)
    return (match & chosen).astype(F32).astype(BF16)


def same_function():
    return (iota((128, 128), 0) % 16 == iota((128, 128), 1) % 16).astype(F32)


def over_octants(values):
    total = values[0:16]
    for p in range(1, 8):
        total = total + values[16 * p : 16 * p + 16]
    return total


def summed(values, table):
    high = values.astype(BF16)
    low = (values - high.astype(F32)).astype(BF16)
    both = dot(jnp.concatenate([high, low], axis=0), table)
    return both[:16] + both[16:]


def repeated(values):
    return jnp.concatenate([values] * 8, axis=0)


def pack_body(boxes, anchor, potential_rows, t, roll=rolled):
    places, base = octant_places(anchor())
    table = export_table(base)
    split = dot(dot(t["prow"](), boxes()).astype(BF16), t["pcol"]())
    octant = to_octant(split, roll).astype(BF16)
    wide = jnp.concatenate([octant, places.astype(BF16)], axis=1)
    exported = dot(table, wide).astype(BF16)
    lifted = None
    for y8 in range(8):
        part = dot(potential_rows(y8).astype(BF16), t["lift"]()[y8])
        lifted = part if lifted is None else lifted + part
    regrouped = dot(t["regroup"](), lifted.astype(BF16))
    v_rows = jnp.concatenate(to_octants(regrouped, roll)[:5], axis=0).astype(BF16)
    v_faces = dot(t["faces"](), v_rows).astype(BF16)
    v_faces = jnp.concatenate([v_faces, jnp.zeros((3 * VFACE, META), BF16)], axis=1)
    return split.astype(BF16), octant, exported, v_rows, v_faces, places, table


def grid_values(split, t, roll):
    inner = split.astype(F32) + dot(split, t["yz"]())
    return to_octant(inner + dot(t["x"](), inner.astype(BF16)), roll)


def kinetic_values(split, t, roll):
    lanes = dot(split, t["kyz_h"]()) + dot(split, t["kyz_l"]())
    rows = dot(t["kx_h"](), split) + dot(t["kx_l"](), split)
    return to_octant(lanes + rows, roll)


def returned_values(weighted, t, roll):
    split = to_split(weighted, roll)
    inner = split + dot(split.astype(BF16), t["yz_t"]())
    return to_octant(inner + dot(t["x_t"](), inner.astype(BF16)), roll)


def own_weights(overlaps, applied_bf, octant, geometry):
    products = over_octants((dot_nt(applied_bf, octant) * CELL - overlaps) * geometry)
    same = same_function()
    coupling = summed(products, same.astype(BF16)) + PENALTY * same[:16]
    return (repeated(coupling) * geometry).astype(BF16)


def near_weights(octant, applied_bf, cand, near, t):
    products = dot_nt(applied_bf, cand) - PENALTY * dot_nt(octant, cand)
    coupling = summed(over_octants(products * CELL * near), t["same_cand"]())
    return (repeated(coupling) * near).astype(BF16)


AHEAD = ("yz", "x", "kyz_h", "kyz_l", "kx_h", "kx_l")


def ahead_body(split, octant, places, t, roll=rolled):
    row_code = 36.0 * places[:, 0:1] + 6.0 * places[:, 1:2] + places[:, 2:3]
    lanes = across(places)
    lane_code = 36.0 * lanes[0:1] + 6.0 * lanes[1:2] + lanes[2:3]
    geometry = (row_code == lane_code).astype(F32)
    overlaps = dot_nt(octant, octant) * (CELL * PENALTY)
    return grid_values(split, t, roll), kinetic_values(split, t, roll), overlaps, geometry


FIRST = ("yz_t", "x_t", "same_cand", "away", "codes_own", "codes_far")


def first_body(
    octant, places, table, grid, kinetic, overlaps, geometry, v_own, cand, v_far, t, roll=rolled
):
    code = 36.0 * places[:, 0:1] + 6.0 * places[:, 1:2] + places[:, 2:3]
    v_box = dot((code == t["codes_own"]()[0:1]).astype(F32).astype(BF16), v_own)
    v_box = v_box + dot((code == t["codes_far"]()[0:1]).astype(F32).astype(BF16), v_far)
    lanes = across_rows(cand[:, 512:] + t["away"]())
    near = (
        (places[:, 0:1] == lanes[0:1])
        & (places[:, 1:2] == lanes[1:2])
        & (places[:, 2:3] == lanes[2:3])
    ).astype(F32)
    cand = cand[:, :512]
    applied = returned_values(grid * v_box, t, roll) + kinetic
    applied_bf = applied.astype(BF16)
    own_w = own_weights(overlaps, applied_bf, octant, geometry)
    near_w = near_weights(octant, applied_bf, cand, near, t)
    correction = dot(own_w, octant) + dot(near_w, cand)
    current = (octant.astype(F32) - STEP * (applied - correction)).astype(BF16)
    sent = dot(table, current).astype(BF16)
    return current, sent, v_box.astype(BF16), near.astype(BF16)


def across_rows(values):
    eye = (iota((8, META), 0) == iota((8, META), 1)).astype(F32).astype(BF16)
    return dot_nt(eye, values)


SECOND = AHEAD + ("yz_t", "x_t")


def second_body(octant, v_box, geometry, t, roll=rolled):
    split = to_split(octant.astype(F32), roll).astype(BF16)
    weighted = grid_values(split, t, roll) * v_box.astype(F32)
    applied = returned_values(weighted, t, roll) + kinetic_values(split, t, roll)
    applied_bf = applied.astype(BF16)
    overlaps = dot_nt(octant, octant) * (CELL * PENALTY)
    own_w = own_weights(overlaps, applied_bf, octant, geometry)
    done = octant.astype(F32) - STEP * (applied - dot(own_w, octant))
    return done, applied_bf


def last_body(done, applied_bf, octant, cand, near, t, roll=rolled):
    near_w = near_weights(octant, applied_bf, cand, near.astype(F32), t)
    current = (done + STEP * dot(near_w, cand)).astype(BF16)
    split = to_split(current.astype(F32), roll).astype(BF16)
    return dot(dot(t["prow_t"](), split).astype(BF16), t["pcol_t"]()).astype(BF16)


def shape(dims, dtype=BF16):
    return jax.ShapeDtypeStruct(dims, dtype)


class Fetched:
    def __init__(self, source, target, semaphore):
        self.copy = pltpu.make_async_copy(source, target, semaphore)
        self.target = target
        self.waiting = True
        self.copy.start()

    def ref(self):
        if self.waiting:
            self.copy.wait()
            self.waiting = False
        return self.target

    def __call__(self):
        return self.ref()[...]


def call(name, body, out_shape, inputs, near_consts, far_inputs, far_consts, flops):
    near = list(inputs) + [jnp.asarray(tables()[k]) for k in near_consts]
    far = list(far_inputs) + [jnp.asarray(tables()[k]) for k in far_consts]
    outs = len(out_shape)

    def kernel(*refs):
        near_refs = refs[: len(near)]
        far_refs = refs[len(near) : len(near) + len(far)]
        out_refs = refs[len(near) + len(far) : len(near) + len(far) + outs]
        scratch = refs[len(near) + len(far) + outs :]
        fetched = [
            Fetched(source, target, scratch[-1].at[i])
            for i, (source, target) in enumerate(zip(far_refs, scratch[:-1]))
        ]
        t = {k: r for k, r in zip(far_consts, fetched[len(far_inputs) :])}
        for k, r in zip(near_consts, near_refs[len(inputs) :]):
            t[k] = functools.partial(lambda ref: ref[...], r)
        body(near_refs[: len(inputs)], fetched[: len(far_inputs)], t, out_refs)
        for piece in fetched:
            piece.ref()

    scratch_shapes = [pltpu.VMEM(a.shape, a.dtype) for a in far]
    if far:
        scratch_shapes.append(pltpu.SemaphoreType.DMA((len(far),)))
    return pl.pallas_call(
        kernel,
        out_shape=out_shape,
        in_specs=[pl.BlockSpec(memory_space=pltpu.VMEM)] * len(near)
        + [pl.BlockSpec(memory_space=pltpu.HBM)] * len(far),
        out_specs=tuple(pl.BlockSpec(memory_space=pltpu.VMEM) for _ in out_shape),
        scratch_shapes=scratch_shapes,
        compiler_params=pltpu.CompilerParams(vmem_limit_bytes=24 << 20),
        cost_estimate=pl.CostEstimate(
            flops=flops, bytes_accessed=flops // 1000, transcendentals=0
        ),
        name=name,
    )(*near, *far)


def pack_kernel(near, far, t, outs):
    boxes, potential, anchor = far
    split, octant, exported, v_rows, v_faces, places, table = pack_body(
        boxes,
        lambda: anchor().astype(F32),
        lambda y8: potential.ref()[pl.ds(y8, 200, stride=8), :],
        t,
    )
    outs[0][...] = split
    outs[1][...] = octant
    outs[2][...] = exported
    outs[3][...] = v_rows
    outs[4][...] = jnp.concatenate([exported[0:32], v_faces[0:VFACE]], axis=0)
    outs[5][...] = exported[32:64]
    outs[6][...] = v_faces[VFACE:]
    outs[7][...] = places
    outs[8][...] = table


def whole_kernel(body):
    def run(near, far, t, outs):
        got = body(*[r[...] for r in near], *[r() for r in far], t)
        for ref, value in zip(outs, got):
            ref[...] = value

    return run


def first_kernel(near, far, t, outs):
    got = first_body(*[r[...] for r in near], t)
    for ref, value in zip(outs, got):
        ref[...] = value
    outs[4][...] = got[1][0:32]
    outs[5][...] = got[1][32:64]


def passed_along(value, axis, step):
    count = lax.axis_size(axis)
    return lax.ppermute(value, axis, [(i, (i + step) % count) for i in range(count)])


def half_of(rows, size, keep):
    count = rows.shape[0] // (2 * size)
    return rows.reshape(count, 2, size, rows.shape[1])[:, keep].reshape(count * size, -1)


def exchange(exported, to_low, to_high, v_faces, send=passed_along):
    v_x, v_y, v_z = [], [], []
    xp = send(to_low, "gx", -1)
    xm = send(to_high, "gx", 1)
    x_rows = [xm, xp[:32]]
    if v_faces is not None:
        v_x = [xp[32:]]
        v_y = [v_faces[:VFACE], xp[32:40]]
        v_z = [v_faces[VFACE:], xp[32:40]]

    def y_part(keep):
        return [half_of(r, 16, keep) for r in [exported] + x_rows]

    yp = send(jnp.concatenate(y_part(0) + v_y, axis=0), "gy", -1)
    ym = send(jnp.concatenate(y_part(1), axis=0), "gy", 1)
    y_rows = [ym, yp[:64]]
    if v_faces is not None:
        v_y = [yp[64:]]
        v_z = v_z + [yp[64:72], yp[80:88]]

    def z_part(keep):
        return [half_of(r, 8, keep) for r in [exported] + x_rows + y_rows]

    zp = send(jnp.concatenate(z_part(0) + v_z, axis=0), "gz", -1)
    zm = send(jnp.concatenate(z_part(1), axis=0), "gz", 1)
    cand = jnp.concatenate(x_rows + y_rows + [zm, zp[:128]], axis=0)
    if v_faces is None:
        return cand
    return cand, jnp.concatenate(v_x + v_y + [zp[128:]], axis=0)[:, :512]


def local(boxes, anchors, potential):
    wide = 512 + META
    split, octant, exported, v_own, to_low, to_high, v_faces, places, table = call(
        "pack",
        pack_kernel,
        (
            shape((256, 256)),
            shape((128, 512)),
            shape((64, wide)),
            shape((200, 512)),
            shape((32 + VFACE, wide)),
            shape((32, wide)),
            shape((2 * VFACE, wide)),
            shape((128, 128), F32),
            shape((64, 128)),
        ),
        (),
        (),
        (boxes.reshape(256, 256), potential.reshape(1600, 40), anchors.reshape(16, 3)),
        ("prow", "pcol", "lift", "regroup", "faces"),
        10**8,
    )
    cand, v_far = exchange(exported, to_low, to_high, v_faces)
    grid, kinetic, overlaps, geometry = call(
        "ahead",
        whole_kernel(ahead_body),
        (
            shape((128, 512), F32),
            shape((128, 512), F32),
            shape((128, 128), F32),
            shape((128, 128), F32),
        ),
        (split, octant, places),
        AHEAD,
        (),
        (),
        10**9,
    )
    current, sent, v_box, near, to_low, to_high = call(
        "first",
        first_kernel,
        (
            shape((128, 512)),
            shape((64, 512)),
            shape((128, 512)),
            shape((128, 448)),
            shape((32, 512)),
            shape((32, 512)),
        ),
        (octant, places, table, grid, kinetic, overlaps, geometry, v_own, cand, v_far),
        FIRST,
        (),
        (),
        10**9,
    )
    cand = exchange(sent, to_low, to_high, None)
    done, applied_bf = call(
        "second",
        whole_kernel(second_body),
        (shape((128, 512), F32), shape((128, 512))),
        (current, v_box, geometry),
        SECOND,
        (),
        (),
        10**9,
    )
    (relaxed,) = call(
        "last",
        whole_kernel(lambda *a: (last_body(*a),)),
        (shape((256, 256)),),
        (done, applied_bf, current, cand, near),
        ("same_cand",),
        (),
        ("prow_t", "pcol_t"),
        10**9,
    )
    return relaxed.reshape(boxes.shape)


def solution(mesh):
    placed = (
        P("gx", "gy", "gz", None, None, None),
        P("gx", "gy", "gz", None, None),
        P("gx", "gy", "gz"),
    )
    return jax.shard_map(
        local,
        mesh=mesh,
        in_specs=placed,
        out_specs=P("gx", "gy", "gz", None, None, None),
        check_vma=False,
    )
```

```python
import functools

import jax
import jax.numpy as jnp
import ml_dtypes
import numpy as np
from jax import lax
from jax.experimental import pallas as pl
from jax.experimental.pallas import tpu as pltpu
from jax.sharding import PartitionSpec as P

F32 = jnp.float32
BF16 = jnp.bfloat16

MAGIC = [
    8.433424733352934e-07,
    -1.290557201342061e-05,
    8.76298447621056e-05,
    -0.00030158038132690465,
    0.001747237136729939,
    -0.009420470302010804,
    0.023738214637249424,
    0.0612625895831208,
    0.9940415697834004,
    -0.06048952891969835,
    -0.021030251609303816,
    0.013372634148547948,
    -0.0034412814449349387,
    0.0004944322768868992,
    -5.185986881173433e-05,
    2.7273449291197967e-06,
]
KINETIC = [
    -3.55369228991319,
    2.2191465938911166,
    -0.6156141465570069,
    0.2371780582153806,
    -0.0822663999742123,
    0.0220702918848226,
    -0.004097656893426338,
    0.00045167920287502236,
    -2.3982285245075998e-05,
    2.0904234952920368e-06,
    -3.7230763047369276e-07,
    -1.0585705549674146e-08,
    -5.8138798302825405e-11,
    2.7080049362631943e-13,
    -6.9244749406392e-18,
]
CELL = 1.0 / 4096.0
STEP = 0.1
PENALTY = 3.0

META = 128
VEDGE = (0, 1, 4)
VFACE = 16


def split_parts(values):
    high = values.astype(ml_dtypes.bfloat16)
    low = (values - high.astype(np.float64)).astype(ml_dtypes.bfloat16)
    return high, low


def candidate_rows():
    own = [((0, 0, 0), k) for q in range(8) for k in range(8)]

    def moved(rows, axis, step, groups):
        size = len(rows) // groups
        kept = []
        for g in range(1 if step < 0 else 0, groups, 2):
            kept += rows[g * size : (g + 1) * size]
        return [(d[:axis] + (d[axis] + step,) + d[axis + 1 :], k) for d, k in kept]

    parts = [own]
    for axis, groups in ((0, lambda n: 2), (1, lambda n: n // 16), (2, lambda n: n // 8)):
        here = list(parts)
        for step in (-1, 1):
            parts.append(sum((moved(p, axis, step, groups(len(p))) for p in here), []))
    return sum(parts[1:], [])


def face_places(axis):
    groups = ([], [])
    for a in VEDGE:
        for b in VEDGE:
            place = [a, b]
            place.insert(axis, 0)
            groups[0 if 0 in (a, b) else 1].append(tuple(place))
    return sum((g + [None] * (8 - len(g)) for g in groups), [])


def carried(block, axis):
    return [
        None if p is None or p[axis] != 0 else p[:axis] + (5,) + p[axis + 1 :] for p in block
    ]


@functools.cache
def tables():
    out = {}
    magic = np.zeros((16, 16))
    kinetic = np.zeros((16, 16))
    for r in range(16):
        for c in range(16):
            if 0 <= c - r + 8 < 16:
                magic[r, c] = MAGIC[c - r + 8]
            if abs(c - r) < 15:
                kinetic[r, c] = KINETIC[abs(c - r)]
    eye = np.eye(16)
    full = np.eye(256)
    row_of = np.array(
        [f * 16 + px * 8 + x8 for x8 in range(8) for px in range(2) for f in range(16)]
    )
    lane_of = np.array(
        [
            (py * 8 + y8) * 16 + pz * 8 + z8
            for py in range(2)
            for pz in range(2)
            for y8 in range(8)
            for z8 in range(8)
        ]
    )
    prow = full[row_of]
    pcol = full[:, lane_of]
    out["prow"], out["prow_t"] = prow, prow.T
    out["pcol"], out["pcol_t"] = pcol, pcol.T
    pair = np.kron(magic, magic)[np.ix_(lane_of, lane_of)] - full
    out["yz"], out["yz_t"] = pair.T, pair
    along = np.kron(eye, magic)[np.ix_(row_of, row_of)] - full
    out["x"], out["x_t"] = along, along.T
    second = (np.kron(kinetic, eye) + np.kron(eye, kinetic))[np.ix_(lane_of, lane_of)]
    out["kyz_h"], out["kyz_l"] = split_parts(-0.5 * second)
    along = np.kron(eye, kinetic)[np.ix_(row_of, row_of)]
    out["kx_h"], out["kx_l"] = split_parts(-0.5 * along)

    cand = candidate_rows()
    away = np.zeros((len(cand), META))
    away[:, :3] = [[5 * c for c in d] for d, k in cand]
    out["away"] = away
    out["same_cand"] = [[a == b for b in cand] for a in cand]
    regroup = np.zeros((320, 200))
    for x8 in range(8):
        for x in range(5):
            for y in range(5):
                regroup[x8 * 40 + x * 8 + y, (x * 8 + x8) * 5 + y] = 1
    out["regroup"] = regroup
    own = [None] * 200
    for z in range(5):
        for x in range(5):
            for y in range(5):
                own[z * 40 + x * 8 + y] = (x, y, z)
    blocks = [face_places(axis) for axis in range(3)]
    faces = np.zeros((3 * VFACE, 200))
    for row, place in enumerate(sum(blocks, [])):
        if place is not None:
            faces[row, own.index(place)] = 1
    out["faces"] = faces
    vx = carried(blocks[0], 0)
    vy = carried(blocks[1] + vx[:8], 1)
    vz = carried(blocks[2] + vx[:8] + vy[:8] + vy[16:], 2)

    def coded(places):
        codes = [-1.0 if p is None else 36 * p[0] + 6 * p[1] + p[2] for p in places]
        return np.broadcast_to(np.array(codes), (8, len(codes)))

    out["codes_own"] = coded(own)
    out["codes_far"] = coded(vx + vy + vz)
    return {
        k: np.ascontiguousarray(
            v, dtype=np.float32 if k.startswith("codes") else ml_dtypes.bfloat16
        )
        for k, v in out.items()
    }


def dot(a, b):
    return lax.dot_general(a, b, (((1,), (0,)), ((), ())), preferred_element_type=F32)


def dot_nt(a, b):
    return lax.dot_general(a, b, (((1,), (1,)), ((), ())), preferred_element_type=F32)


def rolled(values):
    return pltpu.roll(values, 64, 1)


def iota(dims, axis):
    return lax.broadcasted_iota(jnp.int32, dims, axis)


def low_lanes(values):
    return iota(values.shape, 1) < 64


def to_octants(split, roll):
    rows = split.shape[0] // 8
    blocks = []
    for py in range(split.shape[1] // 128):
        here = split[:, py * 128 : (py + 1) * 128]
        other = roll(here)
        for pz in range(2):
            pieces = []
            for x8 in range(0, 8, 2):
                one = slice(x8 * rows, (x8 + 1) * rows)
                two = slice((x8 + 1) * rows, (x8 + 2) * rows)
                if pz == 0:
                    left, right = here[one], other[two]
                else:
                    left, right = other[one], here[two]
                pieces.append(jnp.where(low_lanes(left), left, right))
            blocks.append(jnp.concatenate(pieces, axis=1))
    return blocks


def to_octant(split, roll):
    return jnp.concatenate(to_octants(split, roll), axis=0)


def to_split(octant, roll):
    columns = []
    for py in range(2):
        first = octant[(2 * py) * 32 : (2 * py + 1) * 32]
        second = octant[(2 * py + 1) * 32 : (2 * py + 2) * 32]
        pieces = []
        for pair in range(4):
            lanes = slice(pair * 128, (pair + 1) * 128)
            one, two = first[:, lanes], second[:, lanes]
            pieces.append(jnp.where(low_lanes(one), one, roll(two)))
            pieces.append(jnp.where(low_lanes(one), roll(one), two))
        columns.append(jnp.concatenate(pieces, axis=0))
    return jnp.concatenate(columns, axis=1)


def octant_places(anchor):
    row = iota((8, 16), 0)
    base = jnp.zeros((8, 16), F32)
    for c in range(3):
        base = jnp.where(row == c, jnp.broadcast_to(anchor[c], (8, 16)), base)
    spread = (iota((16, 128), 0) == iota((16, 128), 1) % 16).astype(F32).astype(BF16)
    base = dot(base.astype(BF16), spread)
    turned = jnp.concatenate([base] * 16, axis=0).T
    row, lane = iota((128, 128), 0), iota((128, 128), 1)
    bit = jnp.where(lane == 0, row // 16, jnp.where(lane == 1, row // 64, row // 32)) % 2
    return jnp.where(lane < 3, turned + bit.astype(F32), 0.0), base


def lift_table(y8):
    row, lane = iota((40, 384), 0), iota((40, 384), 1)
    match = (lane // 64 == row // 8) & (lane % 8 == row % 8) & ((lane // 8) % 8 == y8)
    return match.astype(F32).astype(BF16)


def across(values):
    eye = (iota((8, 128), 0) == iota((8, 128), 1)).astype(F32).astype(BF16)
    return dot_nt(eye, values.astype(BF16))


def export_table(base):
    edge = ((base == 0.0) | (base == 4.0)).astype(F32)
    edge = jnp.maximum(jnp.maximum(edge[0:1], edge[1:2]), edge[2:3])
    row, lane = iota((128, 128), 0), iota((128, 128), 1)
    before = (row < lane % 16).astype(F32).astype(BF16)
    before = jnp.where(row < 16, before, jnp.zeros_like(before))
    rank = dot(jnp.broadcast_to(edge, (8, 128)).astype(BF16), before)[0:1]
    row, lane = iota((64, 128), 0), iota((64, 128), 1)
    match = (
        (row // 32 == (lane // 16) % 2)
        & ((row // 16) % 2 == lane // 64)
        & ((row // 8) % 2 == (lane // 32) % 2)
    )
    chosen = (rank == (row % 8).astype(F32)) & (edge > 0.5)
    return (match & chosen).astype(F32).astype(BF16)


def same_function():
    return (iota((128, 128), 0) % 16 == iota((128, 128), 1) % 16).astype(F32)


def over_octants(values):
    total = values[0:16]
    for p in range(1, 8):
        total = total + values[16 * p : 16 * p + 16]
    return total


def summed(values, table):
    high = values.astype(BF16)
    low = (values - high.astype(F32)).astype(BF16)
    both = dot(jnp.concatenate([high, low], axis=0), table)
    return both[:16] + both[16:]


def repeated(values):
    return jnp.concatenate([values] * 8, axis=0)


def pack_body(boxes, anchor, potential_rows, t, roll=rolled):
    places, base = octant_places(anchor())
    table = export_table(base)
    split = dot(dot(t["prow"](), boxes()).astype(BF16), t["pcol"]())
    octant = to_octant(split, roll).astype(BF16)
    wide = jnp.concatenate([octant, places.astype(BF16)], axis=1)
    exported = dot(table, wide).astype(BF16)
    lifted = None
    for y8 in range(8):
        part = dot(potential_rows(y8).astype(BF16), lift_table(y8))
        lifted = part if lifted is None else lifted + part
    regrouped = dot(t["regroup"](), lifted.astype(BF16))
    v_rows = jnp.concatenate(to_octants(regrouped, roll)[:5], axis=0).astype(BF16)
    v_faces = dot(t["faces"](), v_rows).astype(BF16)
    v_faces = jnp.concatenate([v_faces, jnp.zeros((3 * VFACE, META), BF16)], axis=1)
    return split.astype(BF16), octant, exported, v_rows, v_faces, places, table


def grid_values(split, t, roll):
    inner = split.astype(F32) + dot(split, t["yz"]())
    return to_octant(inner + dot(t["x"](), inner.astype(BF16)), roll)


def kinetic_values(split, t, roll):
    lanes = dot(split, t["kyz_h"]()) + dot(split, t["kyz_l"]())
    rows = dot(t["kx_h"](), split) + dot(t["kx_l"](), split)
    return to_octant(lanes + rows, roll)


def returned_values(weighted, t, roll):
    split = to_split(weighted, roll)
    inner = split + dot(split.astype(BF16), t["yz_t"]())
    return to_octant(inner + dot(t["x_t"](), inner.astype(BF16)), roll)


def own_weights(overlaps, applied_bf, octant, geometry):
    products = over_octants((dot_nt(applied_bf, octant) * CELL - overlaps) * geometry)
    same = same_function()
    coupling = summed(products, same.astype(BF16)) + PENALTY * same[:16]
    return (repeated(coupling) * geometry).astype(BF16)


def near_weights(octant, applied_bf, cand, near, t):
    products = dot_nt(applied_bf, cand) - PENALTY * dot_nt(octant, cand)
    coupling = summed(over_octants(products * CELL * near), t["same_cand"]())
    return (repeated(coupling) * near).astype(BF16)


OPERATE = ("yz", "x", "kyz_h", "kyz_l", "kx_h", "kx_l")


def row_codes(places):
    return 36.0 * places[:, 0:1] + 6.0 * places[:, 1:2] + places[:, 2:3]


def picked(code, codes, rows):
    return dot((code == codes[0:1]).astype(F32).astype(BF16), rows)


def ahead_body(split, octant, places, v_own, t, roll=rolled):
    row_code = row_codes(places)
    lanes = across(places)
    lane_code = 36.0 * lanes[0:1] + 6.0 * lanes[1:2] + lanes[2:3]
    geometry = (row_code == lane_code).astype(F32)
    overlaps = dot_nt(octant, octant) * (CELL * PENALTY)
    v_box = picked(row_code, t["codes_own"](), v_own).astype(BF16)
    return grid_values(split, t, roll), kinetic_values(split, t, roll), overlaps, geometry, v_box


FIRST = ("yz_t", "x_t", "same_cand", "away", "codes_far")
AHEAD = OPERATE + ("codes_own",)


def first_body(
    octant, places, table, grid, kinetic, overlaps, geometry, v_box, cand, v_far, t, roll=rolled
):
    v_box = v_box.astype(F32) + picked(row_codes(places), t["codes_far"](), v_far)
    lanes = across_rows(cand[:, 512:] + t["away"]())
    near = (
        (places[:, 0:1] == lanes[0:1])
        & (places[:, 1:2] == lanes[1:2])
        & (places[:, 2:3] == lanes[2:3])
    ).astype(F32)
    cand = cand[:, :512]
    applied = returned_values(grid * v_box, t, roll) + kinetic
    applied_bf = applied.astype(BF16)
    own_w = own_weights(overlaps, applied_bf, octant, geometry)
    near_w = near_weights(octant, applied_bf, cand, near, t)
    correction = dot(own_w, octant) + dot(near_w, cand)
    current = (octant.astype(F32) - STEP * (applied - correction)).astype(BF16)
    sent = dot(table, current).astype(BF16)
    return current, sent, v_box.astype(BF16), near.astype(BF16)


def across_rows(values):
    eye = (iota((8, META), 0) == iota((8, META), 1)).astype(F32).astype(BF16)
    return dot_nt(eye, values)


SECOND = OPERATE + ("yz_t", "x_t")


def second_body(octant, v_box, geometry, t, roll=rolled):
    split = to_split(octant.astype(F32), roll).astype(BF16)
    weighted = grid_values(split, t, roll) * v_box.astype(F32)
    applied = returned_values(weighted, t, roll) + kinetic_values(split, t, roll)
    applied_bf = applied.astype(BF16)
    overlaps = dot_nt(octant, octant) * (CELL * PENALTY)
    own_w = own_weights(overlaps, applied_bf, octant, geometry)
    done = octant.astype(F32) - STEP * (applied - dot(own_w, octant))
    return done, applied_bf


LAST = ("same_cand", "prow_t", "pcol_t")


def last_body(done, applied_bf, octant, cand, near, t, roll=rolled):
    near_w = near_weights(octant, applied_bf, cand, near.astype(F32), t)
    current = (done + STEP * dot(near_w, cand)).astype(BF16)
    split = to_split(current.astype(F32), roll).astype(BF16)
    return dot(dot(t["prow_t"](), split).astype(BF16), t["pcol_t"]()).astype(BF16)


def shape(dims, dtype=BF16):
    return jax.ShapeDtypeStruct(dims, dtype)


class Stored:
    def __init__(self, source, target, semaphore):
        self.source = source
        self.copy = pltpu.make_async_copy(source, target, semaphore)

    def put(self, value):
        self.source[...] = value
        self.copy.start()


class Fetched:
    def __init__(self, source, target, semaphore):
        self.copy = pltpu.make_async_copy(source, target, semaphore)
        self.target = target
        self.waiting = True
        self.copy.start()

    def ref(self):
        if self.waiting:
            self.copy.wait()
            self.waiting = False
        return self.target

    def __call__(self):
        return self.ref()[...]


def call(name, body, out_shape, inputs, consts, flops):
    arrays = list(inputs) + [jnp.asarray(tables()[k]) for k in consts]

    def kernel(*refs):
        t = {
            k: functools.partial(lambda ref: ref[...], r)
            for k, r in zip(consts, refs[len(inputs) : len(arrays)])
        }
        body(refs[: len(inputs)], t, refs[len(arrays) :])

    return pl.pallas_call(
        kernel,
        out_shape=out_shape,
        in_specs=[pl.BlockSpec(memory_space=pltpu.VMEM)] * len(arrays),
        out_specs=tuple(pl.BlockSpec(memory_space=pltpu.VMEM) for _ in out_shape),
        compiler_params=pltpu.CompilerParams(vmem_limit_bytes=24 << 20),
        cost_estimate=pl.CostEstimate(
            flops=flops, bytes_accessed=flops // 1000, transcendentals=0
        ),
        name=name,
    )(*arrays)


PACK = ("prow", "pcol", "regroup", "faces")


def pack_call(boxes, anchor, potential):
    wide = 512 + META
    arrays = [boxes, anchor, potential] + [jnp.asarray(tables()[k]) for k in PACK]
    out_shape = (
        shape((32, wide)),
        shape((32 + VFACE, wide)),
        shape((64, wide)),
        shape((2 * VFACE, wide)),
        shape((256, 256)),
        shape((128, 512)),
        shape((200, 512)),
        shape((128, 128), F32),
        shape((64, 128)),
    )
    count = len(arrays)

    def kernel(*refs):
        sources, targets = refs[:count], refs[count : count + len(out_shape)]
        scratch, semaphores = refs[count + len(out_shape) : -1], refs[-1]
        fetched = [
            Fetched(a, b, semaphores.at[i])
            for i, (a, b) in enumerate(zip(sources, scratch[:count]))
        ]
        stored = [
            Stored(a, b, semaphores.at[count + i])
            for i, (a, b) in enumerate(zip(scratch[count:], targets))
        ]
        for piece in fetched:
            piece.ref()
        rows = fetched[2].ref()
        split, octant, exported, v_rows, v_faces, places, table = pack_body(
            fetched[0],
            lambda: fetched[1]()[0, 0].astype(F32),
            lambda y8: rows[pl.ds(y8, 200, stride=8), :],
            dict(zip(PACK, fetched[3:])),
        )
        stored[0].put(exported[32:64])
        stored[1].put(jnp.concatenate([exported[0:32], v_faces[0:VFACE]], axis=0))
        stored[2].put(exported)
        stored[3].put(v_faces[VFACE:])
        stored[4].put(split)
        stored[5].put(octant)
        stored[6].put(v_rows)
        stored[7].put(places)
        stored[8].put(table)
        for piece in stored:
            piece.copy.wait()

    return pl.pallas_call(
        kernel,
        out_shape=out_shape,
        in_specs=[pl.BlockSpec(memory_space=pltpu.HBM)] * count,
        out_specs=tuple(pl.BlockSpec(memory_space=pltpu.HBM) for _ in out_shape),
        scratch_shapes=[pltpu.VMEM(a.shape, a.dtype) for a in arrays]
        + [pltpu.VMEM(o.shape, o.dtype) for o in out_shape]
        + [pltpu.SemaphoreType.DMA((count + len(out_shape),))],
        compiler_params=pltpu.CompilerParams(vmem_limit_bytes=56 << 20),
        cost_estimate=pl.CostEstimate(flops=10**8, bytes_accessed=10**6, transcendentals=0),
        name="pack",
    )(*arrays)


def whole_kernel(body):
    def run(ins, t, outs):
        got = body(*[r[...] for r in ins], t)
        for ref, value in zip(outs, got):
            ref[...] = value

    return run


def first_kernel(ins, t, outs):
    got = first_body(*[r[...] for r in ins], t)
    for ref, value in zip(outs, got):
        ref[...] = value
    outs[4][...] = got[1][0:32]
    outs[5][...] = got[1][32:64]


def passed_along(value, axis, step):
    count = lax.axis_size(axis)
    return lax.ppermute(value, axis, [(i, (i + step) % count) for i in range(count)])


def half_of(rows, size, keep):
    count = rows.shape[0] // (2 * size)
    return rows.reshape(count, 2, size, rows.shape[1])[:, keep].reshape(count * size, -1)


def exchange(exported, to_low, to_high, v_faces, send=passed_along):
    v_x, v_y, v_z = [], [], []
    xp = send(to_low, "gx", -1)
    xm = send(to_high, "gx", 1)
    x_rows = [xm, xp[:32]]
    if v_faces is not None:
        v_x = [xp[32:]]
        v_y = [v_faces[:VFACE], xp[32:40]]
        v_z = [v_faces[VFACE:], xp[32:40]]

    def y_part(keep):
        return [half_of(r, 16, keep) for r in [exported] + x_rows]

    yp = send(jnp.concatenate(y_part(0) + v_y, axis=0), "gy", -1)
    ym = send(jnp.concatenate(y_part(1), axis=0), "gy", 1)
    y_rows = [ym, yp[:64]]
    if v_faces is not None:
        v_y = [yp[64:]]
        v_z = v_z + [yp[64:72], yp[80:88]]

    def z_part(keep):
        return [half_of(r, 8, keep) for r in [exported] + x_rows + y_rows]

    zp = send(jnp.concatenate(z_part(0) + v_z, axis=0), "gz", -1)
    zm = send(jnp.concatenate(z_part(1), axis=0), "gz", 1)
    cand = jnp.concatenate(x_rows + y_rows + [zm, zp[:128]], axis=0)
    if v_faces is None:
        return cand
    return cand, jnp.concatenate(v_x + v_y + [zp[128:]], axis=0)[:, :512]


def local(boxes, anchors, potential):
    to_high, to_low, exported, v_faces, split, octant, v_own, places, table = pack_call(
        boxes.reshape(256, 256),
        jnp.transpose(anchors, (0, 1, 4, 2, 3)),
        potential.reshape(1600, 40),
    )
    cand, v_far = exchange(exported, to_low, to_high, v_faces)
    grid, kinetic, overlaps, geometry, v_box = call(
        "ahead",
        whole_kernel(lambda a, b, c, d, unused, t: ahead_body(a, b, c, d, t)),
        (
            shape((128, 512), F32),
            shape((128, 512), F32),
            shape((128, 128), F32),
            shape((128, 128), F32),
            shape((128, 512)),
        ),
        (split, octant, places, v_own, table),
        AHEAD + FIRST,
        10**9,
    )
    current, sent, v_box, near, to_low, to_high = call(
        "first",
        first_kernel,
        (
            shape((128, 512)),
            shape((64, 512)),
            shape((128, 512)),
            shape((128, 448)),
            shape((32, 512)),
            shape((32, 512)),
        ),
        (octant, places, table, grid, kinetic, overlaps, geometry, v_box, cand, v_far),
        FIRST,
        10**9,
    )
    cand = exchange(sent, to_low, to_high, None)
    done, applied_bf = call(
        "second",
        whole_kernel(second_body),
        (shape((128, 512), F32), shape((128, 512))),
        (current, v_box, geometry),
        SECOND + LAST,
        10**9,
    )
    (relaxed,) = call(
        "last",
        whole_kernel(lambda *a: (last_body(*a),)),
        (shape((256, 256)),),
        (done, applied_bf, current, cand, near),
        LAST,
        10**9,
    )
    return relaxed.reshape(boxes.shape)


def solution(mesh):
    placed = (
        P("gx", "gy", "gz", None, None, None),
        P("gx", "gy", "gz", None, None),
        P("gx", "gy", "gz"),
    )
    return jax.shard_map(
        local,
        mesh=mesh,
        in_specs=placed,
        out_specs=P("gx", "gy", "gz", None, None, None),
        check_vma=False,
    )
```

```python
import functools

import jax
import jax.numpy as jnp
import ml_dtypes
import numpy as np
from jax import lax
from jax.experimental import pallas as pl
from jax.experimental.pallas import tpu as pltpu
from jax.sharding import PartitionSpec as P

F32 = jnp.float32
BF16 = jnp.bfloat16

MAGIC = [
    8.433424733352934e-07,
    -1.290557201342061e-05,
    8.76298447621056e-05,
    -0.00030158038132690465,
    0.001747237136729939,
    -0.009420470302010804,
    0.023738214637249424,
    0.0612625895831208,
    0.9940415697834004,
    -0.06048952891969835,
    -0.021030251609303816,
    0.013372634148547948,
    -0.0034412814449349387,
    0.0004944322768868992,
    -5.185986881173433e-05,
    2.7273449291197967e-06,
]
KINETIC = [
    -3.55369228991319,
    2.2191465938911166,
    -0.6156141465570069,
    0.2371780582153806,
    -0.0822663999742123,
    0.0220702918848226,
    -0.004097656893426338,
    0.00045167920287502236,
    -2.3982285245075998e-05,
    2.0904234952920368e-06,
    -3.7230763047369276e-07,
    -1.0585705549674146e-08,
    -5.8138798302825405e-11,
    2.7080049362631943e-13,
    -6.9244749406392e-18,
]
CELL = 1.0 / 4096.0
STEP = 0.1
PENALTY = 3.0

META = 128
VEDGE = (0, 1, 4)
VFACE = 16


def split_parts(values):
    high = values.astype(ml_dtypes.bfloat16)
    low = (values - high.astype(np.float64)).astype(ml_dtypes.bfloat16)
    return high, low


def candidate_rows():
    own = [((0, 0, 0), k) for q in range(8) for k in range(8)]

    def moved(rows, axis, step, groups):
        size = len(rows) // groups
        kept = []
        for g in range(1 if step < 0 else 0, groups, 2):
            kept += rows[g * size : (g + 1) * size]
        return [(d[:axis] + (d[axis] + step,) + d[axis + 1 :], k) for d, k in kept]

    parts = [own]
    for axis, groups in ((0, lambda n: 2), (1, lambda n: n // 16), (2, lambda n: n // 8)):
        here = list(parts)
        for step in (-1, 1):
            parts.append(sum((moved(p, axis, step, groups(len(p))) for p in here), []))
    return sum(parts[1:], [])


def face_places(axis):
    groups = ([], [])
    for a in VEDGE:
        for b in VEDGE:
            place = [a, b]
            place.insert(axis, 0)
            groups[0 if 0 in (a, b) else 1].append(tuple(place))
    return sum((g + [None] * (8 - len(g)) for g in groups), [])


def carried(block, axis):
    return [
        None if p is None or p[axis] != 0 else p[:axis] + (5,) + p[axis + 1 :] for p in block
    ]


@functools.cache
def tables():
    out = {}
    magic = np.zeros((16, 16))
    kinetic = np.zeros((16, 16))
    for r in range(16):
        for c in range(16):
            if 0 <= c - r + 8 < 16:
                magic[r, c] = MAGIC[c - r + 8]
            if abs(c - r) < 15:
                kinetic[r, c] = KINETIC[abs(c - r)]
    eye = np.eye(16)
    full = np.eye(256)
    row_of = np.array(
        [f * 16 + px * 8 + x8 for x8 in range(8) for px in range(2) for f in range(16)]
    )
    lane_of = np.array(
        [
            (py * 8 + y8) * 16 + pz * 8 + z8
            for py in range(2)
            for pz in range(2)
            for y8 in range(8)
            for z8 in range(8)
        ]
    )
    prow = full[row_of]
    pcol = full[:, lane_of]
    out["prow"], out["prow_t"] = prow, prow.T
    out["pcol"], out["pcol_t"] = pcol, pcol.T
    pair = np.kron(magic, magic)[np.ix_(lane_of, lane_of)] - full
    out["yz"], out["yz_t"] = pair.T, pair
    along = np.kron(eye, magic)[np.ix_(row_of, row_of)] - full
    out["x"], out["x_t"] = along, along.T
    second = (np.kron(kinetic, eye) + np.kron(eye, kinetic))[np.ix_(lane_of, lane_of)]
    out["kyz_h"], out["kyz_l"] = split_parts(-0.5 * second)
    along = np.kron(eye, kinetic)[np.ix_(row_of, row_of)]
    out["kx_h"], out["kx_l"] = split_parts(-0.5 * along)

    cand = candidate_rows()
    away = np.zeros((len(cand), META))
    away[:, :3] = [[5 * c for c in d] for d, k in cand]
    out["away"] = away
    out["same_cand"] = [[a == b for b in cand] for a in cand]
    own = [None] * 200
    for z in range(5):
        for x in range(5):
            for y in range(5):
                own[z * 40 + x * 8 + y] = (x, y, z)
    blocks = [face_places(axis) for axis in range(3)]
    faces = np.zeros((3 * VFACE, 200))
    for row, place in enumerate(sum(blocks, [])):
        if place is not None:
            faces[row, own.index(place)] = 1
    out["faces"] = faces
    face_x = np.zeros((VFACE, 24))
    for row, place in enumerate(blocks[0]):
        if place is not None:
            face_x[row, VEDGE.index(place[2]) * 8 + place[1]] = 1
    out["face_x"] = face_x
    vx = carried(blocks[0], 0)
    vy = carried(blocks[1] + vx[:8], 1)
    vz = carried(blocks[2] + vx[:8] + vy[:8] + vy[16:], 2)

    def coded(places):
        codes = [-1.0 if p is None else 36 * p[0] + 6 * p[1] + p[2] for p in places]
        return np.broadcast_to(np.array(codes), (8, len(codes)))

    out["codes_own"] = coded(own)
    out["codes_far"] = coded(vx + vy + vz)
    return {
        k: np.ascontiguousarray(
            v, dtype=np.float32 if k.startswith("codes") else ml_dtypes.bfloat16
        )
        for k, v in out.items()
    }


def dot(a, b):
    return lax.dot_general(a, b, (((1,), (0,)), ((), ())), preferred_element_type=F32)


def dot_nt(a, b):
    return lax.dot_general(a, b, (((1,), (1,)), ((), ())), preferred_element_type=F32)


def rolled(values):
    return pltpu.roll(values, 64, 1)


def iota(dims, axis):
    return lax.broadcasted_iota(jnp.int32, dims, axis)


def low_lanes(values):
    return iota(values.shape, 1) < 64


def to_octants(split, roll):
    rows = split.shape[0] // 8
    blocks = []
    for py in range(split.shape[1] // 128):
        here = split[:, py * 128 : (py + 1) * 128]
        other = roll(here)
        for pz in range(2):
            pieces = []
            for x8 in range(0, 8, 2):
                one = slice(x8 * rows, (x8 + 1) * rows)
                two = slice((x8 + 1) * rows, (x8 + 2) * rows)
                if pz == 0:
                    left, right = here[one], other[two]
                else:
                    left, right = other[one], here[two]
                pieces.append(jnp.where(low_lanes(left), left, right))
            blocks.append(jnp.concatenate(pieces, axis=1))
    return blocks


def to_octant(split, roll):
    return jnp.concatenate(to_octants(split, roll), axis=0)


def to_split(octant, roll):
    columns = []
    for py in range(2):
        first = octant[(2 * py) * 32 : (2 * py + 1) * 32]
        second = octant[(2 * py + 1) * 32 : (2 * py + 2) * 32]
        pieces = []
        for pair in range(4):
            lanes = slice(pair * 128, (pair + 1) * 128)
            one, two = first[:, lanes], second[:, lanes]
            pieces.append(jnp.where(low_lanes(one), one, roll(two)))
            pieces.append(jnp.where(low_lanes(one), roll(one), two))
        columns.append(jnp.concatenate(pieces, axis=0))
    return jnp.concatenate(columns, axis=1)


def octant_places(anchor):
    row = iota((8, 16), 0)
    base = jnp.zeros((8, 16), F32)
    for c in range(3):
        base = jnp.where(row == c, jnp.broadcast_to(anchor[c], (8, 16)), base)
    spread = (iota((16, 128), 0) == iota((16, 128), 1) % 16).astype(F32).astype(BF16)
    base = dot(base.astype(BF16), spread)
    turned = jnp.concatenate([base] * 16, axis=0).T
    row, lane = iota((128, 128), 0), iota((128, 128), 1)
    bit = jnp.where(lane == 0, row // 16, jnp.where(lane == 1, row // 64, row // 32)) % 2
    return jnp.where(lane < 3, turned + bit.astype(F32), 0.0), base


def lift_table(y8):
    row, lane = iota((40, 384), 0), iota((40, 384), 1)
    match = (lane // 64 == row // 8) & (lane % 8 == row % 8) & ((lane // 8) % 8 == y8)
    return match.astype(F32).astype(BF16)


def across(values):
    eye = (iota((8, 128), 0) == iota((8, 128), 1)).astype(F32).astype(BF16)
    return dot_nt(eye, values.astype(BF16))


def export_table(base):
    edge = ((base == 0.0) | (base == 4.0)).astype(F32)
    edge = jnp.maximum(jnp.maximum(edge[0:1], edge[1:2]), edge[2:3])
    row, lane = iota((128, 128), 0), iota((128, 128), 1)
    before = (row < lane % 16).astype(F32).astype(BF16)
    before = jnp.where(row < 16, before, jnp.zeros_like(before))
    rank = dot(jnp.broadcast_to(edge, (8, 128)).astype(BF16), before)[0:1]
    row, lane = iota((64, 128), 0), iota((64, 128), 1)
    match = (
        (row // 32 == (lane // 16) % 2)
        & ((row // 16) % 2 == lane // 64)
        & ((row // 8) % 2 == (lane // 32) % 2)
    )
    chosen = (rank == (row % 8).astype(F32)) & (edge > 0.5)
    return (match & chosen).astype(F32).astype(BF16)


def same_function():
    return (iota((128, 128), 0) % 16 == iota((128, 128), 1) % 16).astype(F32)


def over_octants(values):
    total = values[0:16]
    for p in range(1, 8):
        total = total + values[16 * p : 16 * p + 16]
    return total


def summed(values, table):
    high = values.astype(BF16)
    low = (values - high.astype(F32)).astype(BF16)
    both = dot(jnp.concatenate([high, low], axis=0), table)
    return both[:16] + both[16:]


def repeated(values):
    return jnp.concatenate([values] * 8, axis=0)


def function_rows(boxes, anchor, t, roll):
    places, base = octant_places(anchor)
    table = export_table(base)
    split = dot(dot(t["prow"](), boxes).astype(BF16), t["pcol"]())
    octant = to_octant(split, roll).astype(BF16)
    wide = jnp.concatenate([octant, places.astype(BF16)], axis=1)
    exported = dot(table, wide).astype(BF16)
    return split.astype(BF16), octant, exported, places, table


def lifted_rows(potential_rows):
    total = None
    for y8 in range(8):
        part = dot(potential_rows(y8).astype(BF16), lift_table(y8))
        total = part if total is None else total + part
    return total.astype(BF16)


def with_meta(rows):
    return jnp.concatenate([rows, jnp.zeros((rows.shape[0], META), BF16)], axis=1)


PACK = ("prow", "pcol", "face_x")


def pack_body(boxes, anchor, slab_rows, t, roll=rolled):
    exported = function_rows(boxes(), anchor(), t, roll)[2]
    row, lane = iota((64, 40), 0), iota((64, 40), 1)
    regroup = ((row // 8 * 5 + row % 8 == lane) & (row % 8 < 5)).astype(F32).astype(BF16)
    by_z = to_octants(dot(regroup, lifted_rows(slab_rows)), roll)
    slab = jnp.concatenate([by_z[z] for z in VEDGE], axis=0).astype(BF16)
    face = with_meta(dot(t["face_x"](), slab).astype(BF16))
    return exported[32:64], jnp.concatenate([exported[0:32], face], axis=0)


def regroup_table():
    row, lane = iota((40, 200), 0), iota((40, 200), 1)
    target = jnp.where(row % 8 < 5, row // 8 * 40 + row % 8, -200)
    blocks = [(lane == target + 5 * x8).astype(F32).astype(BF16) for x8 in range(8)]
    return jnp.concatenate(blocks, axis=0)


LAYOUT = ("prow", "pcol", "faces")


def layout_body(boxes, anchor, potential_rows, t, roll=rolled):
    split, octant, exported, places, table = function_rows(boxes, anchor, t, roll)
    by_z = to_octants(dot(regroup_table(), lifted_rows(potential_rows)), roll)
    v_rows = jnp.concatenate(by_z[:5], axis=0).astype(BF16)
    v_faces = with_meta(dot(t["faces"](), v_rows).astype(BF16)[VFACE:])
    return exported, v_faces, split, octant, v_rows, places, table


def grid_values(split, t, roll):
    inner = split.astype(F32) + dot(split, t["yz"]())
    return to_octant(inner + dot(t["x"](), inner.astype(BF16)), roll)


def kinetic_values(split, t, roll):
    lanes = dot(split, t["kyz_h"]()) + dot(split, t["kyz_l"]())
    rows = dot(t["kx_h"](), split) + dot(t["kx_l"](), split)
    return to_octant(lanes + rows, roll)


def returned_values(weighted, t, roll):
    split = to_split(weighted, roll)
    inner = split + dot(split.astype(BF16), t["yz_t"]())
    return to_octant(inner + dot(t["x_t"](), inner.astype(BF16)), roll)


def own_weights(overlaps, applied_bf, octant, geometry):
    products = over_octants((dot_nt(applied_bf, octant) * CELL - overlaps) * geometry)
    same = same_function()
    coupling = summed(products, same.astype(BF16)) + PENALTY * same[:16]
    return (repeated(coupling) * geometry).astype(BF16)


def near_weights(octant, applied_bf, cand, near, t):
    products = dot_nt(applied_bf, cand) - PENALTY * dot_nt(octant, cand)
    coupling = summed(over_octants(products * CELL * near), t["same_cand"]())
    return (repeated(coupling) * near).astype(BF16)


OPERATE = ("yz", "x", "kyz_h", "kyz_l", "kx_h", "kx_l")


def row_codes(places):
    return 36.0 * places[:, 0:1] + 6.0 * places[:, 1:2] + places[:, 2:3]


def picked(code, codes, rows):
    return dot((code == codes[0:1]).astype(F32).astype(BF16), rows)


def ahead_body(split, octant, places, v_own, t, roll=rolled):
    row_code = row_codes(places)
    lanes = across(places)
    lane_code = 36.0 * lanes[0:1] + 6.0 * lanes[1:2] + lanes[2:3]
    geometry = (row_code == lane_code).astype(F32)
    overlaps = dot_nt(octant, octant) * (CELL * PENALTY)
    v_box = picked(row_code, t["codes_own"](), v_own).astype(BF16)
    return grid_values(split, t, roll), kinetic_values(split, t, roll), overlaps, geometry, v_box


FIRST = ("yz_t", "x_t", "same_cand", "away", "codes_far")
AHEAD = OPERATE + ("codes_own",)


def first_body(
    octant, places, table, grid, kinetic, overlaps, geometry, v_box, cand, v_far, t, roll=rolled
):
    v_box = v_box.astype(F32) + picked(row_codes(places), t["codes_far"](), v_far)
    lanes = across_rows(cand[:, 512:] + t["away"]())
    near = (
        (places[:, 0:1] == lanes[0:1])
        & (places[:, 1:2] == lanes[1:2])
        & (places[:, 2:3] == lanes[2:3])
    ).astype(F32)
    cand = cand[:, :512]
    applied = returned_values(grid * v_box, t, roll) + kinetic
    applied_bf = applied.astype(BF16)
    own_w = own_weights(overlaps, applied_bf, octant, geometry)
    near_w = near_weights(octant, applied_bf, cand, near, t)
    correction = dot(own_w, octant) + dot(near_w, cand)
    current = (octant.astype(F32) - STEP * (applied - correction)).astype(BF16)
    sent = dot(table, current).astype(BF16)
    return current, sent, v_box.astype(BF16), near.astype(BF16)


def across_rows(values):
    eye = (iota((8, META), 0) == iota((8, META), 1)).astype(F32).astype(BF16)
    return dot_nt(eye, values)


SECOND = OPERATE + ("yz_t", "x_t")


def second_body(octant, v_box, geometry, t, roll=rolled):
    split = to_split(octant.astype(F32), roll).astype(BF16)
    weighted = grid_values(split, t, roll) * v_box.astype(F32)
    applied = returned_values(weighted, t, roll) + kinetic_values(split, t, roll)
    applied_bf = applied.astype(BF16)
    overlaps = dot_nt(octant, octant) * (CELL * PENALTY)
    own_w = own_weights(overlaps, applied_bf, octant, geometry)
    done = octant.astype(F32) - STEP * (applied - dot(own_w, octant))
    return done, applied_bf


LAST = ("same_cand", "prow_t", "pcol_t")


def last_body(done, applied_bf, octant, cand, near, t, roll=rolled):
    near_w = near_weights(octant, applied_bf, cand, near.astype(F32), t)
    current = (done + STEP * dot(near_w, cand)).astype(BF16)
    split = to_split(current.astype(F32), roll).astype(BF16)
    return dot(dot(t["prow_t"](), split).astype(BF16), t["pcol_t"]()).astype(BF16)


def shape(dims, dtype=BF16):
    return jax.ShapeDtypeStruct(dims, dtype)


class Stored:
    def __init__(self, source, target, semaphore):
        self.source = source
        self.copy = pltpu.make_async_copy(source, target, semaphore)

    def put(self, value):
        self.source[...] = value
        self.copy.start()


class Fetched:
    def __init__(self, source, target, semaphore):
        self.copy = pltpu.make_async_copy(source, target, semaphore)
        self.target = target
        self.waiting = True
        self.copy.start()

    def ref(self):
        if self.waiting:
            self.copy.wait()
            self.waiting = False
        return self.target

    def __call__(self):
        return self.ref()[...]


def call(name, body, out_shape, inputs, consts, flops):
    arrays = list(inputs) + [jnp.asarray(tables()[k]) for k in consts]

    def kernel(*refs):
        t = {
            k: functools.partial(lambda ref: ref[...], r)
            for k, r in zip(consts, refs[len(inputs) : len(arrays)])
        }
        body(refs[: len(inputs)], t, refs[len(arrays) :])

    return pl.pallas_call(
        kernel,
        out_shape=out_shape,
        in_specs=[pl.BlockSpec(memory_space=pltpu.VMEM)] * len(arrays),
        out_specs=tuple(pl.BlockSpec(memory_space=pltpu.VMEM) for _ in out_shape),
        compiler_params=pltpu.CompilerParams(vmem_limit_bytes=24 << 20),
        cost_estimate=pl.CostEstimate(
            flops=flops, bytes_accessed=flops // 1000, transcendentals=0
        ),
        name=name,
    )(*arrays)


def pack_call(boxes, anchor, slab):
    wide = 512 + META
    arrays = [boxes, anchor, slab] + [jnp.asarray(tables()[k]) for k in PACK]
    shapes = [(a.shape, a.dtype) for a in arrays]
    shapes[2] = ((320, 40), F32)
    out_shape = (shape((32, wide)), shape((32 + VFACE, wide)))
    count = len(arrays)

    def kernel(*refs):
        sources = list(refs[:count])
        sources[2] = sources[2].at[pl.ds(0, 320)]
        targets = refs[count : count + len(out_shape)]
        scratch, semaphores = refs[count + len(out_shape) : -1], refs[-1]
        fetched = [
            Fetched(a, b, semaphores.at[i])
            for i, (a, b) in enumerate(zip(sources, scratch[:count]))
        ]
        stored = [
            Stored(a, b, semaphores.at[count + i])
            for i, (a, b) in enumerate(zip(scratch[count:], targets))
        ]
        for piece in fetched:
            piece.ref()
        rows = fetched[2].ref()
        got = pack_body(
            fetched[0],
            lambda: fetched[1]()[0, 0].astype(F32),
            lambda y8: rows[pl.ds(y8, 40, stride=8), :],
            dict(zip(PACK, fetched[3:])),
        )
        for piece, value in zip(stored, got):
            piece.put(value)
        for piece in stored:
            piece.copy.wait()

    return pl.pallas_call(
        kernel,
        out_shape=out_shape,
        in_specs=[pl.BlockSpec(memory_space=pltpu.HBM)] * count,
        out_specs=tuple(pl.BlockSpec(memory_space=pltpu.HBM) for _ in out_shape),
        scratch_shapes=[pltpu.VMEM(*a) for a in shapes]
        + [pltpu.VMEM(o.shape, o.dtype) for o in out_shape]
        + [pltpu.SemaphoreType.DMA((count + len(out_shape),))],
        compiler_params=pltpu.CompilerParams(vmem_limit_bytes=56 << 20),
        cost_estimate=pl.CostEstimate(flops=10**8, bytes_accessed=10**6, transcendentals=0),
        name="pack",
    )(*arrays)


def layout_kernel(ins, t, outs):
    boxes, anchor, potential = ins
    got = layout_body(
        boxes[...],
        anchor[...][0, 0].astype(F32),
        lambda y8: potential[pl.ds(y8, 200, stride=8), :],
        t,
    )
    for ref, value in zip(outs, got):
        ref[...] = value


def whole_kernel(body):
    def run(ins, t, outs):
        got = body(*[r[...] for r in ins], t)
        for ref, value in zip(outs, got):
            ref[...] = value

    return run


def first_kernel(ins, t, outs):
    got = first_body(*[r[...] for r in ins], t)
    for ref, value in zip(outs, got):
        ref[...] = value
    outs[4][...] = got[1][0:32]
    outs[5][...] = got[1][32:64]


def passed_along(value, axis, step):
    count = lax.axis_size(axis)
    return lax.ppermute(value, axis, [(i, (i + step) % count) for i in range(count)])


def half_of(rows, size, keep):
    count = rows.shape[0] // (2 * size)
    return rows.reshape(count, 2, size, rows.shape[1])[:, keep].reshape(count * size, -1)


def exchange_x(to_low, to_high, send=passed_along):
    return send(to_high, "gx", 1), send(to_low, "gx", -1)


def exchange(exported, xm, xp, v_faces, send=passed_along):
    v_x, v_y, v_z = [], [], []
    x_rows = [xm, xp[:32]]
    if v_faces is not None:
        v_x = [xp[32:]]
        v_y = [v_faces[:VFACE], xp[32:40]]
        v_z = [v_faces[VFACE:], xp[32:40]]

    def y_part(keep):
        return [half_of(r, 16, keep) for r in [exported] + x_rows]

    yp = send(jnp.concatenate(y_part(0) + v_y, axis=0), "gy", -1)
    ym = send(jnp.concatenate(y_part(1), axis=0), "gy", 1)
    y_rows = [ym, yp[:64]]
    if v_faces is not None:
        v_y = [yp[64:]]
        v_z = v_z + [yp[64:72], yp[80:88]]

    def z_part(keep):
        return [half_of(r, 8, keep) for r in [exported] + x_rows + y_rows]

    zp = send(jnp.concatenate(z_part(0) + v_z, axis=0), "gz", -1)
    zm = send(jnp.concatenate(z_part(1), axis=0), "gz", 1)
    cand = jnp.concatenate(x_rows + y_rows + [zm, zp[:128]], axis=0)
    if v_faces is None:
        return cand
    return cand, jnp.concatenate(v_x + v_y + [zp[128:]], axis=0)[:, :512]


def local(boxes, anchors, potential):
    wide = 512 + META
    own = boxes.reshape(256, 256)
    anchor = jnp.transpose(anchors, (0, 1, 4, 2, 3))
    rows = potential.reshape(1600, 40)
    to_high, to_low = pack_call(own, anchor, rows)
    xm, xp = exchange_x(to_low, to_high)
    exported, v_faces, split, octant, v_own, places, table = call(
        "layout",
        layout_kernel,
        (
            shape((64, wide)),
            shape((2 * VFACE, wide)),
            shape((256, 256)),
            shape((128, 512)),
            shape((200, 512)),
            shape((128, 128), F32),
            shape((64, 128)),
        ),
        (own, anchor, rows),
        LAYOUT,
        10**9,
    )
    cand, v_far = exchange(exported, xm, xp, v_faces)
    grid, kinetic, overlaps, geometry, v_box = call(
        "ahead",
        whole_kernel(lambda a, b, c, d, unused, t: ahead_body(a, b, c, d, t)),
        (
            shape((128, 512), F32),
            shape((128, 512), F32),
            shape((128, 128), F32),
            shape((128, 128), F32),
            shape((128, 512)),
        ),
        (split, octant, places, v_own, table),
        AHEAD + FIRST,
        10**9,
    )
    current, sent, v_box, near, to_low, to_high = call(
        "first",
        first_kernel,
        (
            shape((128, 512)),
            shape((64, 512)),
            shape((128, 512)),
            shape((128, 448)),
            shape((32, 512)),
            shape((32, 512)),
        ),
        (octant, places, table, grid, kinetic, overlaps, geometry, v_box, cand, v_far),
        FIRST,
        10**9,
    )
    xm, xp = exchange_x(to_low, to_high)
    cand = exchange(sent, xm, xp, None)
    done, applied_bf = call(
        "second",
        whole_kernel(second_body),
        (shape((128, 512), F32), shape((128, 512))),
        (current, v_box, geometry),
        SECOND + LAST,
        10**9,
    )
    (relaxed,) = call(
        "last",
        whole_kernel(lambda *a: (last_body(*a),)),
        (shape((256, 256)),),
        (done, applied_bf, current, cand, near),
        LAST,
        10**9,
    )
    return relaxed.reshape(boxes.shape)


def solution(mesh):
    placed = (
        P("gx", "gy", "gz", None, None, None),
        P("gx", "gy", "gz", None, None),
        P("gx", "gy", "gz"),
    )
    return jax.shard_map(
        local,
        mesh=mesh,
        in_specs=placed,
        out_specs=P("gx", "gy", "gz", None, None, None),
        check_vma=False,
    )
```

```python
import functools

import jax
import jax.numpy as jnp
import ml_dtypes
import numpy as np
from jax import lax
from jax.experimental import pallas as pl
from jax.experimental.pallas import tpu as pltpu
from jax.sharding import PartitionSpec as P

F32 = jnp.float32
BF16 = jnp.bfloat16

MAGIC = [
    8.433424733352934e-07,
    -1.290557201342061e-05,
    8.76298447621056e-05,
    -0.00030158038132690465,
    0.001747237136729939,
    -0.009420470302010804,
    0.023738214637249424,
    0.0612625895831208,
    0.9940415697834004,
    -0.06048952891969835,
    -0.021030251609303816,
    0.013372634148547948,
    -0.0034412814449349387,
    0.0004944322768868992,
    -5.185986881173433e-05,
    2.7273449291197967e-06,
]
KINETIC = [
    -3.55369228991319,
    2.2191465938911166,
    -0.6156141465570069,
    0.2371780582153806,
    -0.0822663999742123,
    0.0220702918848226,
    -0.004097656893426338,
    0.00045167920287502236,
    -2.3982285245075998e-05,
    2.0904234952920368e-06,
    -3.7230763047369276e-07,
    -1.0585705549674146e-08,
    -5.8138798302825405e-11,
    2.7080049362631943e-13,
    -6.9244749406392e-18,
]
CELL = 1.0 / 4096.0
STEP = 0.1
PENALTY = 3.0

META = 128
VEDGE = (0, 1, 4)
SLAB = (0, 1, 4)


def split_parts(values):
    high = values.astype(ml_dtypes.bfloat16)
    low = (values - high.astype(np.float64)).astype(ml_dtypes.bfloat16)
    return high, low


def half_of(rows, size, keep):
    if isinstance(rows, list):
        return [r for i, r in enumerate(rows) if i // size % 2 == keep]
    count = rows.shape[0] // (2 * size)
    return rows.reshape(count, 2, size, rows.shape[1])[:, keep].reshape(count * size, -1)


def candidate_rows():
    own = [
        ((0, 0, 0), "border", (qy, qz, qx), k)
        for qy in range(2)
        for qz in range(2)
        for qx in range(2)
        for k in range(8)
    ]

    def moved(rows, axis, step):
        return [
            (d[:axis] + (d[axis] + step,) + d[axis + 1 :], kind, q, k) for d, kind, q, k in rows
        ]

    def onward(parts):
        low = moved(sum((half_of(r, 32, 1) for r in parts), []), 1, -1)
        high = moved(sum((half_of(r, 32, 0) for r in parts), []), 1, 1)
        parts = parts + [low, high]
        far_low = moved(sum((half_of(r, 16, 1) for r in parts), []), 2, -1)
        far_high = moved(sum((half_of(r, 16, 0) for r in parts), []), 2, 1)
        return low + high + far_low + far_high

    left, right = moved(own, 0, -1), moved(own, 0, 1)
    inner = [((d, 0, 0), "inner", (0, 0, 0), k) for d in (-1, 1) for k in range(8)]
    first = left + right + inner + onward([own, left, right])
    facing = [
        ((2 * side - 1, 0, 0), "border", (qy, qz, 1 - side), k)
        for qy in range(2)
        for qz in range(2)
        for side in range(2)
        for k in range(8)
    ]
    return first, facing + onward([own, facing])


def second_groups():
    first, second = candidate_rows()
    return [first.index(second[r]) // 8 for r in range(0, len(second), 8)]


def code_number(place):
    return 256.0 * (place[0] + 5) + 16.0 * (place[1] + 5) + (place[2] + 5)


def placed(layer, pairs, axis=0):
    return [(layer, a, b) if axis == 0 else (a, layer, b) if axis == 1 else (a, b, layer) for a, b in pairs]


def filled(places, size):
    return places + [None] * (size - len(places))


def potential_blocks():
    on_y = [(0, b) for b in VEDGE]
    on_z = [(a, 0) for a in VEDGE]
    off = [(a, b) for a in (1, 4) for b in (1, 4)]
    x_low = (
        filled(placed(0, on_y) + placed(1, on_y), 8)
        + filled(placed(0, on_z) + placed(1, on_z), 8)
        + filled(placed(0, off) + placed(1, off), 8)
    )
    x_high = filled(placed(4, on_y) + placed(4, off), 8) + filled(placed(4, on_z), 8)
    y_low = filled(placed(0, [(a, b) for a in VEDGE for b in (1, 4)], 1), 8) + filled(
        placed(0, on_z, 1), 8
    )
    z_low = filled(placed(0, [(a, b) for a in VEDGE for b in VEDGE], 2), 16)
    return x_low, x_high, y_low, z_low


def carried(block, axis, layer, step):
    return [
        None
        if p is None or (layer is not None and p[axis] != layer)
        else p[:axis] + (p[axis] + step,) + p[axis + 1 :]
        for p in block
    ]


@functools.cache
def tables():
    out = {}
    magic = np.zeros((16, 16))
    kinetic = np.zeros((16, 16))
    for r in range(16):
        for c in range(16):
            if 0 <= c - r + 8 < 16:
                magic[r, c] = MAGIC[c - r + 8]
            if abs(c - r) < 15:
                kinetic[r, c] = KINETIC[abs(c - r)]
    eye = np.eye(16)
    full = np.eye(256)
    row_of = np.array(
        [f * 16 + px * 8 + x8 for x8 in range(8) for px in range(2) for f in range(16)]
    )
    lane_of = np.array(
        [
            (py * 8 + y8) * 16 + pz * 8 + z8
            for py in range(2)
            for pz in range(2)
            for y8 in range(8)
            for z8 in range(8)
        ]
    )
    prow = full[row_of]
    pcol = full[:, lane_of]
    out["prow"], out["prow_t"] = prow, prow.T
    out["pcol"], out["pcol_t"] = pcol, pcol.T
    pair = np.kron(magic, magic)[np.ix_(lane_of, lane_of)] - full
    out["yz"], out["yz_t"] = pair.T, pair
    along = np.kron(eye, magic)[np.ix_(row_of, row_of)] - full
    out["x"], out["x_t"] = along, along.T
    second = (np.kron(kinetic, eye) + np.kron(eye, kinetic))[np.ix_(lane_of, lane_of)]
    out["kyz_h"], out["kyz_l"] = split_parts(-0.5 * second)
    along = np.kron(eye, kinetic)[np.ix_(row_of, row_of)]
    out["kx_h"], out["kx_l"] = split_parts(-0.5 * along)

    first, second = candidate_rows()
    names = [((0, 0, 0), "own", f) for f in range(16)]
    names += [((d, 0, 0), "border", k) for d in (-1, 1) for k in range(8)]
    columns = [((0, 0, 0), "own", c % 16) for c in range(128)]
    columns += [(d, kind, k) for d, kind, q, k in first]
    names += sorted(set(columns) - set(names))
    out["fold"] = np.zeros((len(columns), 256))
    for row, name in enumerate(columns):
        out["fold"][row, names.index(name)] = 1
    away = [0] * 128 + [1280 * d[0] + 80 * d[1] + 5 * d[2] for d, *_ in first]
    out["codes_away"] = np.broadcast_to(np.array(away) + code_number((0, 0, 0)), (8, len(away)))
    away = [1280 * d[0] + 80 * d[1] + 5 * d[2] for d, *_ in second]
    out["codes_last"] = np.broadcast_to(np.array(away) + code_number((0, 0, 0)), (8, len(away)))
    names = sorted({(d, kind, k) for d, kind, q, k in second})
    out["fold_last"] = np.zeros((len(second), 256))
    for row, (d, kind, q, k) in enumerate(second):
        out["fold_last"][row, names.index((d, kind, k))] = 1
    own = [None] * 200
    for z in range(5):
        for x in range(5):
            for y in range(5):
                own[z * 40 + x * 8 + y] = (x, y, z)
    x_low, x_high, y_low, z_low = potential_blocks()
    out["faces"] = np.zeros((32, 200))
    for row, place in enumerate(y_low + z_low):
        if place is not None:
            out["faces"][row, own.index(place)] = 1
    out["face_x"] = np.zeros((40, 72))
    for row, place in enumerate(x_low + x_high):
        if place is not None:
            x, y, z = place
            out["face_x"][row, VEDGE.index(z) * 24 + SLAB.index(x) * 8 + y] = 1
    far_x = carried(x_low, 0, None, 5)
    near_x = carried(x_high, 0, None, -5)
    far_y = carried(y_low + far_x[0:8] + near_x[0:8], 1, 0, 5)
    far_z = carried(
        z_low + far_x[8:16] + near_x[8:16] + far_y[8:16] + far_y[16:24] + far_y[24:32], 2, 0, 5
    )
    codes = []
    for place in far_x + near_x + far_y + far_z:
        code = -1.0 if place is None else code_number(place)
        codes.append(-1.0 if code in codes else code)
    out["codes_far"] = np.broadcast_to(np.array(codes), (8, len(codes)))
    codes = [-1.0 if p is None else code_number(p) for p in own]
    out["codes_own"] = np.broadcast_to(np.array(codes), (8, len(codes)))
    return {
        k: np.ascontiguousarray(
            v, dtype=np.float32 if k.startswith("codes") else ml_dtypes.bfloat16
        )
        for k, v in out.items()
    }


def dot(a, b):
    return lax.dot_general(a, b, (((1,), (0,)), ((), ())), preferred_element_type=F32)


def dot_nt(a, b):
    return lax.dot_general(a, b, (((1,), (1,)), ((), ())), preferred_element_type=F32)


def rolled(values):
    return pltpu.roll(values, 64, 1)


def iota(dims, axis):
    return lax.broadcasted_iota(jnp.int32, dims, axis)


def low_lanes(values):
    return iota(values.shape, 1) < 64


def to_octants(split, roll):
    rows = split.shape[0] // 8
    blocks = []
    for py in range(split.shape[1] // 128):
        here = split[:, py * 128 : (py + 1) * 128]
        other = roll(here)
        for pz in range(2):
            pieces = []
            for x8 in range(0, 8, 2):
                one = slice(x8 * rows, (x8 + 1) * rows)
                two = slice((x8 + 1) * rows, (x8 + 2) * rows)
                if pz == 0:
                    left, right = here[one], other[two]
                else:
                    left, right = other[one], here[two]
                pieces.append(jnp.where(low_lanes(left), left, right))
            blocks.append(jnp.concatenate(pieces, axis=1))
    return blocks


def to_octant(split, roll):
    return jnp.concatenate(to_octants(split, roll), axis=0)


def to_split(octant, roll):
    columns = []
    for py in range(2):
        first = octant[(2 * py) * 32 : (2 * py + 1) * 32]
        second = octant[(2 * py + 1) * 32 : (2 * py + 2) * 32]
        pieces = []
        for pair in range(4):
            lanes = slice(pair * 128, (pair + 1) * 128)
            one, two = first[:, lanes], second[:, lanes]
            pieces.append(jnp.where(low_lanes(one), one, roll(two)))
            pieces.append(jnp.where(low_lanes(one), roll(one), two))
        columns.append(jnp.concatenate(pieces, axis=0))
    return jnp.concatenate(columns, axis=1)


def octant_places(anchor):
    row = iota((8, 16), 0)
    base = jnp.zeros((8, 16), F32)
    for c in range(3):
        base = jnp.where(row == c, jnp.broadcast_to(anchor[c], (8, 16)), base)
    spread = (iota((16, 128), 0) == iota((16, 128), 1) % 16).astype(F32).astype(BF16)
    base = dot(base.astype(BF16), spread)
    turned = jnp.concatenate([base] * 16, axis=0).T
    row, lane = iota((128, 128), 0), iota((128, 128), 1)
    bit = jnp.where(lane == 0, row // 16, jnp.where(lane == 1, row // 64, row // 32)) % 2
    return jnp.where(lane < 3, turned + bit.astype(F32), 0.0), base


def lift_table(y8):
    row, lane = iota((40, 384), 0), iota((40, 384), 1)
    match = (lane // 64 == row // 8) & (lane % 8 == row % 8) & ((lane // 8) % 8 == y8)
    return match.astype(F32).astype(BF16)


def across(values):
    eye = (iota((8, 128), 0) == iota((8, 128), 1)).astype(F32).astype(BF16)
    return dot_nt(eye, values.astype(BF16))


def export_tables(base):
    edge = ((base == 0.0) | (base == 4.0)).astype(F32)
    edge = jnp.maximum(jnp.maximum(edge[0:1], edge[1:2]), edge[2:3])
    row, lane = iota((128, 128), 0), iota((128, 128), 1)
    before = (row < lane % 16).astype(F32).astype(BF16)
    before = jnp.where(row < 16, before, jnp.zeros_like(before))
    rank = dot(jnp.broadcast_to(edge, (8, 128)).astype(BF16), before)[0:1]
    row, lane = iota((64, 128), 0), iota((64, 128), 1)
    chosen = (rank == (row % 8).astype(F32)) & (edge > 0.5) & (row // 8 == lane // 16)
    row, lane = iota((16, 128), 0), iota((16, 128), 1)
    rank = (lane % 16).astype(F32) - rank
    inner = (
        (rank == (row % 8).astype(F32))
        & (edge < 0.5)
        & (row // 8 == (lane // 16) % 2)
        & ((lane // 64 == 1) == (base[1:2] == 3.0))
        & (((lane // 32) % 2 == 1) == (base[2:3] == 3.0))
    )
    return chosen.astype(F32).astype(BF16), inner.astype(F32).astype(BF16)


def same_function():
    return (iota((128, 128), 0) % 16 == iota((128, 128), 1) % 16).astype(F32)


def over_octants(values):
    total = values[0:16]
    for p in range(1, 8):
        total = total + values[16 * p : 16 * p + 16]
    return total


def summed(values, table):
    high = values.astype(BF16)
    low = (values - high.astype(F32)).astype(BF16)
    both = dot(jnp.concatenate([high, low], axis=0), table)
    return both[:16] + both[16:]


def repeated(values):
    return jnp.concatenate([values] * 8, axis=0)


def function_rows(boxes, anchor, t, roll):
    places, base = octant_places(anchor)
    table, inner = export_tables(base)
    split = dot(dot(t["prow"](), boxes).astype(BF16), t["pcol"]())
    octant = to_octant(split, roll).astype(BF16)
    wide = jnp.concatenate([octant, places.astype(BF16)], axis=1)
    return split.astype(BF16), octant, wide, places, table, inner


def regroup_table(layers):
    row, lane = iota((8 * layers, 40 * layers), 0), iota((8 * layers, 40 * layers), 1)
    target = jnp.where(row % 8 < 5, row // 8 * 40 + row % 8, -400)
    blocks = [(lane == target + 5 * x8).astype(F32).astype(BF16) for x8 in range(8)]
    return jnp.concatenate(blocks, axis=0)


def lifted_rows(potential_rows):
    total = None
    for y8 in range(8):
        part = dot(potential_rows(y8).astype(BF16), lift_table(y8))
        total = part if total is None else total + part
    return total.astype(BF16)


def with_meta(rows):
    return jnp.concatenate([rows, jnp.zeros((rows.shape[0], META), BF16)], axis=1)


PACK = ("prow", "pcol", "face_x")


def pack_body(boxes, anchor, slab_rows, t, roll=rolled):
    _, _, wide, _, table, inner = function_rows(boxes(), anchor(), t, roll)
    exported = dot(table, wide).astype(BF16)
    corners = dot(inner, wide)
    by_z = to_octants(dot(regroup_table(3), lifted_rows(slab_rows)), roll)
    slab = jnp.concatenate([by_z[z] for z in VEDGE], axis=0).astype(BF16)
    face = dot(t["face_x"](), slab)
    face = jnp.concatenate([face, jnp.zeros((40, META), F32)], axis=1)
    low = jnp.concatenate([corners[0:8], face[0:24]], axis=0).astype(BF16)
    high = jnp.concatenate([corners[8:16], face[24:40]], axis=0).astype(BF16)
    return exported, low, high


LAYOUT = ("prow", "pcol", "faces")


def layout_body(boxes, anchor, potential_rows, t, roll=rolled):
    split, octant, wide, places, table, _ = function_rows(boxes, anchor, t, roll)
    exported = dot(table, wide).astype(BF16)
    by_z = to_octants(dot(regroup_table(5), lifted_rows(potential_rows)), roll)
    v_rows = jnp.concatenate(by_z[:5], axis=0).astype(BF16)
    v_faces = with_meta(dot(t["faces"](), v_rows).astype(BF16))
    return exported, v_faces, split, octant, v_rows, places, table


def grid_values(split, t, roll):
    inner = split.astype(F32) + dot(split, t["yz"]())
    return to_octant(inner + dot(t["x"](), inner.astype(BF16)), roll)


def kinetic_values(split, t, roll):
    lanes = dot(split, t["kyz_h"]()) + dot(split, t["kyz_l"]())
    rows = dot(t["kx_h"](), split) + dot(t["kx_l"](), split)
    return to_octant(lanes + rows, roll)


def returned_values(weighted, t, roll):
    split = to_split(weighted, roll)
    inner = split + dot(split.astype(BF16), t["yz_t"]())
    return to_octant(inner + dot(t["x_t"](), inner.astype(BF16)), roll)


def own_weights(overlaps, applied_bf, octant, geometry):
    products = over_octants((dot_nt(applied_bf, octant) * CELL - overlaps) * geometry)
    same = same_function()
    coupling = summed(products, same.astype(BF16)) + PENALTY * same[:16]
    return (repeated(coupling) * geometry).astype(BF16)


OPERATE = ("yz", "x", "kyz_h", "kyz_l", "kx_h", "kx_l")


def row_codes(places):
    x, y, z = (places[:, c : c + 1] + 5.0 for c in range(3))
    return 256.0 * x + 16.0 * y + z


def lane_codes(places):
    lanes = across(places)
    return 256.0 * lanes[0:1] + 16.0 * lanes[1:2] + lanes[2:3]


def picked(code, codes, rows):
    return dot((code == codes[0:1]).astype(F32).astype(BF16), rows)


def beside(left, right):
    pieces = []
    for q in range(8):
        pieces += [left[8 * q : 8 * q + 8], right[8 * q : 8 * q + 8]]
    return jnp.concatenate(pieces, axis=0)


def ahead_body(split, octant, places, v_own, xm, xp, t, roll=rolled):
    left, right = xm[:64].astype(F32), xp[:64].astype(F32)
    side = beside(left[:, :512], right[:, :512])
    side_split = to_split(side, roll).astype(BF16)
    shift = jnp.where(iota((64, META), 1) == 0, 5.0, 0.0)
    side_places = beside(left[:, 512:] - shift, right[:, 512:] + shift)
    code = row_codes(jnp.concatenate([places, side_places], axis=0))
    v_box = picked(code, t["codes_own"](), v_own).astype(BF16)
    grid = [grid_values(r, t, roll) for r in (split, side_split)]
    kinetic = [kinetic_values(r, t, roll) for r in (split, side_split)]
    target = jnp.concatenate([octant, side.astype(BF16)], axis=0)
    code = jnp.broadcast_to(code, (256, 128))
    return jnp.concatenate(grid, axis=0), jnp.concatenate(kinetic, axis=0), v_box, target, code


FIRST = ("yz_t", "x_t", "fold", "codes_away", "codes_far")
AHEAD = OPERATE + ("codes_own",)


def first_body(target, code, places, table, grid, kinetic, v_box, cand, v_far, t, roll=rolled):
    code = code[:, 0:1]
    v_box = v_box.astype(F32) + picked(code, t["codes_far"](), v_far)
    weighted = grid * v_box
    applied = [returned_values(weighted[r], t, roll) for r in (slice(0, 128), slice(128, 256))]
    applied = jnp.concatenate(applied, axis=0) + kinetic
    applied_bf = applied.astype(BF16)
    meta = jnp.concatenate([places.astype(BF16), cand[:, 512:]], axis=0)
    same_place = code == lane_codes(meta) + t["codes_away"]()[0:1]
    rows = jnp.concatenate([target[:128], cand[:, :512]], axis=0)
    products = dot_nt(applied_bf, rows) - PENALTY * dot_nt(target, rows)
    products = jnp.where(same_place, products * CELL, 0.0)
    products = jnp.concatenate(
        [over_octants(products[:128]), over_octants(products[128:])], axis=0
    )
    coupling = folded(products, t["fold"]())
    identity = (iota((32, 256), 0) == iota((32, 256), 1)).astype(F32)
    coupling = dot_nt((coupling + PENALTY * identity).astype(BF16), t["fold"]())
    coupling = jnp.concatenate([coupling[:16]] * 8 + [coupling[16:]] * 8, axis=0)
    weights = jnp.where(same_place, coupling, 0.0).astype(BF16)
    correction = dot(weights, rows)
    current = (target.astype(F32) - STEP * (applied - correction)).astype(BF16)
    sent = dot(table, current[:128]).astype(BF16)
    side = current[128:].astype(F32)
    facing = []
    for q in range(4):
        facing += [side[32 * q + 16 : 32 * q + 24], side[32 * q + 8 : 32 * q + 16]]
    facing = jnp.concatenate(facing, axis=0).astype(BF16)
    return current[:128], sent, facing, v_box[:128].astype(BF16)


def folded(values, table):
    count = values.shape[0]
    high = values.astype(BF16)
    low = (values - high.astype(F32)).astype(BF16)
    both = dot(jnp.concatenate([high, low], axis=0), table)
    return both[:count] + both[count:]


SECOND = OPERATE + ("yz_t", "x_t", "codes_last")


def second_body(octant, v_box, places, cand, t, roll=rolled):
    split = to_split(octant.astype(F32), roll).astype(BF16)
    weighted = grid_values(split, t, roll) * v_box.astype(F32)
    applied = returned_values(weighted, t, roll) + kinetic_values(split, t, roll)
    applied_bf = applied.astype(BF16)
    code = row_codes(places)
    geometry = (code == lane_codes(places) + code_number((0, 0, 0))).astype(F32)
    overlaps = dot_nt(octant, octant) * (CELL * PENALTY)
    own_w = own_weights(overlaps, applied_bf, octant, geometry)
    done = octant.astype(F32) - STEP * (applied - dot(own_w, octant))
    meta = cand[:, 512:].astype(F32)
    meta = jnp.concatenate([meta[8 * g : 8 * g + 8] for g in second_groups()], axis=0)
    near = (code == lane_codes(meta) + t["codes_last"]()[0:1]).astype(F32)
    return done, applied_bf, near.astype(BF16)


LAST = ("fold_last", "prow_t", "pcol_t")


def last_body(done, applied_bf, octant, cand, near, t, roll=rolled):
    near = near.astype(F32)
    products = dot_nt(applied_bf, cand) - PENALTY * dot_nt(octant, cand)
    coupling = folded(over_octants(products * CELL * near), t["fold_last"]())
    coupling = dot_nt(coupling.astype(BF16), t["fold_last"]())
    weights = (repeated(coupling) * near).astype(BF16)
    current = (done + STEP * dot(weights, cand)).astype(BF16)
    split = to_split(current.astype(F32), roll).astype(BF16)
    return dot(dot(t["prow_t"](), split).astype(BF16), t["pcol_t"]()).astype(BF16)


def shape(dims, dtype=BF16):
    return jax.ShapeDtypeStruct(dims, dtype)


class Fetched:
    def __init__(self, source, target, semaphore):
        self.copy = pltpu.make_async_copy(source, target, semaphore)
        self.target = target
        self.waiting = True
        self.copy.start()

    def ref(self):
        if self.waiting:
            self.copy.wait()
            self.waiting = False
        return self.target

    def __call__(self):
        return self.ref()[...]


def call(name, body, out_shape, inputs, consts, flops):
    arrays = list(inputs) + [jnp.asarray(tables()[k]) for k in consts]

    def kernel(*refs):
        t = {
            k: functools.partial(lambda ref: ref[...], r)
            for k, r in zip(consts, refs[len(inputs) : len(arrays)])
        }
        body(refs[: len(inputs)], t, refs[len(arrays) :])

    return pl.pallas_call(
        kernel,
        out_shape=out_shape,
        in_specs=[pl.BlockSpec(memory_space=pltpu.VMEM)] * len(arrays),
        out_specs=tuple(pl.BlockSpec(memory_space=pltpu.VMEM) for _ in out_shape),
        compiler_params=pltpu.CompilerParams(vmem_limit_bytes=24 << 20),
        cost_estimate=pl.CostEstimate(
            flops=flops, bytes_accessed=flops // 1000, transcendentals=0
        ),
        name=name,
    )(*arrays)


def pack_call(boxes, anchor, rows):
    wide = 512 + META
    arrays = [boxes, anchor, rows, rows] + [jnp.asarray(tables()[k]) for k in PACK]
    shapes = [(a.shape, a.dtype) for a in arrays]
    shapes[2:4] = [((960, 40), F32)]
    out_shape = (shape((96, wide)), shape((88, wide)))
    count = len(arrays)

    def kernel(*refs):
        sources = list(refs[:count])
        sources[2] = sources[2].at[pl.ds(0, 640)]
        sources[3] = sources[3].at[pl.ds(1280, 320)]
        targets = refs[count : count + 2]
        scratch = list(refs[count + 2 : -1])
        semaphores = refs[-1]
        low, high = scratch[-2:]
        slab = scratch[2]
        landing = scratch[:2] + [slab.at[pl.ds(0, 640)], slab.at[pl.ds(640, 320)]] + scratch[3:-2]
        fetched = [
            Fetched(a, b, semaphores.at[i]) for i, (a, b) in enumerate(zip(sources, landing))
        ]
        for piece in fetched:
            piece.ref()
        exported, low_rest, high_rest = pack_body(
            fetched[0],
            lambda: fetched[1]()[0, 0].astype(F32),
            lambda y8: slab[pl.ds(y8, 120, stride=8), :],
            dict(zip(PACK, fetched[4:])),
        )
        copies = []
        for i, (message, rest) in enumerate(((low, low_rest), (high, high_rest))):
            message[...] = jnp.concatenate([exported, rest], axis=0)
            copies.append(pltpu.make_async_copy(message, targets[i], semaphores.at[count + i]))
            copies[-1].start()
        for copy in copies:
            copy.wait()

    return pl.pallas_call(
        kernel,
        out_shape=out_shape,
        in_specs=[pl.BlockSpec(memory_space=pltpu.HBM)] * count,
        out_specs=tuple(pl.BlockSpec(memory_space=pltpu.HBM) for _ in out_shape),
        scratch_shapes=[pltpu.VMEM(*a) for a in shapes]
        + [pltpu.VMEM(o.shape, o.dtype) for o in out_shape]
        + [pltpu.SemaphoreType.DMA((count + 2,))],
        compiler_params=pltpu.CompilerParams(vmem_limit_bytes=56 << 20),
        cost_estimate=pl.CostEstimate(flops=10**8, bytes_accessed=10**6, transcendentals=0),
        name="pack",
    )(*arrays)


def layout_kernel(ins, t, outs):
    boxes, anchor, potential = ins
    got = layout_body(
        boxes[...],
        anchor[...][0, 0].astype(F32),
        lambda y8: potential[pl.ds(y8, 200, stride=8), :],
        t,
    )
    for ref, value in zip(outs, got):
        ref[...] = value


def whole_kernel(body):
    def run(ins, t, outs):
        got = body(*[r[...] for r in ins], t)
        for ref, value in zip(outs, got):
            ref[...] = value

    return run


def passed_along(value, axis, step):
    count = lax.axis_size(axis)
    return lax.ppermute(value, axis, [(i, (i + step) % count) for i in range(count)])


def onward(parts, v_y=(), v_z=None, send=passed_along):
    low = [half_of(r, 32, 0) for r in parts] + list(v_y)
    yp = send(jnp.concatenate(low, axis=0), "gy", -1)
    ym = send(jnp.concatenate([half_of(r, 32, 1) for r in parts], axis=0), "gy", 1)
    size = ym.shape[0]
    parts = parts + [ym, yp[:size]]
    low = [half_of(r, 16, 0) for r in parts]
    if v_z is not None:
        low += v_z(yp[size:])
    zp = send(jnp.concatenate(low, axis=0), "gz", -1)
    zm = send(jnp.concatenate([half_of(r, 16, 1) for r in parts], axis=0), "gz", 1)
    far = zm.shape[0]
    return [ym, yp[:size], zm, zp[:far]], [yp[size:], zp[far:]]


def first_exchange(exported, xm, xp, v_faces, send=passed_along):
    v_far, v_near = xp[72:], xm[72:]

    def v_z(v_y):
        return [v_faces[16:], v_far[8:16], v_near[8:16], v_y[8:16], v_y[16:24], v_y[24:32]]

    rows, v_rest = onward(
        [exported, xm[:64], xp[:64]], [v_faces[:16], v_far[:8], v_near[:8]], v_z, send
    )
    rows = [xm[:64], xp[:64], xm[64:72], xp[64:72]] + rows
    v_rows = jnp.concatenate([v_far, v_near] + v_rest, axis=0)[:, :512]
    return jnp.concatenate(rows, axis=0), v_rows


def second_exchange(exported, facing, send=passed_along):
    rows, _ = onward([exported, facing], send=send)
    return jnp.concatenate([facing] + rows, axis=0)


def local(boxes, anchors, potential):
    wide = 512 + META
    own = boxes.reshape(256, 256)
    anchor = jnp.transpose(anchors, (0, 1, 4, 2, 3))
    rows = potential.reshape(1600, 40)
    to_low, to_high = pack_call(own, anchor, rows)
    xm = passed_along(to_high, "gx", 1)
    xp = passed_along(to_low, "gx", -1)
    exported, v_faces, split, octant, v_own, places, table = call(
        "layout",
        layout_kernel,
        (
            shape((64, wide)),
            shape((32, wide)),
            shape((256, 256)),
            shape((128, 512)),
            shape((200, 512)),
            shape((128, 128), F32),
            shape((64, 128)),
        ),
        (own, anchor, rows),
        LAYOUT,
        10**9,
    )
    cand, v_far = first_exchange(exported, xm, xp, v_faces)
    grid, kinetic, v_box, target, code = call(
        "ahead",
        whole_kernel(lambda *a: ahead_body(*a[:6], a[-1])),
        (
            shape((256, 512), F32),
            shape((256, 512), F32),
            shape((256, 512)),
            shape((256, 512)),
            shape((256, 128), F32),
        ),
        (split, octant, places, v_own, xm, xp, table),
        AHEAD + FIRST,
        10**9,
    )
    current, sent, facing, v_box = call(
        "first",
        whole_kernel(first_body),
        (shape((128, 512)), shape((64, 512)), shape((64, 512)), shape((128, 512))),
        (target, code, places, table, grid, kinetic, v_box, cand, v_far),
        FIRST,
        10**9,
    )
    near_rows = second_exchange(sent, facing)
    done, applied_bf, near = call(
        "second",
        whole_kernel(lambda *a: second_body(*a[:4], a[-1])),
        (shape((128, 512), F32), shape((128, 512)), shape((128, 448))),
        (current, v_box, places, cand),
        SECOND + LAST,
        10**9,
    )
    (relaxed,) = call(
        "last",
        whole_kernel(lambda *a: (last_body(*a),)),
        (shape((256, 256)),),
        (done, applied_bf, current, near_rows, near),
        LAST,
        10**9,
    )
    return relaxed.reshape(boxes.shape)


def solution(mesh):
    placed = (
        P("gx", "gy", "gz", None, None, None),
        P("gx", "gy", "gz", None, None),
        P("gx", "gy", "gz"),
    )
    return jax.shard_map(
        local,
        mesh=mesh,
        in_specs=placed,
        out_specs=P("gx", "gy", "gz", None, None, None),
        check_vma=False,
    )
```

```python
import functools

import jax
import jax.numpy as jnp
import ml_dtypes
import numpy as np
from jax import lax
from jax.experimental import pallas as pl
from jax.experimental.pallas import tpu as pltpu
from jax.sharding import PartitionSpec as P

F32 = jnp.float32
BF16 = jnp.bfloat16

MAGIC = [
    8.433424733352934e-07,
    -1.290557201342061e-05,
    8.76298447621056e-05,
    -0.00030158038132690465,
    0.001747237136729939,
    -0.009420470302010804,
    0.023738214637249424,
    0.0612625895831208,
    0.9940415697834004,
    -0.06048952891969835,
    -0.021030251609303816,
    0.013372634148547948,
    -0.0034412814449349387,
    0.0004944322768868992,
    -5.185986881173433e-05,
    2.7273449291197967e-06,
]
KINETIC = [
    -3.55369228991319,
    2.2191465938911166,
    -0.6156141465570069,
    0.2371780582153806,
    -0.0822663999742123,
    0.0220702918848226,
    -0.004097656893426338,
    0.00045167920287502236,
    -2.3982285245075998e-05,
    2.0904234952920368e-06,
    -3.7230763047369276e-07,
    -1.0585705549674146e-08,
    -5.8138798302825405e-11,
    2.7080049362631943e-13,
    -6.9244749406392e-18,
]
CELL = 1.0 / 4096.0
STEP = 0.1
PENALTY = 3.0

META = 128
VEDGE = (0, 1, 4)
SLAB = (0, 1, 4)


def split_parts(values):
    high = values.astype(ml_dtypes.bfloat16)
    low = (values - high.astype(np.float64)).astype(ml_dtypes.bfloat16)
    return high, low


def half_of(rows, size, keep):
    if isinstance(rows, list):
        return [r for i, r in enumerate(rows) if i // size % 2 == keep]
    count = rows.shape[0] // (2 * size)
    return rows.reshape(count, 2, size, rows.shape[1])[:, keep].reshape(count * size, -1)


def candidate_rows():
    own = [
        ((0, 0, 0), "border", (qy, qz, qx), k)
        for qy in range(2)
        for qz in range(2)
        for qx in range(2)
        for k in range(8)
    ]

    def moved(rows, axis, step):
        return [
            (d[:axis] + (d[axis] + step,) + d[axis + 1 :], kind, q, k) for d, kind, q, k in rows
        ]

    def onward(parts):
        low = moved(sum((half_of(r, 32, 1) for r in parts), []), 1, -1)
        high = moved(sum((half_of(r, 32, 0) for r in parts), []), 1, 1)
        parts = parts + [low, high]
        far_low = moved(sum((half_of(r, 16, 1) for r in parts), []), 2, -1)
        far_high = moved(sum((half_of(r, 16, 0) for r in parts), []), 2, 1)
        return low + high + far_low + far_high

    left, right = moved(own, 0, -1), moved(own, 0, 1)
    inner = [((d, 0, 0), "inner", (0, 0, 0), k) for d in (-1, 1) for k in range(8)]
    first = left + right + inner + onward([own, left, right])
    facing = [
        ((2 * side - 1, 0, 0), "border", (qy, qz, 1 - side), k)
        for qy in range(2)
        for qz in range(2)
        for side in range(2)
        for k in range(8)
    ]
    return first, facing + onward([own, facing])


def second_groups():
    first, second = candidate_rows()
    return [first.index(second[r]) // 8 for r in range(0, len(second), 8)]


def code_number(place):
    return 256.0 * (place[0] + 5) + 16.0 * (place[1] + 5) + (place[2] + 5)


def placed(layer, pairs, axis=0):
    return [(layer, a, b) if axis == 0 else (a, layer, b) if axis == 1 else (a, b, layer) for a, b in pairs]


def filled(places, size):
    return places + [None] * (size - len(places))


def potential_blocks():
    on_y = [(0, b) for b in VEDGE]
    on_z = [(a, 0) for a in VEDGE]
    off = [(a, b) for a in (1, 4) for b in (1, 4)]
    x_low = (
        filled(placed(0, on_y) + placed(1, on_y), 8)
        + filled(placed(0, on_z) + placed(1, on_z), 8)
        + filled(placed(0, off) + placed(1, off), 8)
    )
    x_high = filled(placed(4, on_y) + placed(4, off), 8) + filled(placed(4, on_z), 8)
    y_low = filled(placed(0, [(a, b) for a in VEDGE for b in (1, 4)], 1), 8) + filled(
        placed(0, on_z, 1), 8
    )
    z_low = filled(placed(0, [(a, b) for a in VEDGE for b in VEDGE], 2), 16)
    return x_low, x_high, y_low, z_low


def carried(block, axis, layer, step):
    return [
        None
        if p is None or (layer is not None and p[axis] != layer)
        else p[:axis] + (p[axis] + step,) + p[axis + 1 :]
        for p in block
    ]


@functools.cache
def tables():
    out = {}
    magic = np.zeros((16, 16))
    kinetic = np.zeros((16, 16))
    for r in range(16):
        for c in range(16):
            if 0 <= c - r + 8 < 16:
                magic[r, c] = MAGIC[c - r + 8]
            if abs(c - r) < 15:
                kinetic[r, c] = KINETIC[abs(c - r)]
    eye = np.eye(16)
    full = np.eye(256)
    row_of = np.array(
        [f * 16 + px * 8 + x8 for x8 in range(8) for px in range(2) for f in range(16)]
    )
    lane_of = np.array(
        [
            (py * 8 + y8) * 16 + pz * 8 + z8
            for py in range(2)
            for pz in range(2)
            for y8 in range(8)
            for z8 in range(8)
        ]
    )
    prow = full[row_of]
    pcol = full[:, lane_of]
    out["prow"], out["prow_t"] = prow, prow.T
    out["pcol"], out["pcol_t"] = pcol, pcol.T
    pair = np.kron(magic, magic)[np.ix_(lane_of, lane_of)] - full
    out["yz"], out["yz_t"] = pair.T, pair
    along = np.kron(eye, magic)[np.ix_(row_of, row_of)] - full
    out["x"], out["x_t"] = along, along.T
    second = (np.kron(kinetic, eye) + np.kron(eye, kinetic))[np.ix_(lane_of, lane_of)]
    out["kyz_h"], out["kyz_l"] = split_parts(-0.5 * second)
    along = np.kron(eye, kinetic)[np.ix_(row_of, row_of)]
    out["kx_h"], out["kx_l"] = split_parts(-0.5 * along)

    first, second = candidate_rows()
    names = [((0, 0, 0), "own", f) for f in range(16)]
    names += [((d, 0, 0), "border", k) for d in (-1, 1) for k in range(8)]
    columns = [((0, 0, 0), "own", c % 16) for c in range(128)]
    columns += [(d, kind, k) for d, kind, q, k in first]
    names += sorted(set(columns) - set(names))
    out["fold"] = np.zeros((len(columns), 256))
    for row, name in enumerate(columns):
        out["fold"][row, names.index(name)] = 1
    away = [0] * 128 + [1280 * d[0] + 80 * d[1] + 5 * d[2] for d, *_ in first]
    out["codes_away"] = np.broadcast_to(np.array(away) + code_number((0, 0, 0)), (8, len(away)))
    away = [1280 * d[0] + 80 * d[1] + 5 * d[2] for d, *_ in second]
    out["codes_last"] = np.broadcast_to(np.array(away) + code_number((0, 0, 0)), (8, len(away)))
    names = sorted({(d, kind, k) for d, kind, q, k in second})
    out["fold_last"] = np.zeros((len(second), 256))
    for row, (d, kind, q, k) in enumerate(second):
        out["fold_last"][row, names.index((d, kind, k))] = 1
    own = [None] * 200
    for z in range(5):
        for x in range(5):
            for y in range(5):
                own[z * 40 + x * 8 + y] = (x, y, z)
    x_low, x_high, y_low, z_low = potential_blocks()
    out["faces"] = np.zeros((32, 200))
    for row, place in enumerate(y_low + z_low):
        if place is not None:
            out["faces"][row, own.index(place)] = 1
    out["face_x"] = np.zeros((40, 72))
    for row, place in enumerate(x_low + x_high):
        if place is not None:
            x, y, z = place
            out["face_x"][row, VEDGE.index(z) * 24 + SLAB.index(x) * 8 + y] = 1
    far_x = carried(x_low, 0, None, 5)
    near_x = carried(x_high, 0, None, -5)
    far_y = carried(y_low + far_x[0:8] + near_x[0:8], 1, 0, 5)
    far_z = carried(
        z_low + far_x[8:16] + near_x[8:16] + far_y[8:16] + far_y[16:24] + far_y[24:32], 2, 0, 5
    )
    codes = []
    for place in far_x + near_x + far_y + far_z:
        code = -1.0 if place is None else code_number(place)
        codes.append(-1.0 if code in codes else code)
    out["codes_far"] = np.broadcast_to(np.array(codes), (8, len(codes)))
    codes = [-1.0 if p is None else code_number(p) for p in own]
    out["codes_own"] = np.broadcast_to(np.array(codes), (8, len(codes)))
    return {
        k: np.ascontiguousarray(
            v, dtype=np.float32 if k.startswith("codes") else ml_dtypes.bfloat16
        )
        for k, v in out.items()
    }


def dot(a, b):
    return lax.dot_general(a, b, (((1,), (0,)), ((), ())), preferred_element_type=F32)


def dot_nt(a, b):
    return lax.dot_general(a, b, (((1,), (1,)), ((), ())), preferred_element_type=F32)


def rolled(values):
    return pltpu.roll(values, 64, 1)


def iota(dims, axis):
    return lax.broadcasted_iota(jnp.int32, dims, axis)


def low_lanes(values):
    return iota(values.shape, 1) < 64


def to_octants(split, roll):
    rows = split.shape[0] // 8
    blocks = []
    for py in range(split.shape[1] // 128):
        here = split[:, py * 128 : (py + 1) * 128]
        other = roll(here)
        for pz in range(2):
            pieces = []
            for x8 in range(0, 8, 2):
                one = slice(x8 * rows, (x8 + 1) * rows)
                two = slice((x8 + 1) * rows, (x8 + 2) * rows)
                if pz == 0:
                    left, right = here[one], other[two]
                else:
                    left, right = other[one], here[two]
                pieces.append(jnp.where(low_lanes(left), left, right))
            blocks.append(jnp.concatenate(pieces, axis=1))
    return blocks


def to_octant(split, roll):
    return jnp.concatenate(to_octants(split, roll), axis=0)


def to_split(octant, roll):
    columns = []
    for py in range(2):
        first = octant[(2 * py) * 32 : (2 * py + 1) * 32]
        second = octant[(2 * py + 1) * 32 : (2 * py + 2) * 32]
        pieces = []
        for pair in range(4):
            lanes = slice(pair * 128, (pair + 1) * 128)
            one, two = first[:, lanes], second[:, lanes]
            pieces.append(jnp.where(low_lanes(one), one, roll(two)))
            pieces.append(jnp.where(low_lanes(one), roll(one), two))
        columns.append(jnp.concatenate(pieces, axis=0))
    return jnp.concatenate(columns, axis=1)


def octant_places(anchor):
    row = iota((8, 16), 0)
    base = jnp.zeros((8, 16), F32)
    for c in range(3):
        base = jnp.where(row == c, jnp.broadcast_to(anchor[c], (8, 16)), base)
    spread = (iota((16, 128), 0) == iota((16, 128), 1) % 16).astype(F32).astype(BF16)
    base = dot(base.astype(BF16), spread)
    turned = jnp.concatenate([base] * 16, axis=0).T
    row, lane = iota((128, 128), 0), iota((128, 128), 1)
    bit = jnp.where(lane == 0, row // 16, jnp.where(lane == 1, row // 64, row // 32)) % 2
    return jnp.where(lane < 3, turned + bit.astype(F32), 0.0), base


def lift_table(y8):
    row, lane = iota((40, 384), 0), iota((40, 384), 1)
    match = (lane // 64 == row // 8) & (lane % 8 == row % 8) & ((lane // 8) % 8 == y8)
    return match.astype(F32).astype(BF16)


def across(values):
    eye = (iota((8, 128), 0) == iota((8, 128), 1)).astype(F32).astype(BF16)
    return dot_nt(eye, values.astype(BF16))


def export_tables(base):
    edge = ((base == 0.0) | (base == 4.0)).astype(F32)
    edge = jnp.maximum(jnp.maximum(edge[0:1], edge[1:2]), edge[2:3])
    row, lane = iota((128, 128), 0), iota((128, 128), 1)
    before = (row < lane % 16).astype(F32).astype(BF16)
    before = jnp.where(row < 16, before, jnp.zeros_like(before))
    rank = dot(jnp.broadcast_to(edge, (8, 128)).astype(BF16), before)[0:1]
    row, lane = iota((64, 128), 0), iota((64, 128), 1)
    chosen = (rank == (row % 8).astype(F32)) & (edge > 0.5) & (row // 8 == lane // 16)
    row, lane = iota((16, 128), 0), iota((16, 128), 1)
    rank = (lane % 16).astype(F32) - rank
    inner = (
        (rank == (row % 8).astype(F32))
        & (edge < 0.5)
        & (row // 8 == (lane // 16) % 2)
        & ((lane // 64 == 1) == (base[1:2] == 3.0))
        & (((lane // 32) % 2 == 1) == (base[2:3] == 3.0))
    )
    return chosen.astype(F32).astype(BF16), inner.astype(F32).astype(BF16)


def same_function():
    return (iota((128, 128), 0) % 16 == iota((128, 128), 1) % 16).astype(F32)


def over_octants(values):
    total = values[0:16]
    for p in range(1, 8):
        total = total + values[16 * p : 16 * p + 16]
    return total


def summed(values, table):
    high = values.astype(BF16)
    low = (values - high.astype(F32)).astype(BF16)
    both = dot(jnp.concatenate([high, low], axis=0), table)
    return both[:16] + both[16:]


def repeated(values):
    return jnp.concatenate([values] * 8, axis=0)


def function_rows(boxes, anchor, t, roll):
    places, base = octant_places(anchor)
    table, inner = export_tables(base)
    split = dot(dot(t["prow"](), boxes).astype(BF16), t["pcol"]())
    octant = to_octant(split, roll).astype(BF16)
    wide = jnp.concatenate([octant, places.astype(BF16)], axis=1)
    return split.astype(BF16), octant, wide, places, table, inner


def regroup_table(layers):
    row, lane = iota((8 * layers, 40 * layers), 0), iota((8 * layers, 40 * layers), 1)
    target = jnp.where(row % 8 < 5, row // 8 * 40 + row % 8, -400)
    blocks = [(lane == target + 5 * x8).astype(F32).astype(BF16) for x8 in range(8)]
    return jnp.concatenate(blocks, axis=0)


def lifted_rows(potential_rows):
    total = None
    for y8 in range(8):
        part = dot(potential_rows(y8).astype(BF16), lift_table(y8))
        total = part if total is None else total + part
    return total.astype(BF16)


def with_meta(rows):
    return jnp.concatenate([rows, jnp.zeros((rows.shape[0], META), BF16)], axis=1)


PACK = ("prow", "pcol", "face_x")


def pack_body(boxes, anchor, slab_rows, t, roll=rolled):
    _, _, wide, _, table, inner = function_rows(boxes(), anchor(), t, roll)
    exported = dot(table, wide).astype(BF16)
    corners = dot(inner, wide)
    by_z = to_octants(dot(regroup_table(3), lifted_rows(slab_rows)), roll)
    slab = jnp.concatenate([by_z[z] for z in VEDGE], axis=0).astype(BF16)
    face = dot(t["face_x"](), slab)
    face = jnp.concatenate([face, jnp.zeros((40, META), F32)], axis=1)
    low = jnp.concatenate([corners[0:8], face[0:24]], axis=0).astype(BF16)
    high = jnp.concatenate([corners[8:16], face[24:40]], axis=0).astype(BF16)
    return exported, low, high


LAYOUT = ("prow", "pcol", "faces")


def layout_body(boxes, anchor, potential_rows, t, roll=rolled):
    split, octant, wide, places, table, _ = function_rows(boxes, anchor, t, roll)
    exported = dot(table, wide).astype(BF16)
    by_z = to_octants(dot(regroup_table(5), lifted_rows(potential_rows)), roll)
    v_rows = jnp.concatenate(by_z[:5], axis=0).astype(BF16)
    v_faces = with_meta(dot(t["faces"](), v_rows).astype(BF16))
    return exported, v_faces, split, octant, v_rows, places, table


def grid_values(split, t, roll):
    inner = split.astype(F32) + dot(split, t["yz"]())
    return to_octant(inner + dot(t["x"](), inner.astype(BF16)), roll)


def kinetic_values(split, t, roll):
    lanes = dot(split, t["kyz_h"]()) + dot(split, t["kyz_l"]())
    rows = dot(t["kx_h"](), split) + dot(t["kx_l"](), split)
    return to_octant(lanes + rows, roll)


def returned_values(weighted, t, roll):
    split = to_split(weighted, roll)
    inner = split + dot(split.astype(BF16), t["yz_t"]())
    return to_octant(inner + dot(t["x_t"](), inner.astype(BF16)), roll)


def own_weights(overlaps, applied_bf, octant, geometry):
    products = over_octants((dot_nt(applied_bf, octant) * CELL - overlaps) * geometry)
    same = same_function()
    coupling = summed(products, same.astype(BF16)) + PENALTY * same[:16]
    return (repeated(coupling) * geometry).astype(BF16)


OPERATE = ("yz", "x", "kyz_h", "kyz_l", "kx_h", "kx_l")


def row_codes(places):
    x, y, z = (places[:, c : c + 1] + 5.0 for c in range(3))
    return 256.0 * x + 16.0 * y + z


def lane_codes(places):
    lanes = across(places)
    return 256.0 * lanes[0:1] + 16.0 * lanes[1:2] + lanes[2:3]


def picked(code, codes, rows):
    return dot((code == codes[0:1]).astype(F32).astype(BF16), rows)


def beside(left, right):
    pieces = []
    for q in range(8):
        pieces += [left[8 * q : 8 * q + 8], right[8 * q : 8 * q + 8]]
    return jnp.concatenate(pieces, axis=0)


def ahead_body(split, octant, places, v_own, xm, xp, t, roll=rolled):
    left, right = xm[:64].astype(F32), xp[:64].astype(F32)
    side = beside(left[:, :512], right[:, :512])
    side_split = to_split(side, roll).astype(BF16)
    shift = jnp.where(iota((64, META), 1) == 0, 5.0, 0.0)
    side_places = beside(left[:, 512:] - shift, right[:, 512:] + shift)
    code = row_codes(jnp.concatenate([places, side_places], axis=0))
    v_box = picked(code, t["codes_own"](), v_own).astype(BF16)
    grid = [grid_values(r, t, roll) for r in (split, side_split)]
    kinetic = [kinetic_values(r, t, roll) for r in (split, side_split)]
    target = jnp.concatenate([octant, side.astype(BF16)], axis=0)
    code = jnp.broadcast_to(code, (256, 128))
    return jnp.concatenate(grid, axis=0), jnp.concatenate(kinetic, axis=0), v_box, target, code


FIRST = ("yz_t", "x_t", "fold", "codes_away", "codes_far")
AHEAD = OPERATE + ("codes_own",)


def first_body(target, code, places, table, grid, kinetic, v_box, cand, v_far, t, roll=rolled):
    code = code[:, 0:1]
    v_box = v_box.astype(F32) + picked(code, t["codes_far"](), v_far)
    weighted = grid * v_box
    applied = [returned_values(weighted[r], t, roll) for r in (slice(0, 128), slice(128, 256))]
    applied = jnp.concatenate(applied, axis=0) + kinetic
    applied_bf = applied.astype(BF16)
    meta = jnp.concatenate([places.astype(BF16), cand[:, 512:]], axis=0)
    same_place = code == lane_codes(meta) + t["codes_away"]()[0:1]
    rows = jnp.concatenate([target[:128], cand[:, :512]], axis=0)
    products = dot_nt(applied_bf, rows) - PENALTY * dot_nt(target, rows)
    products = jnp.where(same_place, products * CELL, 0.0)
    products = jnp.concatenate(
        [over_octants(products[:128]), over_octants(products[128:])], axis=0
    )
    coupling = folded(products, t["fold"]())
    identity = (iota((32, 256), 0) == iota((32, 256), 1)).astype(F32)
    coupling = dot_nt((coupling + PENALTY * identity).astype(BF16), t["fold"]())
    coupling = jnp.concatenate([coupling[:16]] * 8 + [coupling[16:]] * 8, axis=0)
    weights = jnp.where(same_place, coupling, 0.0).astype(BF16)
    correction = dot(weights, rows)
    current = (target.astype(F32) - STEP * (applied - correction)).astype(BF16)
    sent = dot(table, current[:128]).astype(BF16)
    side = current[128:].astype(F32)
    facing = []
    for q in range(4):
        facing += [side[32 * q + 16 : 32 * q + 24], side[32 * q + 8 : 32 * q + 16]]
    facing = jnp.concatenate(facing, axis=0).astype(BF16)
    return current[:128], sent, facing, v_box[:128].astype(BF16)


def folded(values, table):
    count = values.shape[0]
    high = values.astype(BF16)
    low = (values - high.astype(F32)).astype(BF16)
    both = dot(jnp.concatenate([high, low], axis=0), table)
    return both[:count] + both[count:]


SECOND = OPERATE + ("yz_t", "x_t", "codes_last")


def second_body(octant, v_box, places, cand, t, roll=rolled):
    split = to_split(octant.astype(F32), roll).astype(BF16)
    weighted = grid_values(split, t, roll) * v_box.astype(F32)
    applied = returned_values(weighted, t, roll) + kinetic_values(split, t, roll)
    applied_bf = applied.astype(BF16)
    code = row_codes(places)
    geometry = (code == lane_codes(places) + code_number((0, 0, 0))).astype(F32)
    overlaps = dot_nt(octant, octant) * (CELL * PENALTY)
    own_w = own_weights(overlaps, applied_bf, octant, geometry)
    done = octant.astype(F32) - STEP * (applied - dot(own_w, octant))
    meta = cand[:, 512:].astype(F32)
    meta = jnp.concatenate([meta[8 * g : 8 * g + 8] for g in second_groups()], axis=0)
    near = (code == lane_codes(meta) + t["codes_last"]()[0:1]).astype(F32)
    return done, applied_bf, near.astype(BF16)


LAST = ("fold_last", "prow_t", "pcol_t")


def last_body(done, applied_bf, octant, cand, near, t, roll=rolled):
    near = near.astype(F32)
    products = dot_nt(applied_bf, cand) - PENALTY * dot_nt(octant, cand)
    coupling = folded(over_octants(products * CELL * near), t["fold_last"]())
    coupling = dot_nt(coupling.astype(BF16), t["fold_last"]())
    weights = (repeated(coupling) * near).astype(BF16)
    current = (done + STEP * dot(weights, cand)).astype(BF16)
    split = to_split(current.astype(F32), roll).astype(BF16)
    return dot(dot(t["prow_t"](), split).astype(BF16), t["pcol_t"]()).astype(BF16)


def shape(dims, dtype=BF16):
    return jax.ShapeDtypeStruct(dims, dtype)


class Fetched:
    def __init__(self, source, target, semaphore):
        self.copy = pltpu.make_async_copy(source, target, semaphore)
        self.target = target
        self.waiting = True
        self.copy.start()

    def ref(self):
        if self.waiting:
            self.copy.wait()
            self.waiting = False
        return self.target

    def __call__(self):
        return self.ref()[...]


def call(name, body, out_shape, inputs, consts, flops):
    arrays = list(inputs) + [jnp.asarray(tables()[k]) for k in consts]

    def kernel(*refs):
        t = {
            k: functools.partial(lambda ref: ref[...], r)
            for k, r in zip(consts, refs[len(inputs) : len(arrays)])
        }
        body(refs[: len(inputs)], t, refs[len(arrays) :])

    return pl.pallas_call(
        kernel,
        out_shape=out_shape,
        in_specs=[pl.BlockSpec(memory_space=pltpu.VMEM)] * len(arrays),
        out_specs=tuple(pl.BlockSpec(memory_space=pltpu.VMEM) for _ in out_shape),
        compiler_params=pltpu.CompilerParams(vmem_limit_bytes=24 << 20),
        cost_estimate=pl.CostEstimate(
            flops=flops, bytes_accessed=flops // 1000, transcendentals=0
        ),
        name=name,
    )(*arrays)


def pack_call(boxes, anchor, rows):
    wide = 512 + META
    arrays = [boxes, anchor, rows, rows] + [jnp.asarray(tables()[k]) for k in PACK]
    shapes = [(a.shape, a.dtype) for a in arrays]
    shapes[2:4] = [((960, 40), F32)]
    out_shape = (shape((96, wide)), shape((88, wide)))
    count = len(arrays)

    def kernel(*refs):
        sources = list(refs[:count])
        sources[2] = sources[2].at[pl.ds(0, 640)]
        sources[3] = sources[3].at[pl.ds(1280, 320)]
        targets = refs[count : count + 2]
        scratch = list(refs[count + 2 : -1])
        semaphores = refs[-1]
        low, high = scratch[-2:]
        slab = scratch[2]
        landing = scratch[:2] + [slab.at[pl.ds(0, 640)], slab.at[pl.ds(640, 320)]] + scratch[3:-2]
        fetched = [
            Fetched(a, b, semaphores.at[i]) for i, (a, b) in enumerate(zip(sources, landing))
        ]
        for piece in fetched:
            piece.ref()
        exported, low_rest, high_rest = pack_body(
            fetched[0],
            lambda: fetched[1]()[0, 0].astype(F32),
            lambda y8: slab[pl.ds(y8, 120, stride=8), :],
            dict(zip(PACK, fetched[4:])),
        )
        copies = []
        for i, (message, rest) in enumerate(((low, low_rest), (high, high_rest))):
            message[...] = jnp.concatenate([exported, rest], axis=0)
            copies.append(pltpu.make_async_copy(message, targets[i], semaphores.at[count + i]))
            copies[-1].start()
        for copy in copies:
            copy.wait()

    return pl.pallas_call(
        kernel,
        out_shape=out_shape,
        in_specs=[pl.BlockSpec(memory_space=pltpu.HBM)] * count,
        out_specs=tuple(pl.BlockSpec(memory_space=pltpu.HBM) for _ in out_shape),
        scratch_shapes=[pltpu.VMEM(*a) for a in shapes]
        + [pltpu.VMEM(o.shape, o.dtype) for o in out_shape]
        + [pltpu.SemaphoreType.DMA((count + 2,))],
        compiler_params=pltpu.CompilerParams(vmem_limit_bytes=56 << 20),
        cost_estimate=pl.CostEstimate(flops=10**8, bytes_accessed=10**6, transcendentals=0),
        name="pack",
    )(*arrays)


def layout_kernel(ins, t, outs):
    boxes, anchor, potential = ins
    got = layout_body(
        boxes[...],
        anchor[...][0, 0].astype(F32),
        lambda y8: potential[pl.ds(y8, 200, stride=8), :],
        t,
    )
    for ref, value in zip(outs, got):
        ref[...] = value


def whole_kernel(body):
    def run(ins, t, outs):
        got = body(*[r[...] for r in ins], t)
        for ref, value in zip(outs, got):
            ref[...] = value

    return run


def passed_along(value, axis, step):
    count = lax.axis_size(axis)
    return lax.ppermute(value, axis, [(i, (i + step) % count) for i in range(count)])


def onward(parts, v_y=(), v_z=None, send=passed_along):
    low = [half_of(r, 32, 0) for r in parts] + list(v_y)
    yp = send(jnp.concatenate(low, axis=0), "gy", -1)
    ym = send(jnp.concatenate([half_of(r, 32, 1) for r in parts], axis=0), "gy", 1)
    size = ym.shape[0]
    parts = parts + [ym, yp[:size]]
    low = [half_of(r, 16, 0) for r in parts]
    if v_z is not None:
        low += v_z(yp[size:])
    zp = send(jnp.concatenate(low, axis=0), "gz", -1)
    zm = send(jnp.concatenate([half_of(r, 16, 1) for r in parts], axis=0), "gz", 1)
    far = zm.shape[0]
    return [ym, yp[:size], zm, zp[:far]], [yp[size:], zp[far:]]


def first_exchange(exported, xm, xp, v_faces, send=passed_along):
    v_far, v_near = xp[72:], xm[72:]

    def v_z(v_y):
        return [v_faces[16:], v_far[8:16], v_near[8:16], v_y[8:16], v_y[16:24], v_y[24:32]]

    rows, v_rest = onward(
        [exported, xm[:64], xp[:64]], [v_faces[:16], v_far[:8], v_near[:8]], v_z, send
    )
    rows = [xm[:64], xp[:64], xm[64:72], xp[64:72]] + rows
    v_rows = jnp.concatenate([v_far, v_near] + v_rest, axis=0)[:, :512]
    return jnp.concatenate(rows, axis=0), v_rows


def second_exchange(exported, facing, send=passed_along):
    extra = facing[:8]
    rows, _ = onward([exported, facing], [extra], lambda _: [extra], send)
    return jnp.concatenate([facing] + rows, axis=0)


def local(boxes, anchors, potential):
    wide = 512 + META
    own = boxes.reshape(256, 256)
    anchor = jnp.transpose(anchors, (0, 1, 4, 2, 3))
    rows = potential.reshape(1600, 40)
    to_low, to_high = pack_call(own, anchor, rows)
    xm = passed_along(to_high, "gx", 1)
    xp = passed_along(to_low, "gx", -1)
    exported, v_faces, split, octant, v_own, places, table = call(
        "layout",
        layout_kernel,
        (
            shape((64, wide)),
            shape((32, wide)),
            shape((256, 256)),
            shape((128, 512)),
            shape((200, 512)),
            shape((128, 128), F32),
            shape((64, 128)),
        ),
        (own, anchor, rows),
        LAYOUT,
        10**9,
    )
    cand, v_far = first_exchange(exported, xm, xp, v_faces)
    grid, kinetic, v_box, target, code = call(
        "ahead",
        whole_kernel(lambda *a: ahead_body(*a[:6], a[-1])),
        (
            shape((256, 512), F32),
            shape((256, 512), F32),
            shape((256, 512)),
            shape((256, 512)),
            shape((256, 128), F32),
        ),
        (split, octant, places, v_own, xm, xp, table),
        AHEAD + FIRST,
        10**9,
    )
    current, sent, facing, v_box = call(
        "first",
        whole_kernel(first_body),
        (shape((128, 512)), shape((64, 512)), shape((64, 512)), shape((128, 512))),
        (target, code, places, table, grid, kinetic, v_box, cand, v_far),
        FIRST,
        10**9,
    )
    near_rows = second_exchange(sent, facing)
    done, applied_bf, near = call(
        "second",
        whole_kernel(lambda *a: second_body(*a[:4], a[-1])),
        (shape((128, 512), F32), shape((128, 512)), shape((128, 448))),
        (current, v_box, places, cand),
        SECOND + LAST,
        10**9,
    )
    (relaxed,) = call(
        "last",
        whole_kernel(lambda *a: (last_body(*a),)),
        (shape((256, 256)),),
        (done, applied_bf, current, near_rows, near),
        LAST,
        10**9,
    )
    return relaxed.reshape(boxes.shape)


def solution(mesh):
    placed = (
        P("gx", "gy", "gz", None, None, None),
        P("gx", "gy", "gz", None, None),
        P("gx", "gy", "gz"),
    )
    return jax.shard_map(
        local,
        mesh=mesh,
        in_specs=placed,
        out_specs=P("gx", "gy", "gz", None, None, None),
        check_vma=False,
    )
```

```python
import functools

import jax
import jax.numpy as jnp
import ml_dtypes
import numpy as np
from jax import lax
from jax.experimental import pallas as pl
from jax.experimental.pallas import tpu as pltpu
from jax.sharding import PartitionSpec as P

F32 = jnp.float32
BF16 = jnp.bfloat16

MAGIC = [
    8.433424733352934e-07,
    -1.290557201342061e-05,
    8.76298447621056e-05,
    -0.00030158038132690465,
    0.001747237136729939,
    -0.009420470302010804,
    0.023738214637249424,
    0.0612625895831208,
    0.9940415697834004,
    -0.06048952891969835,
    -0.021030251609303816,
    0.013372634148547948,
    -0.0034412814449349387,
    0.0004944322768868992,
    -5.185986881173433e-05,
    2.7273449291197967e-06,
]
KINETIC = [
    -3.55369228991319,
    2.2191465938911166,
    -0.6156141465570069,
    0.2371780582153806,
    -0.0822663999742123,
    0.0220702918848226,
    -0.004097656893426338,
    0.00045167920287502236,
    -2.3982285245075998e-05,
    2.0904234952920368e-06,
    -3.7230763047369276e-07,
    -1.0585705549674146e-08,
    -5.8138798302825405e-11,
    2.7080049362631943e-13,
    -6.9244749406392e-18,
]
CELL = 1.0 / 4096.0
STEP = 0.1
PENALTY = 3.0

VEDGE = (0, 1, 4)
SLAB = (0, 1, 4)


def split_parts(values):
    high = values.astype(ml_dtypes.bfloat16)
    low = (values - high.astype(np.float64)).astype(ml_dtypes.bfloat16)
    return high, low


def half_of(rows, size, keep):
    if isinstance(rows, list):
        return [r for i, r in enumerate(rows) if i // size % 2 == keep]
    count = rows.shape[0] // (2 * size)
    return rows.reshape(count, 2, size, rows.shape[1])[:, keep].reshape(count * size, -1)


def candidate_rows():
    own = [
        ((0, 0, 0), "border", (qy, qz, qx), k)
        for qy in range(2)
        for qz in range(2)
        for qx in range(2)
        for k in range(8)
    ]

    def moved(rows, axis, step):
        return [
            (d[:axis] + (d[axis] + step,) + d[axis + 1 :], kind, q, k) for d, kind, q, k in rows
        ]

    def onward(parts):
        low = moved(sum((half_of(r, 32, 1) for r in parts), []), 1, -1)
        high = moved(sum((half_of(r, 32, 0) for r in parts), []), 1, 1)
        parts = parts + [low, high]
        far_low = moved(sum((half_of(r, 16, 1) for r in parts), []), 2, -1)
        far_high = moved(sum((half_of(r, 16, 0) for r in parts), []), 2, 1)
        return low + high + far_low + far_high

    left, right = moved(own, 0, -1), moved(own, 0, 1)
    inner = [((d, 0, 0), "inner", (0, 0, 0), k) for d in (-1, 1) for k in range(8)]
    first = left + right + inner + onward([own, left, right])
    facing = [
        ((2 * side - 1, 0, 0), "border", (qy, qz, 1 - side), k)
        for qy in range(2)
        for qz in range(2)
        for side in range(2)
        for k in range(8)
    ]
    return first, facing + onward([own, facing])


def told_by(d):
    at = {0: 0, -1: 1, 1: 2}
    if d[2]:
        return (4 if d[2] < 0 else 5), 3 * at[d[1]] + at[d[0]]
    if d[1]:
        return (2 if d[1] < 0 else 3), at[d[0]]
    return (0 if d[0] < 0 else 1), 0


def lane_tables(rows):
    decode = np.zeros((128, len(rows)))
    where = np.zeros((8, len(rows)))
    away = np.zeros((8, len(rows)))
    for column, (d, kind, (qy, qz, qx), k) in enumerate(rows):
        message, group = told_by(d)
        first = 8 * group + (4 if kind == "inner" else 0)
        decode[first : first + 3, column] = (256, 16, 1)
        where[:, column] = 8 * message + k
        away[:, column] = code_number((5 * d[0] + qx, 5 * d[1] + qy, 5 * d[2] + qz))
    return decode, where, away


def code_number(place):
    return 256.0 * (place[0] + 5) + 16.0 * (place[1] + 5) + (place[2] + 5)


def placed(layer, pairs, axis=0):
    return [(layer, a, b) if axis == 0 else (a, layer, b) if axis == 1 else (a, b, layer) for a, b in pairs]


def filled(places, size):
    return places + [None] * (size - len(places))


def potential_blocks():
    on_y = [(0, b) for b in VEDGE]
    on_z = [(a, 0) for a in VEDGE]
    off = [(a, b) for a in (1, 4) for b in (1, 4)]
    x_low = (
        filled(placed(0, on_y) + placed(1, on_y), 8)
        + filled(placed(0, on_z) + placed(1, on_z), 8)
        + filled(placed(0, off) + placed(1, off), 8)
    )
    x_high = filled(placed(4, on_y) + placed(4, off), 8) + filled(placed(4, on_z), 8)
    y_low = filled(placed(0, [(a, b) for a in VEDGE for b in (1, 4)], 1), 8) + filled(
        placed(0, on_z, 1), 8
    )
    z_low = filled(placed(0, [(a, b) for a in VEDGE for b in VEDGE], 2), 16)
    return x_low, x_high, y_low, z_low


def carried(block, axis, layer, step):
    return [
        None
        if p is None or (layer is not None and p[axis] != layer)
        else p[:axis] + (p[axis] + step,) + p[axis + 1 :]
        for p in block
    ]


@functools.cache
def tables():
    out = {}
    magic = np.zeros((16, 16))
    kinetic = np.zeros((16, 16))
    for r in range(16):
        for c in range(16):
            if 0 <= c - r + 8 < 16:
                magic[r, c] = MAGIC[c - r + 8]
            if abs(c - r) < 15:
                kinetic[r, c] = KINETIC[abs(c - r)]
    eye = np.eye(16)
    full = np.eye(256)
    row_of = np.array(
        [f * 16 + px * 8 + x8 for x8 in range(8) for px in range(2) for f in range(16)]
    )
    lane_of = np.array(
        [
            (py * 8 + y8) * 16 + pz * 8 + z8
            for py in range(2)
            for pz in range(2)
            for y8 in range(8)
            for z8 in range(8)
        ]
    )
    prow = full[row_of]
    pcol = full[:, lane_of]
    out["prow"], out["prow_t"] = prow, prow.T
    out["pcol"], out["pcol_t"] = pcol, pcol.T
    pair = np.kron(magic, magic)[np.ix_(lane_of, lane_of)] - full
    out["yz"], out["yz_t"] = pair.T, pair
    along = np.kron(eye, magic)[np.ix_(row_of, row_of)] - full
    out["x"], out["x_t"] = along, along.T
    second = (np.kron(kinetic, eye) + np.kron(eye, kinetic))[np.ix_(lane_of, lane_of)]
    out["kyz_h"], out["kyz_l"] = split_parts(-0.5 * second)
    along = np.kron(eye, kinetic)[np.ix_(row_of, row_of)]
    out["kx_h"], out["kx_l"] = split_parts(-0.5 * along)

    first, second = candidate_rows()
    names = [((0, 0, 0), "own", f) for f in range(16)]
    names += [((d, 0, 0), "border", k) for d in (-1, 1) for k in range(8)]
    columns = [((0, 0, 0), "own", c % 16) for c in range(128)]
    columns += [(d, kind, k) for d, kind, q, k in first]
    names += sorted(set(columns) - set(names))
    out["fold"] = np.zeros((len(columns), 256))
    for row, name in enumerate(columns):
        out["fold"][row, names.index(name)] = 1
    out["decode"], out["codes_where"], out["codes_away"] = lane_tables(first)
    out["decode_last"], out["codes_where_last"], out["codes_away_last"] = lane_tables(second)
    names = sorted({(d, kind, k) for d, kind, q, k in second})
    out["fold_last"] = np.zeros((len(second), 256))
    for row, (d, kind, q, k) in enumerate(second):
        out["fold_last"][row, names.index((d, kind, k))] = 1
    own = [None] * 200
    for z in range(5):
        for x in range(5):
            for y in range(5):
                own[z * 40 + x * 8 + y] = (x, y, z)
    x_low, x_high, y_low, z_low = potential_blocks()
    out["faces"] = np.zeros((32, 200))
    for row, place in enumerate(y_low + z_low):
        if place is not None:
            out["faces"][row, own.index(place)] = 1
    out["face_x"] = np.zeros((40, 72))
    for row, place in enumerate(x_low + x_high):
        if place is not None:
            x, y, z = place
            out["face_x"][row, VEDGE.index(z) * 24 + SLAB.index(x) * 8 + y] = 1
    far_x = carried(x_low, 0, None, 5)
    near_x = carried(x_high, 0, None, -5)
    far_y = carried(y_low + far_x[0:8] + near_x[0:8], 1, 0, 5)
    far_z = carried(
        z_low + far_x[8:16] + near_x[8:16] + far_y[8:16] + far_y[16:24] + far_y[24:32], 2, 0, 5
    )
    codes = []
    for place in far_x + near_x + far_y + far_z:
        code = -1.0 if place is None else code_number(place)
        codes.append(-1.0 if code in codes else code)
    out["codes_far"] = np.broadcast_to(np.array(codes), (8, len(codes)))
    codes = [-1.0 if p is None else code_number(p) for p in own]
    out["codes_own"] = np.broadcast_to(np.array(codes), (8, len(codes)))
    return {
        k: np.ascontiguousarray(
            v, dtype=np.float32 if k.startswith("codes") else ml_dtypes.bfloat16
        )
        for k, v in out.items()
    }


def dot(a, b):
    return lax.dot_general(a, b, (((1,), (0,)), ((), ())), preferred_element_type=F32)


def dot_nt(a, b):
    return lax.dot_general(a, b, (((1,), (1,)), ((), ())), preferred_element_type=F32)


def rolled(values):
    return pltpu.roll(values, 64, 1)


def iota(dims, axis):
    return lax.broadcasted_iota(jnp.int32, dims, axis)


def low_lanes(values):
    return iota(values.shape, 1) < 64


def to_octants(split, roll):
    rows = split.shape[0] // 8
    blocks = []
    for py in range(split.shape[1] // 128):
        here = split[:, py * 128 : (py + 1) * 128]
        other = roll(here)
        for pz in range(2):
            pieces = []
            for x8 in range(0, 8, 2):
                one = slice(x8 * rows, (x8 + 1) * rows)
                two = slice((x8 + 1) * rows, (x8 + 2) * rows)
                if pz == 0:
                    left, right = here[one], other[two]
                else:
                    left, right = other[one], here[two]
                pieces.append(jnp.where(low_lanes(left), left, right))
            blocks.append(jnp.concatenate(pieces, axis=1))
    return blocks


def to_octant(split, roll):
    return jnp.concatenate(to_octants(split, roll), axis=0)


def to_split(octant, roll):
    columns = []
    for py in range(2):
        first = octant[(2 * py) * 32 : (2 * py + 1) * 32]
        second = octant[(2 * py + 1) * 32 : (2 * py + 2) * 32]
        pieces = []
        for pair in range(4):
            lanes = slice(pair * 128, (pair + 1) * 128)
            one, two = first[:, lanes], second[:, lanes]
            pieces.append(jnp.where(low_lanes(one), one, roll(two)))
            pieces.append(jnp.where(low_lanes(one), roll(one), two))
        columns.append(jnp.concatenate(pieces, axis=0))
    return jnp.concatenate(columns, axis=1)


def octant_places(anchor):
    row = iota((8, 16), 0)
    base = jnp.zeros((8, 16), F32)
    for c in range(3):
        base = jnp.where(row % 4 == c, jnp.broadcast_to(anchor[c], (8, 16)), base)
    spread = (iota((16, 128), 0) == iota((16, 128), 1) % 16).astype(F32).astype(BF16)
    base = dot(base.astype(BF16), spread)
    turned = jnp.concatenate([base] * 16, axis=0).T
    row, lane = iota((128, 128), 0), iota((128, 128), 1)
    lane = lane % 4
    bit = jnp.where(lane == 0, row // 16, jnp.where(lane == 1, row // 64, row // 32)) % 2
    return jnp.where(lane < 3, turned + bit.astype(F32), 0.0), base


def lift_table(y8):
    row, lane = iota((40, 384), 0), iota((40, 384), 1)
    match = (lane // 64 == row // 8) & (lane % 8 == row % 8) & ((lane // 8) % 8 == y8)
    return match.astype(F32).astype(BF16)


def across(values):
    eye = (iota((8, 128), 0) == iota((8, 128), 1)).astype(F32).astype(BF16)
    return dot_nt(eye, values.astype(BF16))


def export_tables(base):
    edge = ((base == 0.0) | (base == 4.0)).astype(F32)
    edge = jnp.maximum(jnp.maximum(edge[0:1], edge[1:2]), edge[2:3])
    row, lane = iota((128, 128), 0), iota((128, 128), 1)
    before = (row < lane % 16).astype(F32).astype(BF16)
    before = jnp.where(row < 16, before, jnp.zeros_like(before))
    rank = dot(jnp.broadcast_to(edge, (8, 128)).astype(BF16), before)[0:1]
    row, lane = iota((64, 128), 0), iota((64, 128), 1)
    chosen = (rank == (row % 8).astype(F32)) & (edge > 0.5) & (row // 8 == lane // 16)
    row, lane = iota((16, 128), 0), iota((16, 128), 1)
    rank = (lane % 16).astype(F32) - rank
    inner = (
        (rank == (row % 8).astype(F32))
        & (edge < 0.5)
        & (row // 8 == (lane // 16) % 2)
        & ((lane // 64 == 1) == (base[1:2] == 3.0))
        & (((lane // 32) % 2 == 1) == (base[2:3] == 3.0))
    )
    return chosen.astype(F32).astype(BF16), inner.astype(F32).astype(BF16)


def same_function():
    return (iota((128, 128), 0) % 16 == iota((128, 128), 1) % 16).astype(F32)


def over_octants(values):
    total = values[0:16]
    for p in range(1, 8):
        total = total + values[16 * p : 16 * p + 16]
    return total


def summed(values, table):
    high = values.astype(BF16)
    low = (values - high.astype(F32)).astype(BF16)
    both = dot(jnp.concatenate([high, low], axis=0), table)
    return both[:16] + both[16:]


def repeated(values):
    return jnp.concatenate([values] * 8, axis=0)


def function_rows(boxes, anchor, t, roll):
    places, base = octant_places(anchor)
    table, inner = export_tables(base)
    split = dot(dot(t["prow"](), boxes).astype(BF16), t["pcol"]())
    octant = to_octant(split, roll).astype(BF16)
    return split.astype(BF16), octant, places, table, inner


def coordinate_rows(table, inner, places):
    border = dot(table, places.astype(BF16))[0:8]
    within = dot(inner, places.astype(BF16))
    use = iota((8, 128), 1) % 8 < 4
    rows = [jnp.where(use, border, within[8 * i : 8 * i + 8]) for i in range(2)]
    return [jnp.concatenate([r] * 4, axis=1) for r in rows]


def regroup_table(layers):
    row, lane = iota((8 * layers, 40 * layers), 0), iota((8 * layers, 40 * layers), 1)
    target = jnp.where(row % 8 < 5, row // 8 * 40 + row % 8, -400)
    blocks = [(lane == target + 5 * x8).astype(F32).astype(BF16) for x8 in range(8)]
    return jnp.concatenate(blocks, axis=0)


def lifted_rows(potential_rows):
    total = None
    for y8 in range(8):
        part = dot(potential_rows(y8).astype(BF16), lift_table(y8))
        total = part if total is None else total + part
    return total.astype(BF16)


PACK = ("prow", "pcol", "face_x")


def pack_body(boxes, anchor, slab_rows, t, roll=rolled):
    _, octant, places, table, inner = function_rows(boxes(), anchor(), t, roll)
    exported = dot(table, octant).astype(BF16)
    corners = dot(inner, octant)
    told = coordinate_rows(table, inner, places)
    by_z = to_octants(dot(regroup_table(3), lifted_rows(slab_rows)), roll)
    slab = jnp.concatenate([by_z[z] for z in VEDGE], axis=0).astype(BF16)
    face = dot(t["face_x"](), slab)
    low = jnp.concatenate([corners[0:8], told[0], face[0:24]], axis=0).astype(BF16)
    high = jnp.concatenate([corners[8:16], told[1], face[24:40]], axis=0).astype(BF16)
    return exported, low, high


LAYOUT = ("prow", "pcol", "faces")


def layout_body(boxes, anchor, potential_rows, t, roll=rolled):
    split, octant, places, table, inner = function_rows(boxes, anchor, t, roll)
    exported = dot(table, octant).astype(BF16)
    told = coordinate_rows(table, inner, places)[0].astype(BF16)
    by_z = to_octants(dot(regroup_table(5), lifted_rows(potential_rows)), roll)
    v_rows = jnp.concatenate(by_z[:5], axis=0).astype(BF16)
    v_faces = dot(t["faces"](), v_rows).astype(BF16)
    return exported, told, v_faces, split, octant, v_rows, places, table


def grid_values(split, t, roll):
    inner = split.astype(F32) + dot(split, t["yz"]())
    return to_octant(inner + dot(t["x"](), inner.astype(BF16)), roll)


def kinetic_values(split, t, roll):
    lanes = dot(split, t["kyz_h"]()) + dot(split, t["kyz_l"]())
    rows = dot(t["kx_h"](), split) + dot(t["kx_l"](), split)
    return to_octant(lanes + rows, roll)


def returned_values(weighted, t, roll):
    split = to_split(weighted, roll)
    inner = split + dot(split.astype(BF16), t["yz_t"]())
    return to_octant(inner + dot(t["x_t"](), inner.astype(BF16)), roll)


def own_weights(overlaps, applied_bf, octant, geometry):
    products = over_octants((dot_nt(applied_bf, octant) * CELL - overlaps) * geometry)
    same = same_function()
    coupling = summed(products, same.astype(BF16)) + PENALTY * same[:16]
    return (repeated(coupling) * geometry).astype(BF16)


OPERATE = ("yz", "x", "kyz_h", "kyz_l", "kx_h", "kx_l")


def row_codes(places):
    x, y, z = (places[:, c : c + 1] + 5.0 for c in range(3))
    return 256.0 * x + 16.0 * y + z


def lane_codes(places):
    lanes = across(places) + 5.0
    return 256.0 * lanes[0:1] + 16.0 * lanes[1:2] + lanes[2:3]


def near_codes(told, decode, where, away):
    codes = dot(told[:, :128], decode)
    row = iota(codes.shape, 0).astype(F32)
    return jnp.sum(jnp.where(row == where[0:1], codes, 0.0), axis=0, keepdims=True) + away[0:1]


def picked(code, codes, rows):
    return dot((code == codes[0:1]).astype(F32).astype(BF16), rows)


def beside(left, right):
    pieces = []
    for q in range(8):
        pieces += [left[8 * q : 8 * q + 8], right[8 * q : 8 * q + 8]]
    return jnp.concatenate(pieces, axis=0)


def ahead_body(split, octant, places, v_own, xm, xp, t, roll=rolled):
    left, right = xm.astype(F32), xp.astype(F32)
    side = beside(left[:64], right[:64])
    side_split = to_split(side, roll).astype(BF16)
    codes = []
    for qy in range(2):
        for qz in range(2):
            for qx in range(2):
                for d, rows in ((-5, left[72:80]), (5, right[72:80])):
                    code = 256.0 * rows[:, 0:1] + 16.0 * rows[:, 1:2] + rows[:, 2:3]
                    codes.append(code + code_number((qx + d, qy, qz)))
    code = jnp.concatenate([row_codes(places)] + codes, axis=0)
    v_box = picked(code, t["codes_own"](), v_own).astype(BF16)
    grid = [grid_values(r, t, roll) for r in (split, side_split)]
    kinetic = [kinetic_values(r, t, roll) for r in (split, side_split)]
    target = jnp.concatenate([octant, side.astype(BF16)], axis=0)
    code = jnp.broadcast_to(code, (256, 128))
    return jnp.concatenate(grid, axis=0), jnp.concatenate(kinetic, axis=0), v_box, target, code


FIRST = ("yz_t", "x_t", "fold", "decode", "codes_where", "codes_away", "codes_far")
AHEAD = OPERATE + ("codes_own",)


def first_body(
    target, code, places, table, grid, kinetic, v_box, cand, told, v_far, t, roll=rolled
):
    code = code[:, 0:1]
    v_box = v_box.astype(F32) + picked(code, t["codes_far"](), v_far)
    weighted = grid * v_box
    applied = [returned_values(weighted[r], t, roll) for r in (slice(0, 128), slice(128, 256))]
    applied = jnp.concatenate(applied, axis=0) + kinetic
    applied_bf = applied.astype(BF16)
    near = near_codes(told, t["decode"](), t["codes_where"](), t["codes_away"]())
    same_place = code == jnp.concatenate([lane_codes(places), near], axis=1)
    rows = jnp.concatenate([target[:128], cand], axis=0)
    products = dot_nt(applied_bf, rows) - PENALTY * dot_nt(target, rows)
    products = jnp.where(same_place, products * CELL, 0.0)
    products = jnp.concatenate(
        [over_octants(products[:128]), over_octants(products[128:])], axis=0
    )
    coupling = folded(products, t["fold"]())
    identity = (iota((32, 256), 0) == iota((32, 256), 1)).astype(F32)
    coupling = dot_nt((coupling + PENALTY * identity).astype(BF16), t["fold"]())
    coupling = jnp.concatenate([coupling[:16]] * 8 + [coupling[16:]] * 8, axis=0)
    weights = jnp.where(same_place, coupling, 0.0).astype(BF16)
    correction = dot(weights, rows)
    current = (target.astype(F32) - STEP * (applied - correction)).astype(BF16)
    sent = dot(table, current[:128]).astype(BF16)
    side = current[128:].astype(F32)
    facing = []
    for q in range(4):
        facing += [side[32 * q + 16 : 32 * q + 24], side[32 * q + 8 : 32 * q + 16]]
    facing = jnp.concatenate(facing, axis=0).astype(BF16)
    return current[:128], sent, facing, v_box[:128].astype(BF16)


def folded(values, table):
    count = values.shape[0]
    high = values.astype(BF16)
    low = (values - high.astype(F32)).astype(BF16)
    both = dot(jnp.concatenate([high, low], axis=0), table)
    return both[:count] + both[count:]


SECOND = OPERATE + ("yz_t", "x_t", "decode_last", "codes_where_last", "codes_away_last")


def second_body(octant, v_box, places, told, t, roll=rolled):
    split = to_split(octant.astype(F32), roll).astype(BF16)
    weighted = grid_values(split, t, roll) * v_box.astype(F32)
    applied = returned_values(weighted, t, roll) + kinetic_values(split, t, roll)
    applied_bf = applied.astype(BF16)
    code = row_codes(places)
    geometry = (code == lane_codes(places)).astype(F32)
    overlaps = dot_nt(octant, octant) * (CELL * PENALTY)
    own_w = own_weights(overlaps, applied_bf, octant, geometry)
    done = octant.astype(F32) - STEP * (applied - dot(own_w, octant))
    lanes = near_codes(
        told, t["decode_last"](), t["codes_where_last"](), t["codes_away_last"]()
    )
    near = (code == lanes).astype(F32)
    return done, applied_bf, near.astype(BF16)


LAST = ("fold_last", "prow_t", "pcol_t")


def last_body(done, applied_bf, octant, cand, near, t, roll=rolled):
    near = near.astype(F32)
    products = dot_nt(applied_bf, cand) - PENALTY * dot_nt(octant, cand)
    coupling = folded(over_octants(products * CELL * near), t["fold_last"]())
    coupling = dot_nt(coupling.astype(BF16), t["fold_last"]())
    weights = (repeated(coupling) * near).astype(BF16)
    current = (done + STEP * dot(weights, cand)).astype(BF16)
    split = to_split(current.astype(F32), roll).astype(BF16)
    return dot(dot(t["prow_t"](), split).astype(BF16), t["pcol_t"]()).astype(BF16)


def shape(dims, dtype=BF16):
    return jax.ShapeDtypeStruct(dims, dtype)


class Fetched:
    def __init__(self, source, target, semaphore):
        self.copy = pltpu.make_async_copy(source, target, semaphore)
        self.target = target
        self.waiting = True
        self.copy.start()

    def ref(self):
        if self.waiting:
            self.copy.wait()
            self.waiting = False
        return self.target

    def __call__(self):
        return self.ref()[...]


def call(name, body, out_shape, inputs, consts, flops):
    arrays = list(inputs) + [jnp.asarray(tables()[k]) for k in consts]

    def kernel(*refs):
        t = {
            k: functools.partial(lambda ref: ref[...], r)
            for k, r in zip(consts, refs[len(inputs) : len(arrays)])
        }
        body(refs[: len(inputs)], t, refs[len(arrays) :])

    return pl.pallas_call(
        kernel,
        out_shape=out_shape,
        in_specs=[pl.BlockSpec(memory_space=pltpu.VMEM)] * len(arrays),
        out_specs=tuple(pl.BlockSpec(memory_space=pltpu.VMEM) for _ in out_shape),
        compiler_params=pltpu.CompilerParams(vmem_limit_bytes=24 << 20),
        cost_estimate=pl.CostEstimate(
            flops=flops, bytes_accessed=flops // 1000, transcendentals=0
        ),
        name=name,
    )(*arrays)


def pack_call(boxes, anchor, rows):
    arrays = [boxes, anchor, rows, rows] + [jnp.asarray(tables()[k]) for k in PACK]
    shapes = [(a.shape, a.dtype) for a in arrays]
    shapes[2:4] = [((960, 40), F32)]
    out_shape = (shape((104, 512)), shape((96, 512)))
    count = len(arrays)

    def kernel(*refs):
        sources = list(refs[:count])
        sources[2] = sources[2].at[pl.ds(0, 640)]
        sources[3] = sources[3].at[pl.ds(1280, 320)]
        targets = refs[count : count + 2]
        scratch = list(refs[count + 2 : -1])
        semaphores = refs[-1]
        low, high = scratch[-2:]
        slab = scratch[2]
        landing = scratch[:2] + [slab.at[pl.ds(0, 640)], slab.at[pl.ds(640, 320)]] + scratch[3:-2]
        fetched = [
            Fetched(a, b, semaphores.at[i]) for i, (a, b) in enumerate(zip(sources, landing))
        ]
        for piece in fetched:
            piece.ref()
        exported, low_rest, high_rest = pack_body(
            fetched[0],
            lambda: fetched[1]()[0, 0].astype(F32),
            lambda y8: slab[pl.ds(y8, 120, stride=8), :],
            dict(zip(PACK, fetched[4:])),
        )
        copies = []
        for i, (message, rest) in enumerate(((low, low_rest), (high, high_rest))):
            message[...] = jnp.concatenate([exported, rest], axis=0)
            copies.append(pltpu.make_async_copy(message, targets[i], semaphores.at[count + i]))
            copies[-1].start()
        for copy in copies:
            copy.wait()

    return pl.pallas_call(
        kernel,
        out_shape=out_shape,
        in_specs=[pl.BlockSpec(memory_space=pltpu.HBM)] * count,
        out_specs=tuple(pl.BlockSpec(memory_space=pltpu.HBM) for _ in out_shape),
        scratch_shapes=[pltpu.VMEM(*a) for a in shapes]
        + [pltpu.VMEM(o.shape, o.dtype) for o in out_shape]
        + [pltpu.SemaphoreType.DMA((count + 2,))],
        compiler_params=pltpu.CompilerParams(vmem_limit_bytes=56 << 20),
        cost_estimate=pl.CostEstimate(flops=10**8, bytes_accessed=10**6, transcendentals=0),
        name="pack",
    )(*arrays)


def layout_kernel(ins, t, outs):
    boxes, anchor, potential = ins
    got = layout_body(
        boxes[...],
        anchor[...][0, 0].astype(F32),
        lambda y8: potential[pl.ds(y8, 200, stride=8), :],
        t,
    )
    for ref, value in zip(outs, got):
        ref[...] = value


def whole_kernel(body):
    def run(ins, t, outs):
        got = body(*[r[...] for r in ins], t)
        for ref, value in zip(outs, got):
            ref[...] = value

    return run


def passed_along(value, axis, step):
    count = lax.axis_size(axis)
    return lax.ppermute(value, axis, [(i, (i + step) % count) for i in range(count)])


def y_messages(parts):
    return [[half_of(r, 32, keep) for r in parts] for keep in (0, 1)]


def z_messages(parts):
    return [[half_of(r, 16, keep) for r in parts] for keep in (0, 1)]


def sent_both(low, high, axis, send):
    below = send(jnp.concatenate(high, axis=0), axis, 1)
    return below, send(jnp.concatenate(low, axis=0), axis, -1)


def first_exchange(exported, told, xm, xp, v_faces, send=passed_along):
    v_far, v_near = xp[80:], xm[80:]
    group = lax.broadcasted_iota(jnp.int32, (8, 512), 1) // 8
    told_x = [xm[72:80], xp[72:80]]
    third = group % 3
    told_y = jnp.where(third == 0, told, jnp.where(third == 1, told_x[0], told_x[1]))
    parts = [exported, xm[:64], xp[:64]]
    low, high = y_messages(parts)
    ym, yp = sent_both(
        low + [told_y, v_faces[:16], v_far[:8], v_near[:8]], high + [told_y], "gy", send
    )
    told_z = jnp.where(group < 3, told_y, jnp.where(group < 6, ym[96:], yp[96:104]))
    v_y = yp[104:]
    parts = parts + [ym[:96], yp[:96]]
    low, high = z_messages(parts)
    v_z = [v_faces[16:], v_far[8:16], v_near[8:16], v_y[8:16], v_y[16:24], v_y[24:32]]
    zm, zp = sent_both(low + [told_z] + v_z, high + [told_z], "gz", send)
    rows = [xm[:64], xp[:64], xm[64:72], xp[64:72], ym[:96], yp[:96], zm[:192], zp[:192]]
    told = told_x + [ym[96:], yp[96:104], zm[192:], zp[192:200]]
    v_rows = [v_far, v_near, v_y, zp[200:]]
    return [jnp.concatenate(r, axis=0) for r in (rows, told, v_rows)]


def second_exchange(exported, facing, send=passed_along):
    extra = [facing[:8]]
    low, high = y_messages([exported, facing])
    ym, yp = sent_both(low + extra, high, "gy", send)
    low, high = z_messages([exported, facing, ym, yp[:64]])
    zm, zp = sent_both(low + extra, high, "gz", send)
    return jnp.concatenate([facing, ym, yp[:64], zm, zp[:128]], axis=0)


def local(boxes, anchors, potential):
    own = boxes.reshape(256, 256)
    anchor = jnp.transpose(anchors, (0, 1, 4, 2, 3))
    rows = potential.reshape(1600, 40)
    to_low, to_high = pack_call(own, anchor, rows)
    xm = passed_along(to_high, "gx", 1)
    xp = passed_along(to_low, "gx", -1)
    exported, told, v_faces, split, octant, v_own, places, table = call(
        "layout",
        layout_kernel,
        (
            shape((64, 512)),
            shape((8, 512)),
            shape((32, 512)),
            shape((256, 256)),
            shape((128, 512)),
            shape((200, 512)),
            shape((128, 128), F32),
            shape((64, 128)),
        ),
        (own, anchor, rows),
        LAYOUT,
        10**9,
    )
    cand, told, v_far = first_exchange(exported, told, xm, xp, v_faces)
    grid, kinetic, v_box, target, code = call(
        "ahead",
        whole_kernel(lambda *a: ahead_body(*a[:6], a[-1])),
        (
            shape((256, 512), F32),
            shape((256, 512), F32),
            shape((256, 512)),
            shape((256, 512)),
            shape((256, 128), F32),
        ),
        (split, octant, places, v_own, xm, xp, table),
        AHEAD + FIRST,
        10**9,
    )
    current, sent, facing, v_box = call(
        "first",
        whole_kernel(first_body),
        (shape((128, 512)), shape((64, 512)), shape((64, 512)), shape((128, 512))),
        (target, code, places, table, grid, kinetic, v_box, cand, told, v_far),
        FIRST,
        10**9,
    )
    near_rows = second_exchange(sent, facing)
    done, applied_bf, near = call(
        "second",
        whole_kernel(lambda *a: second_body(*a[:4], a[-1])),
        (shape((128, 512), F32), shape((128, 512)), shape((128, 448))),
        (current, v_box, places, told),
        SECOND + LAST,
        10**9,
    )
    (relaxed,) = call(
        "last",
        whole_kernel(lambda *a: (last_body(*a),)),
        (shape((256, 256)),),
        (done, applied_bf, current, near_rows, near),
        LAST,
        10**9,
    )
    return relaxed.reshape(boxes.shape)


def solution(mesh):
    placed = (
        P("gx", "gy", "gz", None, None, None),
        P("gx", "gy", "gz", None, None),
        P("gx", "gy", "gz"),
    )
    return jax.shard_map(
        local,
        mesh=mesh,
        in_specs=placed,
        out_specs=P("gx", "gy", "gz", None, None, None),
        check_vma=False,
    )
```

```python
import functools

import jax
import jax.numpy as jnp
import ml_dtypes
import numpy as np
from jax import lax
from jax.experimental import pallas as pl
from jax.experimental.pallas import tpu as pltpu
from jax.sharding import PartitionSpec as P

F32 = jnp.float32
BF16 = jnp.bfloat16

MAGIC = [
    8.433424733352934e-07,
    -1.290557201342061e-05,
    8.76298447621056e-05,
    -0.00030158038132690465,
    0.001747237136729939,
    -0.009420470302010804,
    0.023738214637249424,
    0.0612625895831208,
    0.9940415697834004,
    -0.06048952891969835,
    -0.021030251609303816,
    0.013372634148547948,
    -0.0034412814449349387,
    0.0004944322768868992,
    -5.185986881173433e-05,
    2.7273449291197967e-06,
]
KINETIC = [
    -3.55369228991319,
    2.2191465938911166,
    -0.6156141465570069,
    0.2371780582153806,
    -0.0822663999742123,
    0.0220702918848226,
    -0.004097656893426338,
    0.00045167920287502236,
    -2.3982285245075998e-05,
    2.0904234952920368e-06,
    -3.7230763047369276e-07,
    -1.0585705549674146e-08,
    -5.8138798302825405e-11,
    2.7080049362631943e-13,
    -6.9244749406392e-18,
]
CELL = 1.0 / 4096.0
STEP = 0.1
PENALTY = 3.0

VEDGE = (0, 1, 4)
SLAB = (0, 1, 4)


def split_parts(values):
    high = values.astype(ml_dtypes.bfloat16)
    low = (values - high.astype(np.float64)).astype(ml_dtypes.bfloat16)
    return high, low


def half_of(rows, size, keep):
    if isinstance(rows, list):
        return [r for i, r in enumerate(rows) if i // size % 2 == keep]
    count = rows.shape[0] // (2 * size)
    return rows.reshape(count, 2, size, rows.shape[1])[:, keep].reshape(count * size, -1)


def candidate_rows():
    own = [
        ((0, 0, 0), "border", (qy, qz, qx), k)
        for qy in range(2)
        for qz in range(2)
        for qx in range(2)
        for k in range(8)
    ]

    def moved(rows, axis, step):
        return [
            (d[:axis] + (d[axis] + step,) + d[axis + 1 :], kind, q, k) for d, kind, q, k in rows
        ]

    def onward(parts):
        low = moved(sum((half_of(r, 32, 1) for r in parts), []), 1, -1)
        high = moved(sum((half_of(r, 32, 0) for r in parts), []), 1, 1)
        parts = parts + [low, high]
        far_low = moved(sum((half_of(r, 16, 1) for r in parts), []), 2, -1)
        far_high = moved(sum((half_of(r, 16, 0) for r in parts), []), 2, 1)
        return low + high + far_low + far_high

    left, right = moved(own, 0, -1), moved(own, 0, 1)
    inner = [((d, 0, 0), "inner", (0, 0, 0), k) for d in (-1, 1) for k in range(8)]
    first = left + right + inner + onward([own, left, right])
    facing = [
        ((2 * side - 1, 0, 0), "border", (qy, qz, 1 - side), k)
        for qy in range(2)
        for qz in range(2)
        for side in range(2)
        for k in range(8)
    ]
    return first, facing + onward([own, facing])


def told_by(d):
    at = {0: 0, -1: 1, 1: 2}
    if d[2]:
        return (4 if d[2] < 0 else 5), 3 * at[d[1]] + at[d[0]]
    if d[1]:
        return (2 if d[1] < 0 else 3), at[d[0]]
    return (0 if d[0] < 0 else 1), 0


def lane_tables(rows):
    decode = np.zeros((72, len(rows)))
    where = np.zeros((8, len(rows)))
    away = np.zeros((8, len(rows)))
    for column, (d, kind, (qy, qz, qx), k) in enumerate(rows):
        message, group = told_by(d)
        first = 8 * group + (4 if kind == "inner" else 0)
        decode[first : first + 3, column] = (256, 16, 1)
        where[:, column] = 8 * message + k
        away[:, column] = code_number((5 * d[0] + qx, 5 * d[1] + qy, 5 * d[2] + qz))
    return decode, where, away


def code_number(place):
    return 256.0 * (place[0] + 5) + 16.0 * (place[1] + 5) + (place[2] + 5)


def laid(size, places):
    return [places.get(row) for row in range(size)]


def potential_blocks():
    off = [(a, b) for a in (1, 4) for b in (1, 4)]
    x_low = {0: (0, 0, 1), 1: (0, 0, 4), 2: (1, 0, 1), 3: (1, 0, 4), 6: (0, 0, 0), 7: (1, 0, 0)}
    x_low |= {9 + 3 * x + i: (x, a, 0) for x in range(2) for i, a in enumerate(VEDGE)}
    x_low |= {16 + 4 * x + i: (x, a, b) for x in range(2) for i, (a, b) in enumerate(off)}
    x_high = {0: (4, 0, 1), 6: (4, 0, 4), 7: (4, 0, 0)}
    x_high |= {1 + i: (4, a, b) for i, (a, b) in enumerate(off)}
    x_high |= {8 + i: (4, a, 0) for i, a in enumerate(VEDGE)}
    y_low = {2 * i + j: (a, 0, b) for i, a in enumerate(VEDGE) for j, b in enumerate((1, 4))}
    y_low |= {11 + i: (a, 0, 0) for i, a in enumerate(VEDGE)}
    z_low = {3 * i + j: (a, b, 0) for i, a in enumerate(VEDGE) for j, b in enumerate(VEDGE)}
    return laid(24, x_low), laid(16, x_high), laid(16, y_low), laid(16, z_low)


def merged(*blocks):
    if isinstance(blocks[0][1], list):
        ends = [first for first, _ in blocks[1:]] + [8]
        return sum((b[first:end] for (first, b), end in zip(blocks, ends)), [])
    row = lax.broadcasted_iota(jnp.int32, blocks[0][1].shape, 0)
    out = blocks[0][1]
    for first, block in blocks[1:]:
        out = jnp.where(row < first, out, block)
    return out


def y_potential(y_low, far_x, near_x):
    return [y_low[0:8], merged((0, near_x[0:8]), (3, y_low[8:16]), (6, near_x[0:8])), far_x[0:8]]


def z_potential(z_low, far_x, near_x, far_y):
    return [
        z_low[0:8],
        merged((0, z_low[8:16]), (1, far_x[8:16]), (7, far_y[8:16])),
        merged((0, near_x[8:16]), (3, far_y[8:16]), (6, far_y[16:24])),
    ]


def carried(block, axis, layer, step):
    return [
        None
        if p is None or (layer is not None and p[axis] != layer)
        else p[:axis] + (p[axis] + step,) + p[axis + 1 :]
        for p in block
    ]


@functools.cache
def tables():
    out = {}
    magic = np.zeros((16, 16))
    kinetic = np.zeros((16, 16))
    for r in range(16):
        for c in range(16):
            if 0 <= c - r + 8 < 16:
                magic[r, c] = MAGIC[c - r + 8]
            if abs(c - r) < 15:
                kinetic[r, c] = KINETIC[abs(c - r)]
    eye = np.eye(16)
    full = np.eye(256)
    row_of = np.array(
        [f * 16 + px * 8 + x8 for x8 in range(8) for px in range(2) for f in range(16)]
    )
    lane_of = np.array(
        [
            (py * 8 + y8) * 16 + pz * 8 + z8
            for py in range(2)
            for pz in range(2)
            for y8 in range(8)
            for z8 in range(8)
        ]
    )
    prow = full[row_of]
    pcol = full[:, lane_of]
    out["prow"], out["prow_t"] = prow, prow.T
    out["pcol"], out["pcol_t"] = pcol, pcol.T
    pair = np.kron(magic, magic)[np.ix_(lane_of, lane_of)] - full
    out["yz"], out["yz_t"] = pair.T, pair
    along = np.kron(eye, magic)[np.ix_(row_of, row_of)] - full
    out["x"], out["x_t"] = along, along.T
    second = (np.kron(kinetic, eye) + np.kron(eye, kinetic))[np.ix_(lane_of, lane_of)]
    out["kyz_h"], out["kyz_l"] = split_parts(-0.5 * second)
    along = np.kron(eye, kinetic)[np.ix_(row_of, row_of)]
    out["kx_h"], out["kx_l"] = split_parts(-0.5 * along)

    first, second = candidate_rows()
    names = [((0, 0, 0), "own", f) for f in range(16)]
    names += [((d, 0, 0), "border", k) for d in (-1, 1) for k in range(8)]
    columns = [((0, 0, 0), "own", c % 16) for c in range(128)]
    columns += [(d, kind, k) for d, kind, q, k in first]
    names += sorted(set(columns) - set(names))
    out["fold"] = np.zeros((len(columns), 256))
    for row, name in enumerate(columns):
        out["fold"][row, names.index(name)] = 1
    out["decode"], out["codes_where"], out["codes_away"] = lane_tables(first)
    out["decode_last"], out["codes_where_last"], out["codes_away_last"] = lane_tables(second)
    names = sorted({(d, kind, k) for d, kind, q, k in second})
    out["fold_last"] = np.zeros((len(second), 256))
    for row, (d, kind, q, k) in enumerate(second):
        out["fold_last"][row, names.index((d, kind, k))] = 1
    own = [None] * 200
    for z in range(5):
        for x in range(5):
            for y in range(5):
                own[z * 40 + x * 8 + y] = (x, y, z)
    x_low, x_high, y_low, z_low = potential_blocks()
    out["faces"] = np.zeros((32, 200))
    for row, place in enumerate(y_low + z_low):
        if place is not None:
            out["faces"][row, own.index(place)] = 1
    out["face_x"] = np.zeros((40, 72))
    for row, place in enumerate(x_low + x_high):
        if place is not None:
            x, y, z = place
            out["face_x"][row, VEDGE.index(z) * 24 + SLAB.index(x) * 8 + y] = 1
    far_x = carried(x_low, 0, None, 5)
    near_x = carried(x_high, 0, None, -5)
    far_y = carried(sum(y_potential(y_low, far_x, near_x), []), 1, 0, 5)
    far_z = carried(sum(z_potential(z_low, far_x, near_x, far_y), []), 2, 0, 5)
    codes = []
    for place in far_x + near_x + far_y + far_z:
        code = -1.0 if place is None else code_number(place)
        codes.append(-1.0 if code in codes else code)
    out["codes_far"] = np.broadcast_to(np.array(codes), (8, len(codes)))
    codes = [-1.0 if p is None else code_number(p) for p in own]
    out["codes_own"] = np.broadcast_to(np.array(codes), (8, len(codes)))
    return {
        k: np.ascontiguousarray(
            v, dtype=np.float32 if k.startswith("codes") else ml_dtypes.bfloat16
        )
        for k, v in out.items()
    }


def dot(a, b):
    return lax.dot_general(a, b, (((1,), (0,)), ((), ())), preferred_element_type=F32)


def dot_nt(a, b):
    return lax.dot_general(a, b, (((1,), (1,)), ((), ())), preferred_element_type=F32)


def rolled(values):
    return pltpu.roll(values, 64, 1)


def iota(dims, axis):
    return lax.broadcasted_iota(jnp.int32, dims, axis)


def low_lanes(values):
    return iota(values.shape, 1) < 64


def to_octants(split, roll):
    rows = split.shape[0] // 8
    blocks = []
    for py in range(split.shape[1] // 128):
        here = split[:, py * 128 : (py + 1) * 128]
        other = roll(here)
        for pz in range(2):
            pieces = []
            for x8 in range(0, 8, 2):
                one = slice(x8 * rows, (x8 + 1) * rows)
                two = slice((x8 + 1) * rows, (x8 + 2) * rows)
                if pz == 0:
                    left, right = here[one], other[two]
                else:
                    left, right = other[one], here[two]
                pieces.append(jnp.where(low_lanes(left), left, right))
            blocks.append(jnp.concatenate(pieces, axis=1))
    return blocks


def to_octant(split, roll):
    return jnp.concatenate(to_octants(split, roll), axis=0)


def to_split(octant, roll):
    columns = []
    for py in range(2):
        first = octant[(2 * py) * 32 : (2 * py + 1) * 32]
        second = octant[(2 * py + 1) * 32 : (2 * py + 2) * 32]
        pieces = []
        for pair in range(4):
            lanes = slice(pair * 128, (pair + 1) * 128)
            one, two = first[:, lanes], second[:, lanes]
            pieces.append(jnp.where(low_lanes(one), one, roll(two)))
            pieces.append(jnp.where(low_lanes(one), roll(one), two))
        columns.append(jnp.concatenate(pieces, axis=0))
    return jnp.concatenate(columns, axis=1)


def octant_places(anchor):
    row = iota((8, 16), 0)
    base = jnp.zeros((8, 16), F32)
    for c in range(3):
        base = jnp.where(row % 4 == c, jnp.broadcast_to(anchor[c], (8, 16)), base)
    spread = (iota((16, 128), 0) == iota((16, 128), 1) % 16).astype(F32).astype(BF16)
    base = dot(base.astype(BF16), spread)
    turned = jnp.concatenate([base] * 16, axis=0).T
    row, lane = iota((128, 128), 0), iota((128, 128), 1)
    lane = lane % 4
    bit = jnp.where(lane == 0, row // 16, jnp.where(lane == 1, row // 64, row // 32)) % 2
    return jnp.where(lane < 3, turned + bit.astype(F32), 0.0), base


def lift_table(y8):
    row, lane = iota((40, 384), 0), iota((40, 384), 1)
    match = (lane // 64 == row // 8) & (lane % 8 == row % 8) & ((lane // 8) % 8 == y8)
    return match.astype(F32).astype(BF16)


def across(values):
    eye = (iota((8, 128), 0) == iota((8, 128), 1)).astype(F32).astype(BF16)
    return dot_nt(eye, values.astype(BF16))


def export_tables(base):
    edge = ((base == 0.0) | (base == 4.0)).astype(F32)
    edge = jnp.maximum(jnp.maximum(edge[0:1], edge[1:2]), edge[2:3])
    row, lane = iota((128, 128), 0), iota((128, 128), 1)
    before = (row < lane % 16).astype(F32).astype(BF16)
    before = jnp.where(row < 16, before, jnp.zeros_like(before))
    rank = dot(jnp.broadcast_to(edge, (8, 128)).astype(BF16), before)[0:1]
    row, lane = iota((64, 128), 0), iota((64, 128), 1)
    chosen = (rank == (row % 8).astype(F32)) & (edge > 0.5) & (row // 8 == lane // 16)
    row, lane = iota((16, 128), 0), iota((16, 128), 1)
    rank = (lane % 16).astype(F32) - rank
    inner = (
        (rank == (row % 8).astype(F32))
        & (edge < 0.5)
        & (row // 8 == (lane // 16) % 2)
        & ((lane // 64 == 1) == (base[1:2] == 3.0))
        & (((lane // 32) % 2 == 1) == (base[2:3] == 3.0))
    )
    return chosen.astype(F32).astype(BF16), inner.astype(F32).astype(BF16)


def same_function():
    return (iota((128, 128), 0) % 16 == iota((128, 128), 1) % 16).astype(F32)


def over_octants(values):
    total = values[0:16]
    for p in range(1, 8):
        total = total + values[16 * p : 16 * p + 16]
    return total


def summed(values, table):
    high = values.astype(BF16)
    low = (values - high.astype(F32)).astype(BF16)
    both = dot(jnp.concatenate([high, low], axis=0), table)
    return both[:16] + both[16:]


def repeated(values):
    return jnp.concatenate([values] * 8, axis=0)


def function_rows(boxes, anchor, t, roll):
    places, base = octant_places(anchor)
    table, inner = export_tables(base)
    split = dot(dot(t["prow"](), boxes).astype(BF16), t["pcol"]())
    octant = to_octant(split, roll).astype(BF16)
    return split.astype(BF16), octant, places, table, inner


def coordinate_rows(table, inner, places):
    border = dot(table, places.astype(BF16))[0:8]
    within = dot(inner, places.astype(BF16))
    use = iota((8, 128), 1) % 8 < 4
    rows = [jnp.where(use, border, within[8 * i : 8 * i + 8]) for i in range(2)]
    return [jnp.concatenate([r] * 4, axis=1) for r in rows]


def regroup_table(layers):
    row, lane = iota((8 * layers, 40 * layers), 0), iota((8 * layers, 40 * layers), 1)
    target = jnp.where(row % 8 < 5, row // 8 * 40 + row % 8, -400)
    blocks = [(lane == target + 5 * x8).astype(F32).astype(BF16) for x8 in range(8)]
    return jnp.concatenate(blocks, axis=0)


def lifted_rows(potential_rows):
    total = None
    for y8 in range(8):
        part = dot(potential_rows(y8).astype(BF16), lift_table(y8))
        total = part if total is None else total + part
    return total.astype(BF16)


PACK = ("prow", "pcol", "face_x")


def pack_body(boxes, anchor, slab_rows, t, roll=rolled):
    _, octant, places, table, inner = function_rows(boxes(), anchor(), t, roll)
    exported = dot(table, octant).astype(BF16)
    corners = dot(inner, octant)
    told = coordinate_rows(table, inner, places)
    by_z = to_octants(dot(regroup_table(3), lifted_rows(slab_rows)), roll)
    slab = jnp.concatenate([by_z[z] for z in VEDGE], axis=0).astype(BF16)
    face = dot(t["face_x"](), slab)
    low = jnp.concatenate([corners[0:8], told[0], face[0:24]], axis=0).astype(BF16)
    high = jnp.concatenate([corners[8:16], told[1], face[24:40]], axis=0).astype(BF16)
    return exported, low, high


LAYOUT = ("prow", "pcol", "faces")


def layout_body(boxes, anchor, potential_rows, t, roll=rolled):
    split, octant, places, table, inner = function_rows(boxes, anchor, t, roll)
    exported = dot(table, octant).astype(BF16)
    told = coordinate_rows(table, inner, places)[0].astype(BF16)
    by_z = to_octants(dot(regroup_table(5), lifted_rows(potential_rows)), roll)
    v_rows = jnp.concatenate(by_z[:5], axis=0).astype(BF16)
    v_faces = dot(t["faces"](), v_rows).astype(BF16)
    return exported, told, v_faces, split, octant, v_rows, places, table


def grid_values(split, t, roll):
    inner = split.astype(F32) + dot(split, t["yz"]())
    return to_octant(inner + dot(t["x"](), inner.astype(BF16)), roll)


def kinetic_values(split, t, roll):
    lanes = dot(split, t["kyz_h"]()) + dot(split, t["kyz_l"]())
    rows = dot(t["kx_h"](), split) + dot(t["kx_l"](), split)
    return to_octant(lanes + rows, roll)


def returned_values(weighted, t, roll):
    split = to_split(weighted, roll)
    inner = split + dot(split.astype(BF16), t["yz_t"]())
    return to_octant(inner + dot(t["x_t"](), inner.astype(BF16)), roll)


def own_weights(overlaps, applied_bf, octant, geometry):
    products = over_octants((dot_nt(applied_bf, octant) * CELL - overlaps) * geometry)
    same = same_function()
    coupling = summed(products, same.astype(BF16)) + PENALTY * same[:16]
    return (repeated(coupling) * geometry).astype(BF16)


OPERATE = ("yz", "x", "kyz_h", "kyz_l", "kx_h", "kx_l")


def row_codes(places):
    x, y, z = (places[:, c : c + 1] + 5.0 for c in range(3))
    return 256.0 * x + 16.0 * y + z


def lane_codes(places):
    lanes = across(places) + 5.0
    return 256.0 * lanes[0:1] + 16.0 * lanes[1:2] + lanes[2:3]


def near_codes(told, decode, where, away):
    codes = dot(told[:, :72], decode)
    row = iota(codes.shape, 0).astype(F32)
    return jnp.sum(jnp.where(row == where[0:1], codes, 0.0), axis=0, keepdims=True) + away[0:1]


def picked(code, codes, rows):
    return dot((code == codes[0:1]).astype(F32).astype(BF16), rows)


def beside(left, right):
    pieces = []
    for q in range(8):
        pieces += [left[8 * q : 8 * q + 8], right[8 * q : 8 * q + 8]]
    return jnp.concatenate(pieces, axis=0)


def ahead_body(split, octant, places, v_own, xm, xp, t, roll=rolled):
    left, right = xm.astype(F32), xp.astype(F32)
    side = beside(left[:64], right[:64])
    side_split = to_split(side, roll).astype(BF16)
    codes = []
    for qy in range(2):
        for qz in range(2):
            for qx in range(2):
                for d, rows in ((-5, left[72:80]), (5, right[72:80])):
                    code = 256.0 * rows[:, 0:1] + 16.0 * rows[:, 1:2] + rows[:, 2:3]
                    codes.append(code + code_number((qx + d, qy, qz)))
    code = jnp.concatenate([row_codes(places)] + codes, axis=0)
    v_box = picked(code, t["codes_own"](), v_own).astype(BF16)
    grid = [grid_values(r, t, roll) for r in (split, side_split)]
    kinetic = [kinetic_values(r, t, roll) for r in (split, side_split)]
    target = jnp.concatenate([octant, side.astype(BF16)], axis=0)
    code = jnp.broadcast_to(code, (256, 128))
    return jnp.concatenate(grid, axis=0), jnp.concatenate(kinetic, axis=0), v_box, target, code


FIRST = ("yz_t", "x_t", "fold", "decode", "codes_where", "codes_away", "codes_far")
AHEAD = OPERATE + ("codes_own",)


def first_body(
    target, code, places, table, grid, kinetic, v_box, cand, told, v_far, t, roll=rolled
):
    code = code[:, 0:1]
    v_box = v_box.astype(F32) + picked(code, t["codes_far"](), v_far)
    weighted = grid * v_box
    applied = [returned_values(weighted[r], t, roll) for r in (slice(0, 128), slice(128, 256))]
    applied = jnp.concatenate(applied, axis=0) + kinetic
    applied_bf = applied.astype(BF16)
    near = near_codes(told, t["decode"](), t["codes_where"](), t["codes_away"]())
    same_place = code == jnp.concatenate([lane_codes(places), near], axis=1)
    rows = jnp.concatenate([target[:128], cand], axis=0)
    products = dot_nt(applied_bf, rows) - PENALTY * dot_nt(target, rows)
    products = jnp.where(same_place, products * CELL, 0.0)
    products = jnp.concatenate(
        [over_octants(products[:128]), over_octants(products[128:])], axis=0
    )
    coupling = folded(products, t["fold"]())
    identity = (iota((32, 256), 0) == iota((32, 256), 1)).astype(F32)
    coupling = dot_nt((coupling + PENALTY * identity).astype(BF16), t["fold"]())
    coupling = jnp.concatenate([coupling[:16]] * 8 + [coupling[16:]] * 8, axis=0)
    weights = jnp.where(same_place, coupling, 0.0).astype(BF16)
    correction = dot(weights, rows)
    current = (target.astype(F32) - STEP * (applied - correction)).astype(BF16)
    sent = dot(table, current[:128]).astype(BF16)
    side = current[128:].astype(F32)
    facing = []
    for q in range(4):
        facing += [side[32 * q + 16 : 32 * q + 24], side[32 * q + 8 : 32 * q + 16]]
    facing = jnp.concatenate(facing, axis=0).astype(BF16)
    return current[:128], sent, facing, v_box[:128].astype(BF16)


def folded(values, table):
    count = values.shape[0]
    high = values.astype(BF16)
    low = (values - high.astype(F32)).astype(BF16)
    both = dot(jnp.concatenate([high, low], axis=0), table)
    return both[:count] + both[count:]


SECOND = OPERATE + ("yz_t", "x_t", "decode_last", "codes_where_last", "codes_away_last")


def second_body(octant, v_box, places, told, t, roll=rolled):
    split = to_split(octant.astype(F32), roll).astype(BF16)
    weighted = grid_values(split, t, roll) * v_box.astype(F32)
    applied = returned_values(weighted, t, roll) + kinetic_values(split, t, roll)
    applied_bf = applied.astype(BF16)
    code = row_codes(places)
    geometry = (code == lane_codes(places)).astype(F32)
    overlaps = dot_nt(octant, octant) * (CELL * PENALTY)
    own_w = own_weights(overlaps, applied_bf, octant, geometry)
    done = octant.astype(F32) - STEP * (applied - dot(own_w, octant))
    lanes = near_codes(
        told, t["decode_last"](), t["codes_where_last"](), t["codes_away_last"]()
    )
    near = (code == lanes).astype(F32)
    return done, applied_bf, near.astype(BF16)


LAST = ("fold_last", "prow_t", "pcol_t")


def last_body(done, applied_bf, octant, cand, near, t, roll=rolled):
    near = near.astype(F32)
    products = dot_nt(applied_bf, cand) - PENALTY * dot_nt(octant, cand)
    coupling = folded(over_octants(products * CELL * near), t["fold_last"]())
    coupling = dot_nt(coupling.astype(BF16), t["fold_last"]())
    weights = (repeated(coupling) * near).astype(BF16)
    current = (done + STEP * dot(weights, cand)).astype(BF16)
    split = to_split(current.astype(F32), roll).astype(BF16)
    return dot(dot(t["prow_t"](), split).astype(BF16), t["pcol_t"]()).astype(BF16)


def shape(dims, dtype=BF16):
    return jax.ShapeDtypeStruct(dims, dtype)


class Fetched:
    def __init__(self, source, target, semaphore):
        self.copy = pltpu.make_async_copy(source, target, semaphore)
        self.target = target
        self.waiting = True
        self.copy.start()

    def ref(self):
        if self.waiting:
            self.copy.wait()
            self.waiting = False
        return self.target

    def __call__(self):
        return self.ref()[...]


def call(name, body, out_shape, inputs, consts, flops):
    arrays = list(inputs) + [jnp.asarray(tables()[k]) for k in consts]

    def kernel(*refs):
        t = {
            k: functools.partial(lambda ref: ref[...], r)
            for k, r in zip(consts, refs[len(inputs) : len(arrays)])
        }
        body(refs[: len(inputs)], t, refs[len(arrays) :])

    return pl.pallas_call(
        kernel,
        out_shape=out_shape,
        in_specs=[pl.BlockSpec(memory_space=pltpu.VMEM)] * len(arrays),
        out_specs=tuple(pl.BlockSpec(memory_space=pltpu.VMEM) for _ in out_shape),
        compiler_params=pltpu.CompilerParams(vmem_limit_bytes=24 << 20),
        cost_estimate=pl.CostEstimate(
            flops=flops, bytes_accessed=flops // 1000, transcendentals=0
        ),
        name=name,
    )(*arrays)


def pack_call(boxes, anchor, rows):
    arrays = [boxes, anchor, rows, rows] + [jnp.asarray(tables()[k]) for k in PACK]
    shapes = [(a.shape, a.dtype) for a in arrays]
    shapes[2:4] = [((960, 40), F32)]
    out_shape = (shape((104, 512)), shape((96, 512)))
    count = len(arrays)

    def kernel(*refs):
        sources = list(refs[:count])
        sources[2] = sources[2].at[pl.ds(0, 640)]
        sources[3] = sources[3].at[pl.ds(1280, 320)]
        targets = refs[count : count + 2]
        scratch = list(refs[count + 2 : -1])
        semaphores = refs[-1]
        low, high = scratch[-2:]
        slab = scratch[2]
        landing = scratch[:2] + [slab.at[pl.ds(0, 640)], slab.at[pl.ds(640, 320)]] + scratch[3:-2]
        fetched = [
            Fetched(a, b, semaphores.at[i]) for i, (a, b) in enumerate(zip(sources, landing))
        ]
        for piece in fetched:
            piece.ref()
        exported, low_rest, high_rest = pack_body(
            fetched[0],
            lambda: fetched[1]()[0, 0].astype(F32),
            lambda y8: slab[pl.ds(y8, 120, stride=8), :],
            dict(zip(PACK, fetched[4:])),
        )
        copies = []
        for i, (message, rest) in enumerate(((low, low_rest), (high, high_rest))):
            message[...] = jnp.concatenate([exported, rest], axis=0)
            copies.append(pltpu.make_async_copy(message, targets[i], semaphores.at[count + i]))
            copies[-1].start()
        for copy in copies:
            copy.wait()

    return pl.pallas_call(
        kernel,
        out_shape=out_shape,
        in_specs=[pl.BlockSpec(memory_space=pltpu.HBM)] * count,
        out_specs=tuple(pl.BlockSpec(memory_space=pltpu.HBM) for _ in out_shape),
        scratch_shapes=[pltpu.VMEM(*a) for a in shapes]
        + [pltpu.VMEM(o.shape, o.dtype) for o in out_shape]
        + [pltpu.SemaphoreType.DMA((count + 2,))],
        compiler_params=pltpu.CompilerParams(vmem_limit_bytes=56 << 20),
        cost_estimate=pl.CostEstimate(flops=10**8, bytes_accessed=10**6, transcendentals=0),
        name="pack",
    )(*arrays)


def layout_kernel(ins, t, outs):
    boxes, anchor, potential = ins
    got = layout_body(
        boxes[...],
        anchor[...][0, 0].astype(F32),
        lambda y8: potential[pl.ds(y8, 200, stride=8), :],
        t,
    )
    for ref, value in zip(outs, got):
        ref[...] = value


def whole_kernel(body):
    def run(ins, t, outs):
        got = body(*[r[...] for r in ins], t)
        for ref, value in zip(outs, got):
            ref[...] = value

    return run


def passed_along(value, axis, step):
    count = lax.axis_size(axis)
    return lax.ppermute(value, axis, [(i, (i + step) % count) for i in range(count)])


def y_messages(parts):
    return [[half_of(r, 32, keep) for r in parts] for keep in (0, 1)]


def z_messages(parts):
    return [[half_of(r, 16, keep) for r in parts] for keep in (0, 1)]


def sent_both(low, high, axis, send):
    below = send(jnp.concatenate(high, axis=0), axis, 1)
    return below, send(jnp.concatenate(low, axis=0), axis, -1)


def sent_in_pairs(low, high, axis, send):
    if send is not passed_along:
        return sent_both([low], [high], axis, send)
    count = lax.axis_size(axis)
    even = lax.axis_index(axis) % 2 == 0
    outside = [(i, (i + (1 if i % 2 else -1)) % count) for i in range(count)]
    inside = [(i, i + (-1 if i % 2 else 1)) for i in range(count)]
    far = lax.ppermute(jnp.where(even, low, high), axis, outside)
    near = lax.ppermute(jnp.where(even, high, low), axis, inside)
    return jnp.where(even, far, near), jnp.where(even, near, far)


def first_exchange(exported, told, xm, xp, v_faces, send=passed_along):
    v_far, v_near = xp[80:], xm[80:]
    group = lax.broadcasted_iota(jnp.int32, (8, 512), 1) // 8
    told_x = [xm[72:80], xp[72:80]]
    third = group % 3
    told_y = jnp.where(third == 0, told, jnp.where(third == 1, told_x[0], told_x[1]))
    parts = [exported, xm[:64], xp[:64]]
    low, high = y_messages(parts)
    ym, yp = sent_both(
        low + [told_y] + y_potential(v_faces[:16], v_far, v_near), high + [told_y], "gy", send
    )
    told_z = jnp.where(group < 3, told_y, jnp.where(group < 6, ym[96:], yp[96:104]))
    v_y = yp[104:]
    parts = parts + [ym[:96], yp[:96]]
    low, high = z_messages(parts)
    v_z = z_potential(v_faces[16:], v_far, v_near, v_y)
    zm, zp = sent_both(low + [told_z] + v_z, high + [told_z], "gz", send)
    rows = [xm[:64], xp[:64], xm[64:72], xp[64:72], ym[:96], yp[:96], zm[:192], zp[:192]]
    told = told_x + [ym[96:], yp[96:104], zm[192:], zp[192:200]]
    v_rows = [v_far, v_near, v_y, zp[200:]]
    return [jnp.concatenate(r, axis=0) for r in (rows, told, v_rows)]


def second_exchange(exported, facing, send=passed_along):
    extra = [facing[:8]]
    low, high = y_messages([exported, facing])
    ym, yp = sent_both(low + extra, high, "gy", send)
    low, high = z_messages([exported, facing, ym, yp[:64]])
    low, high = jnp.concatenate(low, axis=0), jnp.concatenate(high, axis=0)
    zm, zp = sent_in_pairs(low, high, "gz", send)
    return jnp.concatenate([facing, ym, yp[:64], zm, zp], axis=0)


def local(boxes, anchors, potential):
    own = boxes.reshape(256, 256)
    anchor = jnp.transpose(anchors, (0, 1, 4, 2, 3))
    rows = potential.reshape(1600, 40)
    to_low, to_high = pack_call(own, anchor, rows)
    xm = passed_along(to_high, "gx", 1)
    xp = passed_along(to_low, "gx", -1)
    exported, told, v_faces, split, octant, v_own, places, table = call(
        "layout",
        layout_kernel,
        (
            shape((64, 512)),
            shape((8, 512)),
            shape((32, 512)),
            shape((256, 256)),
            shape((128, 512)),
            shape((200, 512)),
            shape((128, 128), F32),
            shape((64, 128)),
        ),
        (own, anchor, rows),
        LAYOUT,
        10**9,
    )
    cand, told, v_far = first_exchange(exported, told, xm, xp, v_faces)
    grid, kinetic, v_box, target, code = call(
        "ahead",
        whole_kernel(lambda *a: ahead_body(*a[:6], a[-1])),
        (
            shape((256, 512), F32),
            shape((256, 512), F32),
            shape((256, 512)),
            shape((256, 512)),
            shape((256, 128), F32),
        ),
        (split, octant, places, v_own, xm, xp, table),
        AHEAD + FIRST,
        10**9,
    )
    current, sent, facing, v_box = call(
        "first",
        whole_kernel(first_body),
        (shape((128, 512)), shape((64, 512)), shape((64, 512)), shape((128, 512))),
        (target, code, places, table, grid, kinetic, v_box, cand, told, v_far),
        FIRST,
        10**9,
    )
    near_rows = second_exchange(sent, facing)
    done, applied_bf, near = call(
        "second",
        whole_kernel(lambda *a: second_body(*a[:4], a[-1])),
        (shape((128, 512), F32), shape((128, 512)), shape((128, 448))),
        (current, v_box, places, told),
        SECOND + LAST,
        10**9,
    )
    (relaxed,) = call(
        "last",
        whole_kernel(lambda *a: (last_body(*a),)),
        (shape((256, 256)),),
        (done, applied_bf, current, near_rows, near),
        LAST,
        10**9,
    )
    return relaxed.reshape(boxes.shape)


def solution(mesh):
    placed = (
        P("gx", "gy", "gz", None, None, None),
        P("gx", "gy", "gz", None, None),
        P("gx", "gy", "gz"),
    )
    return jax.shard_map(
        local,
        mesh=mesh,
        in_specs=placed,
        out_specs=P("gx", "gy", "gz", None, None, None),
        check_vma=False,
    )
```

```python
import functools

import jax
import jax.numpy as jnp
import ml_dtypes
import numpy as np
from jax import lax
from jax.experimental import pallas as pl
from jax.experimental.pallas import tpu as pltpu
from jax.sharding import PartitionSpec as P

F32 = jnp.float32
BF16 = jnp.bfloat16

MAGIC = [
    8.433424733352934e-07,
    -1.290557201342061e-05,
    8.76298447621056e-05,
    -0.00030158038132690465,
    0.001747237136729939,
    -0.009420470302010804,
    0.023738214637249424,
    0.0612625895831208,
    0.9940415697834004,
    -0.06048952891969835,
    -0.021030251609303816,
    0.013372634148547948,
    -0.0034412814449349387,
    0.0004944322768868992,
    -5.185986881173433e-05,
    2.7273449291197967e-06,
]
KINETIC = [
    -3.55369228991319,
    2.2191465938911166,
    -0.6156141465570069,
    0.2371780582153806,
    -0.0822663999742123,
    0.0220702918848226,
    -0.004097656893426338,
    0.00045167920287502236,
    -2.3982285245075998e-05,
    2.0904234952920368e-06,
    -3.7230763047369276e-07,
    -1.0585705549674146e-08,
    -5.8138798302825405e-11,
    2.7080049362631943e-13,
    -6.9244749406392e-18,
]
CELL = 1.0 / 4096.0
STEP = 0.1
PENALTY = 3.0

VEDGE = (0, 1, 4)
SLAB = (0, 1, 4)


def split_parts(values):
    high = values.astype(ml_dtypes.bfloat16)
    low = (values - high.astype(np.float64)).astype(ml_dtypes.bfloat16)
    return high, low


def half_of(rows, size, keep):
    if isinstance(rows, list):
        return [r for i, r in enumerate(rows) if i // size % 2 == keep]
    count = rows.shape[0] // (2 * size)
    return rows.reshape(count, 2, size, rows.shape[1])[:, keep].reshape(count * size, -1)


def candidate_rows():
    own = [
        ((0, 0, 0), "border", (qy, qz, qx), k)
        for qy in range(2)
        for qz in range(2)
        for qx in range(2)
        for k in range(8)
    ]

    def moved(rows, axis, step):
        return [
            (d[:axis] + (d[axis] + step,) + d[axis + 1 :], kind, q, k) for d, kind, q, k in rows
        ]

    def onward(parts):
        low = moved(sum((half_of(r, 32, 1) for r in parts), []), 1, -1)
        high = moved(sum((half_of(r, 32, 0) for r in parts), []), 1, 1)
        parts = parts + [low, high]
        far_low = moved(sum((half_of(r, 16, 1) for r in parts), []), 2, -1)
        far_high = moved(sum((half_of(r, 16, 0) for r in parts), []), 2, 1)
        return low + high + far_low + far_high

    left, right = moved(own, 0, -1), moved(own, 0, 1)
    inner = [((d, 0, 0), "inner", (0, 0, 0), k) for d in (-1, 1) for k in range(8)]
    first = left + right + inner + onward([own, left, right])
    facing = [
        ((2 * side - 1, 0, 0), "border", (qy, qz, 1 - side), k)
        for qy in range(2)
        for qz in range(2)
        for side in range(2)
        for k in range(8)
    ]
    return first, facing + onward([own, facing])


def told_by(d):
    at = {0: 0, -1: 1, 1: 2}
    if d[2]:
        return (4 if d[2] < 0 else 5), 3 * at[d[1]] + at[d[0]]
    if d[1]:
        return (2 if d[1] < 0 else 3), at[d[0]]
    return (0 if d[0] < 0 else 1), 0


def lane_tables(rows):
    decode = np.zeros((72, len(rows)))
    where = np.zeros((8, len(rows)))
    away = np.zeros((8, len(rows)))
    for column, (d, kind, (qy, qz, qx), k) in enumerate(rows):
        message, group = told_by(d)
        first = 8 * group + (4 if kind == "inner" else 0)
        decode[first : first + 3, column] = (256, 16, 1)
        where[:, column] = 8 * message + k
        away[:, column] = code_number((5 * d[0] + qx, 5 * d[1] + qy, 5 * d[2] + qz))
    return decode, where, away


def code_number(place):
    return 256.0 * (place[0] + 5) + 16.0 * (place[1] + 5) + (place[2] + 5)


def laid(size, places):
    return [places.get(row) for row in range(size)]


def potential_blocks():
    off = [(a, b) for a in (1, 4) for b in (1, 4)]
    x_low = {0: (0, 0, 1), 1: (0, 0, 4), 2: (1, 0, 1), 3: (1, 0, 4), 6: (0, 0, 0), 7: (1, 0, 0)}
    x_low |= {9 + 3 * x + i: (x, a, 0) for x in range(2) for i, a in enumerate(VEDGE)}
    x_low |= {16 + 4 * x + i: (x, a, b) for x in range(2) for i, (a, b) in enumerate(off)}
    x_high = {0: (4, 0, 1), 6: (4, 0, 4), 7: (4, 0, 0)}
    x_high |= {1 + i: (4, a, b) for i, (a, b) in enumerate(off)}
    x_high |= {8 + i: (4, a, 0) for i, a in enumerate(VEDGE)}
    y_low = {2 * i + j: (a, 0, b) for i, a in enumerate(VEDGE) for j, b in enumerate((1, 4))}
    y_low |= {11 + i: (a, 0, 0) for i, a in enumerate(VEDGE)}
    z_low = {3 * i + j: (a, b, 0) for i, a in enumerate(VEDGE) for j, b in enumerate(VEDGE)}
    return laid(24, x_low), laid(16, x_high), laid(16, y_low), laid(16, z_low)


def merged(*blocks):
    if isinstance(blocks[0][1], list):
        ends = [first for first, _ in blocks[1:]] + [8]
        return sum((b[first:end] for (first, b), end in zip(blocks, ends)), [])
    row = lax.broadcasted_iota(jnp.int32, blocks[0][1].shape, 0)
    out = blocks[0][1]
    for first, block in blocks[1:]:
        out = jnp.where(row < first, out, block)
    return out


def y_potential(y_low, far_x, near_x):
    return [y_low[0:8], merged((0, near_x[0:8]), (3, y_low[8:16]), (6, near_x[0:8])), far_x[0:8]]


def z_potential(z_low, far_x, near_x, far_y):
    return [
        z_low[0:8],
        merged((0, z_low[8:16]), (1, far_x[8:16]), (7, far_y[8:16])),
        merged((0, near_x[8:16]), (3, far_y[8:16]), (6, far_y[16:24])),
    ]


def carried(block, axis, layer, step):
    return [
        None
        if p is None or (layer is not None and p[axis] != layer)
        else p[:axis] + (p[axis] + step,) + p[axis + 1 :]
        for p in block
    ]


@functools.cache
def tables():
    out = {}
    magic = np.zeros((16, 16))
    kinetic = np.zeros((16, 16))
    for r in range(16):
        for c in range(16):
            if 0 <= c - r + 8 < 16:
                magic[r, c] = MAGIC[c - r + 8]
            if abs(c - r) < 15:
                kinetic[r, c] = KINETIC[abs(c - r)]
    eye = np.eye(16)
    full = np.eye(256)
    row_of = np.array(
        [f * 16 + px * 8 + x8 for x8 in range(8) for px in range(2) for f in range(16)]
    )
    lane_of = np.array(
        [
            (py * 8 + y8) * 16 + pz * 8 + z8
            for py in range(2)
            for pz in range(2)
            for y8 in range(8)
            for z8 in range(8)
        ]
    )
    prow = full[row_of]
    pcol = full[:, lane_of]
    out["prow"], out["prow_t"] = prow, prow.T
    out["pcol"], out["pcol_t"] = pcol, pcol.T
    pair = np.kron(magic, magic)[np.ix_(lane_of, lane_of)] - full
    out["yz"], out["yz_t"] = pair.T, pair
    along = np.kron(eye, magic)[np.ix_(row_of, row_of)] - full
    out["x"], out["x_t"] = along, along.T
    second = (np.kron(kinetic, eye) + np.kron(eye, kinetic))[np.ix_(lane_of, lane_of)]
    out["kyz_h"], out["kyz_l"] = split_parts(-0.5 * second)
    along = np.kron(eye, kinetic)[np.ix_(row_of, row_of)]
    out["kx_h"], out["kx_l"] = split_parts(-0.5 * along)

    first, second = candidate_rows()
    names = [((0, 0, 0), "own", f) for f in range(16)]
    names += [((d, 0, 0), "border", k) for d in (-1, 1) for k in range(8)]
    columns = [((0, 0, 0), "own", c % 16) for c in range(128)]
    columns += [(d, kind, k) for d, kind, q, k in first]
    names += sorted(set(columns) - set(names))
    out["fold"] = np.zeros((len(columns), 256))
    for row, name in enumerate(columns):
        out["fold"][row, names.index(name)] = 1
    out["decode"], out["codes_where"], out["codes_away"] = lane_tables(first)
    out["decode_last"], out["codes_where_last"], out["codes_away_last"] = lane_tables(second)
    names = sorted({(d, kind, k) for d, kind, q, k in second})
    out["fold_last"] = np.zeros((len(second), 256))
    for row, (d, kind, q, k) in enumerate(second):
        out["fold_last"][row, names.index((d, kind, k))] = 1
    own = [None] * 200
    for z in range(5):
        for x in range(5):
            for y in range(5):
                own[z * 40 + x * 8 + y] = (x, y, z)
    x_low, x_high, y_low, z_low = potential_blocks()
    out["faces"] = np.zeros((32, 200))
    for row, place in enumerate(y_low + z_low):
        if place is not None:
            out["faces"][row, own.index(place)] = 1
    out["face_x"] = np.zeros((40, 72))
    for row, place in enumerate(x_low + x_high):
        if place is not None:
            x, y, z = place
            out["face_x"][row, VEDGE.index(z) * 24 + SLAB.index(x) * 8 + y] = 1
    far_x = carried(x_low, 0, None, 5)
    near_x = carried(x_high, 0, None, -5)
    far_y = carried(sum(y_potential(y_low, far_x, near_x), []), 1, 0, 5)
    far_z = carried(sum(z_potential(z_low, far_x, near_x, far_y), []), 2, 0, 5)
    codes = []
    for place in far_x + near_x + far_y + far_z:
        code = -1.0 if place is None else code_number(place)
        codes.append(-1.0 if code in codes else code)
    codes = np.broadcast_to(np.array(codes), (8, len(codes)))
    out["codes_beside"], out["codes_far"] = codes[:, :40], codes[:, 40:]
    codes = [-1.0 if p is None else code_number(p) for p in own]
    out["codes_own"] = np.broadcast_to(np.array(codes), (8, len(codes)))
    return {
        k: np.ascontiguousarray(
            v, dtype=np.float32 if k.startswith("codes") else ml_dtypes.bfloat16
        )
        for k, v in out.items()
    }


def dot(a, b):
    return lax.dot_general(a, b, (((1,), (0,)), ((), ())), preferred_element_type=F32)


def dot_nt(a, b):
    return lax.dot_general(a, b, (((1,), (1,)), ((), ())), preferred_element_type=F32)


def rolled(values):
    return pltpu.roll(values, 64, 1)


def iota(dims, axis):
    return lax.broadcasted_iota(jnp.int32, dims, axis)


def low_lanes(values):
    return iota(values.shape, 1) < 64


def to_octants(split, roll):
    rows = split.shape[0] // 8
    blocks = []
    for py in range(split.shape[1] // 128):
        here = split[:, py * 128 : (py + 1) * 128]
        other = roll(here)
        for pz in range(2):
            pieces = []
            for x8 in range(0, 8, 2):
                one = slice(x8 * rows, (x8 + 1) * rows)
                two = slice((x8 + 1) * rows, (x8 + 2) * rows)
                if pz == 0:
                    left, right = here[one], other[two]
                else:
                    left, right = other[one], here[two]
                pieces.append(jnp.where(low_lanes(left), left, right))
            blocks.append(jnp.concatenate(pieces, axis=1))
    return blocks


def to_octant(split, roll):
    return jnp.concatenate(to_octants(split, roll), axis=0)


def to_split(octant, roll):
    columns = []
    for py in range(2):
        first = octant[(2 * py) * 32 : (2 * py + 1) * 32]
        second = octant[(2 * py + 1) * 32 : (2 * py + 2) * 32]
        pieces = []
        for pair in range(4):
            lanes = slice(pair * 128, (pair + 1) * 128)
            one, two = first[:, lanes], second[:, lanes]
            pieces.append(jnp.where(low_lanes(one), one, roll(two)))
            pieces.append(jnp.where(low_lanes(one), roll(one), two))
        columns.append(jnp.concatenate(pieces, axis=0))
    return jnp.concatenate(columns, axis=1)


def octant_places(anchor):
    row = iota((8, 16), 0)
    base = jnp.zeros((8, 16), F32)
    for c in range(3):
        base = jnp.where(row % 4 == c, jnp.broadcast_to(anchor[c], (8, 16)), base)
    spread = (iota((16, 128), 0) == iota((16, 128), 1) % 16).astype(F32).astype(BF16)
    base = dot(base.astype(BF16), spread)
    turned = jnp.concatenate([base] * 16, axis=0).T
    row, lane = iota((128, 128), 0), iota((128, 128), 1)
    lane = lane % 4
    bit = jnp.where(lane == 0, row // 16, jnp.where(lane == 1, row // 64, row // 32)) % 2
    return jnp.where(lane < 3, turned + bit.astype(F32), 0.0), base


def lift_table(y8):
    row, lane = iota((40, 384), 0), iota((40, 384), 1)
    match = (lane // 64 == row // 8) & (lane % 8 == row % 8) & ((lane // 8) % 8 == y8)
    return match.astype(F32).astype(BF16)


def across(values):
    eye = (iota((8, 128), 0) == iota((8, 128), 1)).astype(F32).astype(BF16)
    return dot_nt(eye, values.astype(BF16))


def export_tables(base):
    edge = ((base == 0.0) | (base == 4.0)).astype(F32)
    edge = jnp.maximum(jnp.maximum(edge[0:1], edge[1:2]), edge[2:3])
    row, lane = iota((128, 128), 0), iota((128, 128), 1)
    before = (row < lane % 16).astype(F32).astype(BF16)
    before = jnp.where(row < 16, before, jnp.zeros_like(before))
    rank = dot(jnp.broadcast_to(edge, (8, 128)).astype(BF16), before)[0:1]
    row, lane = iota((64, 128), 0), iota((64, 128), 1)
    chosen = (rank == (row % 8).astype(F32)) & (edge > 0.5) & (row // 8 == lane // 16)
    row, lane = iota((16, 128), 0), iota((16, 128), 1)
    rank = (lane % 16).astype(F32) - rank
    inner = (
        (rank == (row % 8).astype(F32))
        & (edge < 0.5)
        & (row // 8 == (lane // 16) % 2)
        & ((lane // 64 == 1) == (base[1:2] == 3.0))
        & (((lane // 32) % 2 == 1) == (base[2:3] == 3.0))
    )
    return chosen.astype(F32).astype(BF16), inner.astype(F32).astype(BF16)


def same_function():
    return (iota((128, 128), 0) % 16 == iota((128, 128), 1) % 16).astype(F32)


def over_octants(values):
    total = values[0:16]
    for p in range(1, 8):
        total = total + values[16 * p : 16 * p + 16]
    return total


def summed(values, table):
    high = values.astype(BF16)
    low = (values - high.astype(F32)).astype(BF16)
    both = dot(jnp.concatenate([high, low], axis=0), table)
    return both[:16] + both[16:]


def repeated(values):
    return jnp.concatenate([values] * 8, axis=0)


def function_rows(boxes, anchor, t, roll):
    places, base = octant_places(anchor)
    table, inner = export_tables(base)
    split = dot(dot(t["prow"](), boxes).astype(BF16), t["pcol"]())
    octant = to_octant(split, roll).astype(BF16)
    return split.astype(BF16), octant, places, table, inner


def coordinate_rows(table, inner, places):
    border = dot(table, places.astype(BF16))[0:8]
    within = dot(inner, places.astype(BF16))
    use = iota((8, 128), 1) % 8 < 4
    rows = [jnp.where(use, border, within[8 * i : 8 * i + 8]) for i in range(2)]
    return [jnp.concatenate([r] * 4, axis=1) for r in rows]


def regroup_table(layers):
    row, lane = iota((8 * layers, 40 * layers), 0), iota((8 * layers, 40 * layers), 1)
    target = jnp.where(row % 8 < 5, row // 8 * 40 + row % 8, -400)
    blocks = [(lane == target + 5 * x8).astype(F32).astype(BF16) for x8 in range(8)]
    return jnp.concatenate(blocks, axis=0)


def lifted_rows(potential_rows):
    total = None
    for y8 in range(8):
        part = dot(potential_rows(y8).astype(BF16), lift_table(y8))
        total = part if total is None else total + part
    return total.astype(BF16)


PACK = ("prow", "pcol", "face_x")


def pack_body(boxes, anchor, slab_rows, t, roll=rolled):
    _, octant, places, table, inner = function_rows(boxes(), anchor(), t, roll)
    exported = dot(table, octant).astype(BF16)
    corners = dot(inner, octant)
    told = coordinate_rows(table, inner, places)
    by_z = to_octants(dot(regroup_table(3), lifted_rows(slab_rows)), roll)
    slab = jnp.concatenate([by_z[z] for z in VEDGE], axis=0).astype(BF16)
    face = dot(t["face_x"](), slab)
    low = jnp.concatenate([corners[0:8], told[0], face[0:24]], axis=0).astype(BF16)
    high = jnp.concatenate([corners[8:16], told[1], face[24:40]], axis=0).astype(BF16)
    return exported, low, high


LAYOUT = ("prow", "pcol", "faces")


def layout_body(boxes, anchor, potential_rows, t, roll=rolled):
    split, octant, places, table, inner = function_rows(boxes, anchor, t, roll)
    exported = dot(table, octant).astype(BF16)
    told = coordinate_rows(table, inner, places)[0].astype(BF16)
    by_z = to_octants(dot(regroup_table(5), lifted_rows(potential_rows)), roll)
    v_rows = jnp.concatenate(by_z[:5], axis=0).astype(BF16)
    v_faces = dot(t["faces"](), v_rows).astype(BF16)
    return exported, told, v_faces, split, octant, v_rows, places, table


def grid_values(split, t, roll):
    inner = split.astype(F32) + dot(split, t["yz"]())
    return to_octant(inner + dot(t["x"](), inner.astype(BF16)), roll)


def kinetic_values(split, t, roll):
    lanes = dot(split, t["kyz_h"]()) + dot(split, t["kyz_l"]())
    rows = dot(t["kx_h"](), split) + dot(t["kx_l"](), split)
    return to_octant(lanes + rows, roll)


def returned_values(weighted, t, roll):
    split = to_split(weighted, roll)
    inner = split + dot(split.astype(BF16), t["yz_t"]())
    return to_octant(inner + dot(t["x_t"](), inner.astype(BF16)), roll)


def own_weights(overlaps, applied_bf, octant, geometry):
    products = over_octants((dot_nt(applied_bf, octant) * CELL - overlaps) * geometry)
    same = same_function()
    coupling = summed(products, same.astype(BF16)) + PENALTY * same[:16]
    return (repeated(coupling) * geometry).astype(BF16)


OPERATE = ("yz", "x", "kyz_h", "kyz_l", "kx_h", "kx_l")


def row_codes(places):
    x, y, z = (places[:, c : c + 1] + 5.0 for c in range(3))
    return 256.0 * x + 16.0 * y + z


def lane_codes(places):
    lanes = across(places) + 5.0
    return 256.0 * lanes[0:1] + 16.0 * lanes[1:2] + lanes[2:3]


def near_codes(told, decode, where, away):
    codes = dot(told[:, :72], decode)
    row = iota(codes.shape, 0).astype(F32)
    return jnp.sum(jnp.where(row == where[0:1], codes, 0.0), axis=0, keepdims=True) + away[0:1]


def picked(code, codes, rows):
    return dot((code == codes[0:1]).astype(F32).astype(BF16), rows)


def beside(left, right):
    pieces = []
    for q in range(8):
        pieces += [left[8 * q : 8 * q + 8], right[8 * q : 8 * q + 8]]
    return jnp.concatenate(pieces, axis=0)


def ahead_body(split, octant, places, v_own, xm, xp, t, roll=rolled):
    left, right = xm.astype(F32), xp.astype(F32)
    side = beside(left[:64], right[:64])
    side_split = to_split(side, roll).astype(BF16)
    codes = []
    for qy in range(2):
        for qz in range(2):
            for qx in range(2):
                for d, rows in ((-5, left[72:80]), (5, right[72:80])):
                    code = 256.0 * rows[:, 0:1] + 16.0 * rows[:, 1:2] + rows[:, 2:3]
                    codes.append(code + code_number((qx + d, qy, qz)))
    code = jnp.concatenate([row_codes(places)] + codes, axis=0)
    v_beside = jnp.concatenate([right[80:], left[80:]], axis=0).astype(BF16)
    v_box = picked(code, t["codes_own"](), v_own) + picked(code, t["codes_beside"](), v_beside)
    v_box = v_box.astype(BF16)
    grid = [grid_values(r, t, roll) for r in (split, side_split)]
    kinetic = [kinetic_values(r, t, roll) for r in (split, side_split)]
    target = jnp.concatenate([octant, side.astype(BF16)], axis=0)
    code = jnp.broadcast_to(code, (256, 128))
    return jnp.concatenate(grid, axis=0), jnp.concatenate(kinetic, axis=0), v_box, target, code


FIRST = ("yz_t", "x_t", "fold", "decode", "codes_where", "codes_away", "codes_far")
AHEAD = OPERATE + ("codes_own", "codes_beside")


def first_body(
    target, code, places, table, grid, kinetic, v_box, cand, told, yp, zp, t, roll=rolled
):
    code = code[:, 0:1]
    v_far = jnp.concatenate([yp.astype(F32)[104:], zp.astype(F32)[200:]], axis=0).astype(BF16)
    v_box = v_box.astype(F32) + picked(code, t["codes_far"](), v_far)
    weighted = grid * v_box
    applied = [returned_values(weighted[r], t, roll) for r in (slice(0, 128), slice(128, 256))]
    applied = jnp.concatenate(applied, axis=0) + kinetic
    applied_bf = applied.astype(BF16)
    near = near_codes(told, t["decode"](), t["codes_where"](), t["codes_away"]())
    same_place = code == jnp.concatenate([lane_codes(places), near], axis=1)
    rows = jnp.concatenate([target[:128], cand], axis=0)
    products = dot_nt(applied_bf, rows) - PENALTY * dot_nt(target, rows)
    products = jnp.where(same_place, products * CELL, 0.0)
    products = jnp.concatenate(
        [over_octants(products[:128]), over_octants(products[128:])], axis=0
    )
    coupling = folded(products, t["fold"]())
    identity = (iota((32, 256), 0) == iota((32, 256), 1)).astype(F32)
    coupling = dot_nt((coupling + PENALTY * identity).astype(BF16), t["fold"]())
    coupling = jnp.concatenate([coupling[:16]] * 8 + [coupling[16:]] * 8, axis=0)
    weights = jnp.where(same_place, coupling, 0.0).astype(BF16)
    correction = dot(weights, rows)
    current = (target.astype(F32) - STEP * (applied - correction)).astype(BF16)
    sent = dot(table, current[:128]).astype(BF16)
    side = current[128:].astype(F32)
    facing = []
    for q in range(4):
        facing += [side[32 * q + 16 : 32 * q + 24], side[32 * q + 8 : 32 * q + 16]]
    facing = jnp.concatenate(facing, axis=0).astype(BF16)
    return current[:128], sent, facing, v_box[:128].astype(BF16)


def folded(values, table):
    count = values.shape[0]
    high = values.astype(BF16)
    low = (values - high.astype(F32)).astype(BF16)
    both = dot(jnp.concatenate([high, low], axis=0), table)
    return both[:count] + both[count:]


SECOND = OPERATE + ("yz_t", "x_t", "decode_last", "codes_where_last", "codes_away_last")


def second_body(octant, v_box, places, told, t, roll=rolled):
    split = to_split(octant.astype(F32), roll).astype(BF16)
    weighted = grid_values(split, t, roll) * v_box.astype(F32)
    applied = returned_values(weighted, t, roll) + kinetic_values(split, t, roll)
    applied_bf = applied.astype(BF16)
    code = row_codes(places)
    geometry = (code == lane_codes(places)).astype(F32)
    overlaps = dot_nt(octant, octant) * (CELL * PENALTY)
    own_w = own_weights(overlaps, applied_bf, octant, geometry)
    done = octant.astype(F32) - STEP * (applied - dot(own_w, octant))
    lanes = near_codes(
        told, t["decode_last"](), t["codes_where_last"](), t["codes_away_last"]()
    )
    near = (code == lanes).astype(F32)
    return done, applied_bf, near.astype(BF16)


LAST = ("fold_last", "prow_t", "pcol_t")


def last_body(done, applied_bf, octant, cand, near, t, roll=rolled):
    near = near.astype(F32)
    products = dot_nt(applied_bf, cand) - PENALTY * dot_nt(octant, cand)
    coupling = folded(over_octants(products * CELL * near), t["fold_last"]())
    coupling = dot_nt(coupling.astype(BF16), t["fold_last"]())
    weights = (repeated(coupling) * near).astype(BF16)
    current = (done + STEP * dot(weights, cand)).astype(BF16)
    split = to_split(current.astype(F32), roll).astype(BF16)
    return dot(dot(t["prow_t"](), split).astype(BF16), t["pcol_t"]()).astype(BF16)


def shape(dims, dtype=BF16):
    return jax.ShapeDtypeStruct(dims, dtype)


class Fetched:
    def __init__(self, source, target, semaphore):
        self.copy = pltpu.make_async_copy(source, target, semaphore)
        self.target = target
        self.waiting = True
        self.copy.start()

    def ref(self):
        if self.waiting:
            self.copy.wait()
            self.waiting = False
        return self.target

    def __call__(self):
        return self.ref()[...]


def call(name, body, out_shape, inputs, consts, flops):
    arrays = list(inputs) + [jnp.asarray(tables()[k]) for k in consts]

    def kernel(*refs):
        t = {
            k: functools.partial(lambda ref: ref[...], r)
            for k, r in zip(consts, refs[len(inputs) : len(arrays)])
        }
        body(refs[: len(inputs)], t, refs[len(arrays) :])

    return pl.pallas_call(
        kernel,
        out_shape=out_shape,
        in_specs=[pl.BlockSpec(memory_space=pltpu.VMEM)] * len(arrays),
        out_specs=tuple(pl.BlockSpec(memory_space=pltpu.VMEM) for _ in out_shape),
        compiler_params=pltpu.CompilerParams(vmem_limit_bytes=24 << 20),
        cost_estimate=pl.CostEstimate(
            flops=flops, bytes_accessed=flops // 1000, transcendentals=0
        ),
        name=name,
    )(*arrays)


def pack_call(boxes, anchor, rows):
    arrays = [boxes, anchor, rows, rows] + [jnp.asarray(tables()[k]) for k in PACK]
    shapes = [(a.shape, a.dtype) for a in arrays]
    shapes[2:4] = [((960, 40), F32)]
    out_shape = (shape((104, 512)), shape((96, 512)))
    count = len(arrays)

    def kernel(*refs):
        sources = list(refs[:count])
        sources[2] = sources[2].at[pl.ds(0, 640)]
        sources[3] = sources[3].at[pl.ds(1280, 320)]
        targets = refs[count : count + 2]
        scratch = list(refs[count + 2 : -1])
        semaphores = refs[-1]
        low, high = scratch[-2:]
        slab = scratch[2]
        landing = scratch[:2] + [slab.at[pl.ds(0, 640)], slab.at[pl.ds(640, 320)]] + scratch[3:-2]
        fetched = [
            Fetched(a, b, semaphores.at[i]) for i, (a, b) in enumerate(zip(sources, landing))
        ]
        for piece in fetched:
            piece.ref()
        exported, low_rest, high_rest = pack_body(
            fetched[0],
            lambda: fetched[1]()[0, 0].astype(F32),
            lambda y8: slab[pl.ds(y8, 120, stride=8), :],
            dict(zip(PACK, fetched[4:])),
        )
        copies = []
        for i, (message, rest) in enumerate(((low, low_rest), (high, high_rest))):
            message[...] = jnp.concatenate([exported, rest], axis=0)
            copies.append(pltpu.make_async_copy(message, targets[i], semaphores.at[count + i]))
            copies[-1].start()
        for copy in copies:
            copy.wait()

    return pl.pallas_call(
        kernel,
        out_shape=out_shape,
        in_specs=[pl.BlockSpec(memory_space=pltpu.HBM)] * count,
        out_specs=tuple(pl.BlockSpec(memory_space=pltpu.HBM) for _ in out_shape),
        scratch_shapes=[pltpu.VMEM(*a) for a in shapes]
        + [pltpu.VMEM(o.shape, o.dtype) for o in out_shape]
        + [pltpu.SemaphoreType.DMA((count + 2,))],
        compiler_params=pltpu.CompilerParams(vmem_limit_bytes=56 << 20),
        cost_estimate=pl.CostEstimate(flops=10**8, bytes_accessed=10**6, transcendentals=0),
        name="pack",
    )(*arrays)


def layout_kernel(ins, t, outs):
    boxes, anchor, potential = ins
    got = layout_body(
        boxes[...],
        anchor[...][0, 0].astype(F32),
        lambda y8: potential[pl.ds(y8, 200, stride=8), :],
        t,
    )
    for ref, value in zip(outs, got):
        ref[...] = value


def whole_kernel(body):
    def run(ins, t, outs):
        got = body(*[r[...] for r in ins], t)
        for ref, value in zip(outs, got):
            ref[...] = value

    return run


def passed_along(value, axis, step):
    count = lax.axis_size(axis)
    return lax.ppermute(value, axis, [(i, (i + step) % count) for i in range(count)])


def y_messages(parts):
    return [[half_of(r, 32, keep) for r in parts] for keep in (0, 1)]


def z_messages(parts):
    return [[half_of(r, 16, keep) for r in parts] for keep in (0, 1)]


def sent_both(low, high, axis, send):
    below = send(jnp.concatenate(high, axis=0), axis, 1)
    return below, send(jnp.concatenate(low, axis=0), axis, -1)


def sent_in_pairs(low, high, axis, send):
    if send is not passed_along:
        return sent_both([low], [high], axis, send)
    count = lax.axis_size(axis)
    even = lax.axis_index(axis) % 2 == 0
    outside = [(i, (i + (1 if i % 2 else -1)) % count) for i in range(count)]
    inside = [(i, i + (-1 if i % 2 else 1)) for i in range(count)]
    far = lax.ppermute(jnp.where(even, low, high), axis, outside)
    near = lax.ppermute(jnp.where(even, high, low), axis, inside)
    return jnp.where(even, far, near), jnp.where(even, near, far)


def first_exchange(exported, told, xm, xp, v_faces, send=passed_along):
    v_far, v_near = xp[80:], xm[80:]
    group = lax.broadcasted_iota(jnp.int32, (8, 512), 1) // 8
    told_x = [xm[72:80], xp[72:80]]
    third = group % 3
    told_y = jnp.where(third == 0, told, jnp.where(third == 1, told_x[0], told_x[1]))
    parts = [exported, xm[:64], xp[:64]]
    low, high = y_messages(parts)
    ym, yp = sent_both(
        low + [told_y] + y_potential(v_faces[:16], v_far, v_near), high + [told_y], "gy", send
    )
    told_z = jnp.where(group < 3, told_y, jnp.where(group < 6, ym[96:], yp[96:104]))
    v_y = yp[104:]
    parts = parts + [ym[:96], yp[:96]]
    low, high = z_messages(parts)
    v_z = z_potential(v_faces[16:], v_far, v_near, v_y)
    zm, zp = sent_both(low + [told_z] + v_z, high + [told_z], "gz", send)
    rows = [xm[:64], xp[:64], xm[64:72], xp[64:72], ym[:96], yp[:96], zm[:192], zp[:192]]
    told = told_x + [ym[96:], yp[96:104], zm[192:], zp[192:200]]
    return jnp.concatenate(rows, axis=0), jnp.concatenate(told, axis=0), yp, zp


def second_exchange(exported, facing, send=passed_along):
    extra = [facing[:8]]
    low, high = y_messages([exported, facing])
    ym, yp = sent_both(low + extra, high, "gy", send)
    low, high = z_messages([exported, facing, ym, yp[:64]])
    low, high = jnp.concatenate(low, axis=0), jnp.concatenate(high, axis=0)
    zm, zp = sent_in_pairs(low, high, "gz", send)
    return jnp.concatenate([facing, ym, yp[:64], zm, zp], axis=0)


def local(boxes, anchors, potential):
    own = boxes.reshape(256, 256)
    anchor = jnp.transpose(anchors, (0, 1, 4, 2, 3))
    rows = potential.reshape(1600, 40)
    to_low, to_high = pack_call(own, anchor, rows)
    xm = passed_along(to_high, "gx", 1)
    xp = passed_along(to_low, "gx", -1)
    exported, told, v_faces, split, octant, v_own, places, table = call(
        "layout",
        layout_kernel,
        (
            shape((64, 512)),
            shape((8, 512)),
            shape((32, 512)),
            shape((256, 256)),
            shape((128, 512)),
            shape((200, 512)),
            shape((128, 128), F32),
            shape((64, 128)),
        ),
        (own, anchor, rows),
        LAYOUT,
        10**9,
    )
    cand, told, yp, zp = first_exchange(exported, told, xm, xp, v_faces)
    grid, kinetic, v_box, target, code = call(
        "ahead",
        whole_kernel(lambda *a: ahead_body(*a[:6], a[-1])),
        (
            shape((256, 512), F32),
            shape((256, 512), F32),
            shape((256, 512)),
            shape((256, 512)),
            shape((256, 128), F32),
        ),
        (split, octant, places, v_own, xm, xp, table),
        AHEAD + FIRST,
        10**9,
    )
    current, sent, facing, v_box = call(
        "first",
        whole_kernel(first_body),
        (shape((128, 512)), shape((64, 512)), shape((64, 512)), shape((128, 512))),
        (target, code, places, table, grid, kinetic, v_box, cand, told, yp, zp),
        FIRST,
        10**9,
    )
    near_rows = second_exchange(sent, facing)
    done, applied_bf, near = call(
        "second",
        whole_kernel(lambda *a: second_body(*a[:4], a[-1])),
        (shape((128, 512), F32), shape((128, 512)), shape((128, 448))),
        (current, v_box, places, told),
        SECOND + LAST,
        10**9,
    )
    (relaxed,) = call(
        "last",
        whole_kernel(lambda *a: (last_body(*a),)),
        (shape((256, 256)),),
        (done, applied_bf, current, near_rows, near),
        LAST,
        10**9,
    )
    return relaxed.reshape(boxes.shape)


def solution(mesh):
    placed = (
        P("gx", "gy", "gz", None, None, None),
        P("gx", "gy", "gz", None, None),
        P("gx", "gy", "gz"),
    )
    return jax.shard_map(
        local,
        mesh=mesh,
        in_specs=placed,
        out_specs=P("gx", "gy", "gz", None, None, None),
        check_vma=False,
    )
```

```python
import functools

import jax
import jax.numpy as jnp
import ml_dtypes
import numpy as np
from jax import lax
from jax.experimental import pallas as pl
from jax.experimental.pallas import tpu as pltpu
from jax.sharding import PartitionSpec as P

F32 = jnp.float32
BF16 = jnp.bfloat16

MAGIC = [
    8.433424733352934e-07,
    -1.290557201342061e-05,
    8.76298447621056e-05,
    -0.00030158038132690465,
    0.001747237136729939,
    -0.009420470302010804,
    0.023738214637249424,
    0.0612625895831208,
    0.9940415697834004,
    -0.06048952891969835,
    -0.021030251609303816,
    0.013372634148547948,
    -0.0034412814449349387,
    0.0004944322768868992,
    -5.185986881173433e-05,
    2.7273449291197967e-06,
]
KINETIC = [
    -3.55369228991319,
    2.2191465938911166,
    -0.6156141465570069,
    0.2371780582153806,
    -0.0822663999742123,
    0.0220702918848226,
    -0.004097656893426338,
    0.00045167920287502236,
    -2.3982285245075998e-05,
    2.0904234952920368e-06,
    -3.7230763047369276e-07,
    -1.0585705549674146e-08,
    -5.8138798302825405e-11,
    2.7080049362631943e-13,
    -6.9244749406392e-18,
]
CELL = 1.0 / 4096.0
STEP = 0.1
PENALTY = 3.0

VEDGE = (0, 1, 4)
SLAB = (0, 1, 4)


def split_parts(values):
    high = values.astype(ml_dtypes.bfloat16)
    low = (values - high.astype(np.float64)).astype(ml_dtypes.bfloat16)
    return high, low


def half_of(rows, size, keep):
    if isinstance(rows, list):
        return [r for i, r in enumerate(rows) if i // size % 2 == keep]
    count = rows.shape[0] // (2 * size)
    return rows.reshape(count, 2, size, rows.shape[1])[:, keep].reshape(count * size, -1)


def candidate_rows():
    own = [
        ((0, 0, 0), "border", (qy, qz, qx), k)
        for qy in range(2)
        for qz in range(2)
        for qx in range(2)
        for k in range(8)
    ]

    def moved(rows, axis, step):
        return [
            (d[:axis] + (d[axis] + step,) + d[axis + 1 :], kind, q, k) for d, kind, q, k in rows
        ]

    def onward(parts):
        low = moved(sum((half_of(r, 32, 1) for r in parts), []), 1, -1)
        high = moved(sum((half_of(r, 32, 0) for r in parts), []), 1, 1)
        parts = parts + [low, high]
        far_low = moved(sum((half_of(r, 16, 1) for r in parts), []), 2, -1)
        far_high = moved(sum((half_of(r, 16, 0) for r in parts), []), 2, 1)
        return low + high + far_low + far_high

    left, right = moved(own, 0, -1), moved(own, 0, 1)
    inner = [((d, 0, 0), "inner", (0, 0, 0), k) for d in (-1, 1) for k in range(8)]
    first = left + right + inner + onward([own, left, right])
    facing = [
        ((2 * side - 1, 0, 0), "border", (qy, qz, 1 - side), k)
        for qy in range(2)
        for qz in range(2)
        for side in range(2)
        for k in range(8)
    ]
    return first, facing + onward([own, facing])


def told_by(d):
    at = {0: 0, -1: 1, 1: 2}
    if d[2]:
        return (4 if d[2] < 0 else 5), 3 * at[d[1]] + at[d[0]]
    if d[1]:
        return (2 if d[1] < 0 else 3), at[d[0]]
    return (0 if d[0] < 0 else 1), 0


def lane_tables(rows):
    decode = np.zeros((72, len(rows)))
    where = np.zeros((8, len(rows)))
    away = np.zeros((8, len(rows)))
    for column, (d, kind, (qy, qz, qx), k) in enumerate(rows):
        message, group = told_by(d)
        first = 8 * group + (4 if kind == "inner" else 0)
        decode[first : first + 3, column] = (256, 16, 1)
        where[:, column] = 8 * message + k
        away[:, column] = code_number((5 * d[0] + qx, 5 * d[1] + qy, 5 * d[2] + qz))
    return decode, where, away


def code_number(place):
    return 256.0 * (place[0] + 5) + 16.0 * (place[1] + 5) + (place[2] + 5)


def laid(size, places):
    return [places.get(row) for row in range(size)]


def potential_blocks():
    off = [(a, b) for a in (1, 4) for b in (1, 4)]
    x_low = {0: (0, 0, 1), 1: (0, 0, 4), 2: (1, 0, 1), 3: (1, 0, 4), 6: (0, 0, 0), 7: (1, 0, 0)}
    x_low |= {9 + 3 * x + i: (x, a, 0) for x in range(2) for i, a in enumerate(VEDGE)}
    x_low |= {16 + 4 * x + i: (x, a, b) for x in range(2) for i, (a, b) in enumerate(off)}
    x_high = {0: (4, 0, 1), 6: (4, 0, 4), 7: (4, 0, 0)}
    x_high |= {1 + i: (4, a, b) for i, (a, b) in enumerate(off)}
    x_high |= {8 + i: (4, a, 0) for i, a in enumerate(VEDGE)}
    y_low = {2 * i + j: (a, 0, b) for i, a in enumerate(VEDGE) for j, b in enumerate((1, 4))}
    y_low |= {11 + i: (a, 0, 0) for i, a in enumerate(VEDGE)}
    z_low = {3 * i + j: (a, b, 0) for i, a in enumerate(VEDGE) for j, b in enumerate(VEDGE)}
    return laid(24, x_low), laid(16, x_high), laid(16, y_low), laid(16, z_low)


def merged(*blocks):
    if isinstance(blocks[0][1], list):
        ends = [first for first, _ in blocks[1:]] + [8]
        return sum((b[first:end] for (first, b), end in zip(blocks, ends)), [])
    row = lax.broadcasted_iota(jnp.int32, blocks[0][1].shape, 0)
    out = blocks[0][1]
    for first, block in blocks[1:]:
        out = jnp.where(row < first, out, block)
    return out


def y_potential(y_low, far_x, near_x):
    return [y_low[0:8], merged((0, near_x[0:8]), (3, y_low[8:16]), (6, near_x[0:8])), far_x[0:8]]


def z_potential(z_low, far_x, near_x, far_y):
    return [
        z_low[0:8],
        merged((0, z_low[8:16]), (1, far_x[8:16]), (7, far_y[8:16])),
        merged((0, near_x[8:16]), (3, far_y[8:16]), (6, far_y[16:24])),
    ]


def carried(block, axis, layer, step):
    return [
        None
        if p is None or (layer is not None and p[axis] != layer)
        else p[:axis] + (p[axis] + step,) + p[axis + 1 :]
        for p in block
    ]


@functools.cache
def tables():
    out = {}
    magic = np.zeros((16, 16))
    kinetic = np.zeros((16, 16))
    for r in range(16):
        for c in range(16):
            if 0 <= c - r + 8 < 16:
                magic[r, c] = MAGIC[c - r + 8]
            if abs(c - r) < 15:
                kinetic[r, c] = KINETIC[abs(c - r)]
    eye = np.eye(16)
    full = np.eye(256)
    row_of = np.array(
        [f * 16 + px * 8 + x8 for x8 in range(8) for px in range(2) for f in range(16)]
    )
    lane_of = np.array(
        [
            (py * 8 + y8) * 16 + pz * 8 + z8
            for py in range(2)
            for pz in range(2)
            for y8 in range(8)
            for z8 in range(8)
        ]
    )
    prow = full[row_of]
    pcol = full[:, lane_of]
    out["prow"], out["prow_t"] = prow, prow.T
    out["pcol"], out["pcol_t"] = pcol, pcol.T
    pair = np.kron(magic, magic)[np.ix_(lane_of, lane_of)] - full
    out["yz"], out["yz_t"] = pair.T, pair
    along = np.kron(eye, magic)[np.ix_(row_of, row_of)] - full
    out["x"], out["x_t"] = along, along.T
    second = (np.kron(kinetic, eye) + np.kron(eye, kinetic))[np.ix_(lane_of, lane_of)]
    out["kyz_h"], out["kyz_l"] = split_parts(-0.5 * second)
    along = np.kron(eye, kinetic)[np.ix_(row_of, row_of)]
    out["kx_h"], out["kx_l"] = split_parts(-0.5 * along)

    first, second = candidate_rows()
    names = [((0, 0, 0), "own", f) for f in range(16)]
    names += [((d, 0, 0), "border", k) for d in (-1, 1) for k in range(8)]
    columns = [((0, 0, 0), "own", c % 16) for c in range(128)]
    columns += [(d, kind, k) for d, kind, q, k in first]
    names += sorted(set(columns) - set(names))
    out["fold"] = np.zeros((len(columns), 256))
    for row, name in enumerate(columns):
        out["fold"][row, names.index(name)] = 1
    out["decode"], out["codes_where"], out["codes_away"] = lane_tables(first)
    out["decode_last"], out["codes_where_last"], out["codes_away_last"] = lane_tables(second)
    names = sorted({(d, kind, k) for d, kind, q, k in second})
    out["fold_last"] = np.zeros((len(second), 256))
    for row, (d, kind, q, k) in enumerate(second):
        out["fold_last"][row, names.index((d, kind, k))] = 1
    own = [None] * 200
    for z in range(5):
        for x in range(5):
            for y in range(5):
                own[z * 40 + x * 8 + y] = (x, y, z)
    x_low, x_high, y_low, z_low = potential_blocks()
    out["faces"] = np.zeros((32, 200))
    for row, place in enumerate(y_low + z_low):
        if place is not None:
            out["faces"][row, own.index(place)] = 1
    out["face_x"] = np.zeros((40, 72))
    for row, place in enumerate(x_low + x_high):
        if place is not None:
            x, y, z = place
            out["face_x"][row, VEDGE.index(z) * 24 + SLAB.index(x) * 8 + y] = 1
    far_x = carried(x_low, 0, None, 5)
    near_x = carried(x_high, 0, None, -5)
    far_y = carried(sum(y_potential(y_low, far_x, near_x), []), 1, 0, 5)
    far_z = carried(sum(z_potential(z_low, far_x, near_x, far_y), []), 2, 0, 5)
    codes = []
    for place in far_x + near_x + far_y + far_z:
        code = -1.0 if place is None else code_number(place)
        codes.append(-1.0 if code in codes else code)
    codes = np.broadcast_to(np.array(codes), (8, len(codes)))
    out["codes_beside"], out["codes_far"] = codes[:, :40], codes[:, 40:]
    codes = [-1.0 if p is None else code_number(p) for p in own]
    out["codes_own"] = np.broadcast_to(np.array(codes), (8, len(codes)))
    return {
        k: np.ascontiguousarray(
            v, dtype=np.float32 if k.startswith("codes") else ml_dtypes.bfloat16
        )
        for k, v in out.items()
    }


def dot(a, b):
    return lax.dot_general(a, b, (((1,), (0,)), ((), ())), preferred_element_type=F32)


def dot_nt(a, b):
    return lax.dot_general(a, b, (((1,), (1,)), ((), ())), preferred_element_type=F32)


def rolled(values):
    return pltpu.roll(values, 64, 1)


def iota(dims, axis):
    return lax.broadcasted_iota(jnp.int32, dims, axis)


def low_lanes(values):
    return iota(values.shape, 1) < 64


def to_octants(split, roll):
    rows = split.shape[0] // 8
    blocks = []
    for py in range(split.shape[1] // 128):
        here = split[:, py * 128 : (py + 1) * 128]
        other = roll(here)
        for pz in range(2):
            pieces = []
            for x8 in range(0, 8, 2):
                one = slice(x8 * rows, (x8 + 1) * rows)
                two = slice((x8 + 1) * rows, (x8 + 2) * rows)
                if pz == 0:
                    left, right = here[one], other[two]
                else:
                    left, right = other[one], here[two]
                pieces.append(jnp.where(low_lanes(left), left, right))
            blocks.append(jnp.concatenate(pieces, axis=1))
    return blocks


def to_octant(split, roll):
    return jnp.concatenate(to_octants(split, roll), axis=0)


def to_split(octant, roll):
    columns = []
    for py in range(2):
        first = octant[(2 * py) * 32 : (2 * py + 1) * 32]
        second = octant[(2 * py + 1) * 32 : (2 * py + 2) * 32]
        pieces = []
        for pair in range(4):
            lanes = slice(pair * 128, (pair + 1) * 128)
            one, two = first[:, lanes], second[:, lanes]
            pieces.append(jnp.where(low_lanes(one), one, roll(two)))
            pieces.append(jnp.where(low_lanes(one), roll(one), two))
        columns.append(jnp.concatenate(pieces, axis=0))
    return jnp.concatenate(columns, axis=1)


def octant_places(anchor):
    row = iota((8, 16), 0)
    base = jnp.zeros((8, 16), F32)
    for c in range(3):
        base = jnp.where(row % 4 == c, jnp.broadcast_to(anchor[c], (8, 16)), base)
    spread = (iota((16, 128), 0) == iota((16, 128), 1) % 16).astype(F32).astype(BF16)
    base = dot(base.astype(BF16), spread)
    turned = jnp.concatenate([base] * 16, axis=0).T
    row, lane = iota((128, 128), 0), iota((128, 128), 1)
    lane = lane % 4
    bit = jnp.where(lane == 0, row // 16, jnp.where(lane == 1, row // 64, row // 32)) % 2
    return jnp.where(lane < 3, turned + bit.astype(F32), 0.0), base


def lift_table(y8):
    row, lane = iota((40, 384), 0), iota((40, 384), 1)
    match = (lane // 64 == row // 8) & (lane % 8 == row % 8) & ((lane // 8) % 8 == y8)
    return match.astype(F32).astype(BF16)


def across(values):
    eye = (iota((8, 128), 0) == iota((8, 128), 1)).astype(F32).astype(BF16)
    return dot_nt(eye, values.astype(BF16))


def export_tables(base):
    edge = ((base == 0.0) | (base == 4.0)).astype(F32)
    edge = jnp.maximum(jnp.maximum(edge[0:1], edge[1:2]), edge[2:3])
    row, lane = iota((128, 128), 0), iota((128, 128), 1)
    before = (row < lane % 16).astype(F32).astype(BF16)
    before = jnp.where(row < 16, before, jnp.zeros_like(before))
    rank = dot(jnp.broadcast_to(edge, (8, 128)).astype(BF16), before)[0:1]
    row, lane = iota((64, 128), 0), iota((64, 128), 1)
    chosen = (rank == (row % 8).astype(F32)) & (edge > 0.5) & (row // 8 == lane // 16)
    row, lane = iota((16, 128), 0), iota((16, 128), 1)
    rank = (lane % 16).astype(F32) - rank
    inner = (
        (rank == (row % 8).astype(F32))
        & (edge < 0.5)
        & (row // 8 == (lane // 16) % 2)
        & ((lane // 64 == 1) == (base[1:2] == 3.0))
        & (((lane // 32) % 2 == 1) == (base[2:3] == 3.0))
    )
    return chosen.astype(F32).astype(BF16), inner.astype(F32).astype(BF16)


def same_function():
    return (iota((128, 128), 0) % 16 == iota((128, 128), 1) % 16).astype(F32)


def over_octants(values):
    total = values[0:16]
    for p in range(1, 8):
        total = total + values[16 * p : 16 * p + 16]
    return total


def summed(values, table):
    high = values.astype(BF16)
    low = (values - high.astype(F32)).astype(BF16)
    both = dot(jnp.concatenate([high, low], axis=0), table)
    return both[:16] + both[16:]


def repeated(values):
    return jnp.concatenate([values] * 8, axis=0)


def function_rows(boxes, anchor, t, roll):
    places, base = octant_places(anchor)
    table, inner = export_tables(base)
    split = dot(dot(t["prow"](), boxes).astype(BF16), t["pcol"]())
    octant = to_octant(split, roll).astype(BF16)
    return split.astype(BF16), octant, places, table, inner


def coordinate_rows(table, inner, places):
    border = dot(table, places.astype(BF16))[0:8]
    within = dot(inner, places.astype(BF16))
    use = iota((8, 128), 1) % 8 < 4
    rows = [jnp.where(use, border, within[8 * i : 8 * i + 8]) for i in range(2)]
    return [jnp.concatenate([r] * 4, axis=1) for r in rows]


def regroup_table(layers):
    row, lane = iota((8 * layers, 40 * layers), 0), iota((8 * layers, 40 * layers), 1)
    target = jnp.where(row % 8 < 5, row // 8 * 40 + row % 8, -400)
    blocks = [(lane == target + 5 * x8).astype(F32).astype(BF16) for x8 in range(8)]
    return jnp.concatenate(blocks, axis=0)


def lifted_rows(potential_rows):
    total = None
    for y8 in range(8):
        part = dot(potential_rows(y8).astype(BF16), lift_table(y8))
        total = part if total is None else total + part
    return total.astype(BF16)


PACK = ("prow", "pcol", "face_x")


def pack_body(boxes, anchor, slab_rows, t, roll=rolled):
    _, octant, places, table, inner = function_rows(boxes(), anchor(), t, roll)
    exported = dot(table, octant).astype(BF16)
    corners = dot(inner, octant)
    told = coordinate_rows(table, inner, places)
    by_z = to_octants(dot(regroup_table(3), lifted_rows(slab_rows)), roll)
    slab = jnp.concatenate([by_z[z] for z in VEDGE], axis=0).astype(BF16)
    face = dot(t["face_x"](), slab)
    low = jnp.concatenate([corners[0:8], told[0], face[0:24]], axis=0).astype(BF16)
    high = jnp.concatenate([corners[8:16], told[1], face[24:40]], axis=0).astype(BF16)
    return exported, low, high


LAYOUT = ("prow", "pcol", "faces")


def layout_body(boxes, anchor, potential_rows, t, roll=rolled):
    split, octant, places, table, inner = function_rows(boxes, anchor, t, roll)
    exported = dot(table, octant).astype(BF16)
    told = coordinate_rows(table, inner, places)[0].astype(BF16)
    by_z = to_octants(dot(regroup_table(5), lifted_rows(potential_rows)), roll)
    v_rows = jnp.concatenate(by_z[:5], axis=0).astype(BF16)
    v_faces = dot(t["faces"](), v_rows).astype(BF16)
    return exported, told, v_faces, split, octant, v_rows, places, table


def grid_values(split, t, roll):
    inner = split.astype(F32) + dot(split, t["yz"]())
    return to_octant(inner + dot(t["x"](), inner.astype(BF16)), roll)


def kinetic_values(split, t, roll):
    lanes = dot(split, t["kyz_h"]()) + dot(split, t["kyz_l"]())
    rows = dot(t["kx_h"](), split) + dot(t["kx_l"](), split)
    return to_octant(lanes + rows, roll)


def returned_values(weighted, t, roll):
    split = to_split(weighted, roll)
    inner = split + dot(split.astype(BF16), t["yz_t"]())
    return to_octant(inner + dot(t["x_t"](), inner.astype(BF16)), roll)


def own_weights(overlaps, applied_bf, octant, geometry):
    products = over_octants((dot_nt(applied_bf, octant) * CELL - overlaps) * geometry)
    same = same_function()
    coupling = summed(products, same.astype(BF16)) + PENALTY * same[:16]
    return (repeated(coupling) * geometry).astype(BF16)


OPERATE = ("yz", "x", "kyz_h", "kyz_l", "kx_h", "kx_l")


def row_codes(places):
    x, y, z = (places[:, c : c + 1] + 5.0 for c in range(3))
    return 256.0 * x + 16.0 * y + z


def lane_codes(places):
    lanes = across(places) + 5.0
    return 256.0 * lanes[0:1] + 16.0 * lanes[1:2] + lanes[2:3]


def near_codes(told, decode, where, away):
    codes = dot(told[:, :72], decode)
    row = iota(codes.shape, 0).astype(F32)
    return jnp.sum(jnp.where(row == where[0:1], codes, 0.0), axis=0, keepdims=True) + away[0:1]


def picked(code, codes, rows):
    return dot((code == codes[0:1]).astype(F32).astype(BF16), rows)


def beside(left, right):
    pieces = []
    for q in range(8):
        pieces += [left[8 * q : 8 * q + 8], right[8 * q : 8 * q + 8]]
    return jnp.concatenate(pieces, axis=0)


def ahead_body(split, octant, places, v_own, xm, xp, t, roll=rolled):
    left, right = xm.astype(F32), xp.astype(F32)
    side = beside(left[:64], right[:64])
    side_split = to_split(side, roll).astype(BF16)
    codes = []
    for qy in range(2):
        for qz in range(2):
            for qx in range(2):
                for d, rows in ((-5, left[72:80]), (5, right[72:80])):
                    code = 256.0 * rows[:, 0:1] + 16.0 * rows[:, 1:2] + rows[:, 2:3]
                    codes.append(code + code_number((qx + d, qy, qz)))
    code = jnp.concatenate([row_codes(places)] + codes, axis=0)
    v_beside = jnp.concatenate([right[80:], left[80:]], axis=0).astype(BF16)
    v_box = picked(code, t["codes_own"](), v_own) + picked(code, t["codes_beside"](), v_beside)
    v_box = v_box.astype(BF16)
    grid = [grid_values(r, t, roll) for r in (split, side_split)]
    kinetic = [kinetic_values(r, t, roll) for r in (split, side_split)]
    target = jnp.concatenate([octant, side.astype(BF16)], axis=0)
    code = jnp.broadcast_to(code, (256, 128))
    return jnp.concatenate(grid, axis=0), jnp.concatenate(kinetic, axis=0), v_box, target, code


FIRST = ("yz_t", "x_t", "fold", "decode", "codes_where", "codes_away", "codes_far")
AHEAD = OPERATE + ("codes_own", "codes_beside")


def first_body(
    target, code, places, table, grid, kinetic, v_box, cand, told, yp, zp, t, roll=rolled
):
    code = code[:, 0:1]
    v_far = jnp.concatenate([yp.astype(F32)[104:], zp.astype(F32)[200:]], axis=0).astype(BF16)
    v_box = v_box.astype(F32) + picked(code, t["codes_far"](), v_far)
    weighted = grid * v_box
    applied = [returned_values(weighted[r], t, roll) for r in (slice(0, 128), slice(128, 256))]
    applied = jnp.concatenate(applied, axis=0) + kinetic
    applied_bf = applied.astype(BF16)
    near = near_codes(told, t["decode"](), t["codes_where"](), t["codes_away"]())
    same_place = code == jnp.concatenate([lane_codes(places), near], axis=1)
    rows = jnp.concatenate([target[:128], cand], axis=0)
    products = dot_nt(applied_bf, rows) - PENALTY * dot_nt(target, rows)
    products = jnp.where(same_place, products * CELL, 0.0)
    products = jnp.concatenate(
        [over_octants(products[:128]), over_octants(products[128:])], axis=0
    )
    coupling = folded(products, t["fold"]())
    identity = (iota((32, 256), 0) == iota((32, 256), 1)).astype(F32)
    coupling = dot_nt((coupling + PENALTY * identity).astype(BF16), t["fold"]())
    coupling = jnp.concatenate([coupling[:16]] * 8 + [coupling[16:]] * 8, axis=0)
    weights = jnp.where(same_place, coupling, 0.0).astype(BF16)
    correction = dot(weights, rows)
    current = (target.astype(F32) - STEP * (applied - correction)).astype(BF16)
    sent = dot(table, current[:128]).astype(BF16)
    side = current[128:].astype(F32)
    facing = []
    for q in range(4):
        facing += [side[32 * q + 16 : 32 * q + 24], side[32 * q + 8 : 32 * q + 16]]
    facing = jnp.concatenate(facing, axis=0).astype(BF16)
    return current[:128], sent, facing, v_box[:128].astype(BF16)


def folded(values, table):
    count = values.shape[0]
    high = values.astype(BF16)
    low = (values - high.astype(F32)).astype(BF16)
    both = dot(jnp.concatenate([high, low], axis=0), table)
    return both[:count] + both[count:]


SECOND = OPERATE + ("yz_t", "x_t", "decode_last", "codes_where_last", "codes_away_last")


def second_body(octant, v_box, places, told, t, roll=rolled):
    split = to_split(octant.astype(F32), roll).astype(BF16)
    weighted = grid_values(split, t, roll) * v_box.astype(F32)
    applied = returned_values(weighted, t, roll) + kinetic_values(split, t, roll)
    applied_bf = applied.astype(BF16)
    code = row_codes(places)
    geometry = (code == lane_codes(places)).astype(F32)
    overlaps = dot_nt(octant, octant) * (CELL * PENALTY)
    own_w = own_weights(overlaps, applied_bf, octant, geometry)
    done = octant.astype(F32) - STEP * (applied - dot(own_w, octant))
    lanes = near_codes(
        told, t["decode_last"](), t["codes_where_last"](), t["codes_away_last"]()
    )
    near = (code == lanes).astype(F32)
    return done, applied_bf, near.astype(BF16)


LAST = ("fold_last", "prow_t", "pcol_t")


def last_body(done, applied_bf, octant, cand, near, t, roll=rolled):
    near = near.astype(F32)
    products = dot_nt(jnp.concatenate([applied_bf, octant], axis=0), cand)
    products = products[:128] - PENALTY * products[128:]
    coupling = folded(over_octants(products * CELL * near), t["fold_last"]())
    coupling = dot_nt(coupling.astype(BF16), t["fold_last"]())
    weights = (repeated(coupling) * near).astype(BF16)
    current = (done + STEP * dot(weights, cand)).astype(BF16)
    split = to_split(current.astype(F32), roll).astype(BF16)
    return dot(dot(t["prow_t"](), split).astype(BF16), t["pcol_t"]()).astype(BF16)


def shape(dims, dtype=BF16):
    return jax.ShapeDtypeStruct(dims, dtype)


class Fetched:
    def __init__(self, source, target, semaphore):
        self.copy = pltpu.make_async_copy(source, target, semaphore)
        self.target = target
        self.waiting = True
        self.copy.start()

    def ref(self):
        if self.waiting:
            self.copy.wait()
            self.waiting = False
        return self.target

    def __call__(self):
        return self.ref()[...]


def call(name, body, out_shape, inputs, consts, flops):
    arrays = list(inputs) + [jnp.asarray(tables()[k]) for k in consts]

    def kernel(*refs):
        t = {
            k: functools.partial(lambda ref: ref[...], r)
            for k, r in zip(consts, refs[len(inputs) : len(arrays)])
        }
        body(refs[: len(inputs)], t, refs[len(arrays) :])

    return pl.pallas_call(
        kernel,
        out_shape=out_shape,
        in_specs=[pl.BlockSpec(memory_space=pltpu.VMEM)] * len(arrays),
        out_specs=tuple(pl.BlockSpec(memory_space=pltpu.VMEM) for _ in out_shape),
        compiler_params=pltpu.CompilerParams(vmem_limit_bytes=24 << 20),
        cost_estimate=pl.CostEstimate(
            flops=flops, bytes_accessed=flops // 1000, transcendentals=0
        ),
        name=name,
    )(*arrays)


def pack_call(boxes, anchor, rows):
    arrays = [boxes, anchor, rows, rows] + [jnp.asarray(tables()[k]) for k in PACK]
    shapes = [(a.shape, a.dtype) for a in arrays]
    shapes[2:4] = [((960, 40), F32)]
    out_shape = (shape((104, 512)), shape((96, 512)))
    count = len(arrays)

    def kernel(*refs):
        sources = list(refs[:count])
        sources[2] = sources[2].at[pl.ds(0, 640)]
        sources[3] = sources[3].at[pl.ds(1280, 320)]
        targets = refs[count : count + 2]
        scratch = list(refs[count + 2 : -1])
        semaphores = refs[-1]
        low, high = scratch[-2:]
        slab = scratch[2]
        landing = scratch[:2] + [slab.at[pl.ds(0, 640)], slab.at[pl.ds(640, 320)]] + scratch[3:-2]
        fetched = [
            Fetched(a, b, semaphores.at[i]) for i, (a, b) in enumerate(zip(sources, landing))
        ]
        for piece in fetched:
            piece.ref()
        exported, low_rest, high_rest = pack_body(
            fetched[0],
            lambda: fetched[1]()[0, 0].astype(F32),
            lambda y8: slab[pl.ds(y8, 120, stride=8), :],
            dict(zip(PACK, fetched[4:])),
        )
        copies = []
        for i, (message, rest) in enumerate(((low, low_rest), (high, high_rest))):
            message[...] = jnp.concatenate([exported, rest], axis=0)
            copies.append(pltpu.make_async_copy(message, targets[i], semaphores.at[count + i]))
            copies[-1].start()
        for copy in copies:
            copy.wait()

    return pl.pallas_call(
        kernel,
        out_shape=out_shape,
        in_specs=[pl.BlockSpec(memory_space=pltpu.HBM)] * count,
        out_specs=tuple(pl.BlockSpec(memory_space=pltpu.HBM) for _ in out_shape),
        scratch_shapes=[pltpu.VMEM(*a) for a in shapes]
        + [pltpu.VMEM(o.shape, o.dtype) for o in out_shape]
        + [pltpu.SemaphoreType.DMA((count + 2,))],
        compiler_params=pltpu.CompilerParams(vmem_limit_bytes=56 << 20),
        cost_estimate=pl.CostEstimate(flops=10**8, bytes_accessed=10**6, transcendentals=0),
        name="pack",
    )(*arrays)


def layout_kernel(ins, t, outs):
    boxes, anchor, potential = ins
    got = layout_body(
        boxes[...],
        anchor[...][0, 0].astype(F32),
        lambda y8: potential[pl.ds(y8, 200, stride=8), :],
        t,
    )
    for ref, value in zip(outs, got):
        ref[...] = value


def whole_kernel(body):
    def run(ins, t, outs):
        got = body(*[r[...] for r in ins], t)
        for ref, value in zip(outs, got):
            ref[...] = value

    return run


def passed_along(value, axis, step):
    count = lax.axis_size(axis)
    return lax.ppermute(value, axis, [(i, (i + step) % count) for i in range(count)])


def y_messages(parts):
    return [[half_of(r, 32, keep) for r in parts] for keep in (0, 1)]


def z_messages(parts):
    return [[half_of(r, 16, keep) for r in parts] for keep in (0, 1)]


def sent_both(low, high, axis, send):
    below = send(jnp.concatenate(high, axis=0), axis, 1)
    return below, send(jnp.concatenate(low, axis=0), axis, -1)


def sent_in_pairs(low, high, axis, send):
    if send is not passed_along:
        return sent_both([low], [high], axis, send)
    count = lax.axis_size(axis)
    even = lax.axis_index(axis) % 2 == 0
    outside = [(i, (i + (1 if i % 2 else -1)) % count) for i in range(count)]
    inside = [(i, i + (-1 if i % 2 else 1)) for i in range(count)]
    far = lax.ppermute(jnp.where(even, low, high), axis, outside)
    near = lax.ppermute(jnp.where(even, high, low), axis, inside)
    return jnp.where(even, far, near), jnp.where(even, near, far)


def first_exchange(exported, told, xm, xp, v_faces, send=passed_along):
    v_far, v_near = xp[80:], xm[80:]
    group = lax.broadcasted_iota(jnp.int32, (8, 512), 1) // 8
    told_x = [xm[72:80], xp[72:80]]
    third = group % 3
    told_y = jnp.where(third == 0, told, jnp.where(third == 1, told_x[0], told_x[1]))
    parts = [exported, xm[:64], xp[:64]]
    low, high = y_messages(parts)
    ym, yp = sent_both(
        low + [told_y] + y_potential(v_faces[:16], v_far, v_near), high + [told_y], "gy", send
    )
    told_z = jnp.where(group < 3, told_y, jnp.where(group < 6, ym[96:], yp[96:104]))
    v_y = yp[104:]
    parts = parts + [ym[:96], yp[:96]]
    low, high = z_messages(parts)
    v_z = z_potential(v_faces[16:], v_far, v_near, v_y)
    zm, zp = sent_both(low + [told_z] + v_z, high + [told_z], "gz", send)
    rows = [xm[:64], xp[:64], xm[64:72], xp[64:72], ym[:96], yp[:96], zm[:192], zp[:192]]
    told = told_x + [ym[96:], yp[96:104], zm[192:], zp[192:200]]
    return jnp.concatenate(rows, axis=0), jnp.concatenate(told, axis=0), yp, zp


def second_exchange(exported, facing, send=passed_along):
    extra = [facing[:8]]
    low, high = y_messages([exported, facing])
    ym, yp = sent_both(low + extra, high, "gy", send)
    low, high = z_messages([exported, facing, ym, yp[:64]])
    low, high = jnp.concatenate(low, axis=0), jnp.concatenate(high, axis=0)
    zm, zp = sent_in_pairs(low, high, "gz", send)
    return jnp.concatenate([facing, ym, yp[:64], zm, zp], axis=0)


def local(boxes, anchors, potential):
    own = boxes.reshape(256, 256)
    anchor = jnp.transpose(anchors, (0, 1, 4, 2, 3))
    rows = potential.reshape(1600, 40)
    to_low, to_high = pack_call(own, anchor, rows)
    xm = passed_along(to_high, "gx", 1)
    xp = passed_along(to_low, "gx", -1)
    exported, told, v_faces, split, octant, v_own, places, table = call(
        "layout",
        layout_kernel,
        (
            shape((64, 512)),
            shape((8, 512)),
            shape((32, 512)),
            shape((256, 256)),
            shape((128, 512)),
            shape((200, 512)),
            shape((128, 128), F32),
            shape((64, 128)),
        ),
        (own, anchor, rows),
        LAYOUT,
        10**9,
    )
    cand, told, yp, zp = first_exchange(exported, told, xm, xp, v_faces)
    grid, kinetic, v_box, target, code = call(
        "ahead",
        whole_kernel(lambda *a: ahead_body(*a[:6], a[-1])),
        (
            shape((256, 512), F32),
            shape((256, 512), F32),
            shape((256, 512)),
            shape((256, 512)),
            shape((256, 128), F32),
        ),
        (split, octant, places, v_own, xm, xp, table),
        AHEAD + FIRST,
        10**9,
    )
    current, sent, facing, v_box = call(
        "first",
        whole_kernel(first_body),
        (shape((128, 512)), shape((64, 512)), shape((64, 512)), shape((128, 512))),
        (target, code, places, table, grid, kinetic, v_box, cand, told, yp, zp),
        FIRST,
        10**9,
    )
    near_rows = second_exchange(sent, facing)
    done, applied_bf, near = call(
        "second",
        whole_kernel(lambda *a: second_body(*a[:4], a[-1])),
        (shape((128, 512), F32), shape((128, 512)), shape((128, 448))),
        (current, v_box, places, told),
        SECOND + LAST,
        10**9,
    )
    (relaxed,) = call(
        "last",
        whole_kernel(lambda *a: (last_body(*a),)),
        (shape((256, 256)),),
        (done, applied_bf, current, near_rows, near),
        LAST,
        10**9,
    )
    return relaxed.reshape(boxes.shape)


def solution(mesh):
    placed = (
        P("gx", "gy", "gz", None, None, None),
        P("gx", "gy", "gz", None, None),
        P("gx", "gy", "gz"),
    )
    return jax.shard_map(
        local,
        mesh=mesh,
        in_specs=placed,
        out_specs=P("gx", "gy", "gz", None, None, None),
        check_vma=False,
    )
```

```python
import functools

import jax
import jax.numpy as jnp
import ml_dtypes
import numpy as np
from jax import lax
from jax.experimental import pallas as pl
from jax.experimental.pallas import tpu as pltpu
from jax.sharding import PartitionSpec as P

F32 = jnp.float32
BF16 = jnp.bfloat16

MAGIC = [
    8.433424733352934e-07,
    -1.290557201342061e-05,
    8.76298447621056e-05,
    -0.00030158038132690465,
    0.001747237136729939,
    -0.009420470302010804,
    0.023738214637249424,
    0.0612625895831208,
    0.9940415697834004,
    -0.06048952891969835,
    -0.021030251609303816,
    0.013372634148547948,
    -0.0034412814449349387,
    0.0004944322768868992,
    -5.185986881173433e-05,
    2.7273449291197967e-06,
]
KINETIC = [
    -3.55369228991319,
    2.2191465938911166,
    -0.6156141465570069,
    0.2371780582153806,
    -0.0822663999742123,
    0.0220702918848226,
    -0.004097656893426338,
    0.00045167920287502236,
    -2.3982285245075998e-05,
    2.0904234952920368e-06,
    -3.7230763047369276e-07,
    -1.0585705549674146e-08,
    -5.8138798302825405e-11,
    2.7080049362631943e-13,
    -6.9244749406392e-18,
]
CELL = 1.0 / 4096.0
STEP = 0.1
PENALTY = 3.0

VEDGE = (0, 1, 4)
SLAB = (0, 1, 4)


def split_parts(values):
    high = values.astype(ml_dtypes.bfloat16)
    low = (values - high.astype(np.float64)).astype(ml_dtypes.bfloat16)
    return high, low


def half_of(rows, size, keep):
    if isinstance(rows, list):
        return [r for i, r in enumerate(rows) if i // size % 2 == keep]
    count = rows.shape[0] // (2 * size)
    return rows.reshape(count, 2, size, rows.shape[1])[:, keep].reshape(count * size, -1)


def candidate_rows():
    own = [
        ((0, 0, 0), "border", (qy, qz, qx), k)
        for qy in range(2)
        for qz in range(2)
        for qx in range(2)
        for k in range(8)
    ]

    def moved(rows, axis, step):
        return [
            (d[:axis] + (d[axis] + step,) + d[axis + 1 :], kind, q, k) for d, kind, q, k in rows
        ]

    def onward(parts):
        low = moved(sum((half_of(r, 32, 1) for r in parts), []), 1, -1)
        high = moved(sum((half_of(r, 32, 0) for r in parts), []), 1, 1)
        parts = parts + [low, high]
        far_low = moved(sum((half_of(r, 16, 1) for r in parts), []), 2, -1)
        far_high = moved(sum((half_of(r, 16, 0) for r in parts), []), 2, 1)
        return low + high + far_low + far_high

    left, right = moved(own, 0, -1), moved(own, 0, 1)
    inner = [((d, 0, 0), "inner", (0, 0, 0), k) for d in (-1, 1) for k in range(8)]
    first = left + right + inner + onward([own, left, right])
    facing = [
        ((2 * side - 1, 0, 0), "border", (qy, qz, 1 - side), k)
        for qy in range(2)
        for qz in range(2)
        for side in range(2)
        for k in range(8)
    ]
    return first, facing + onward([own, facing])


def told_by(d):
    at = {0: 0, -1: 1, 1: 2}
    if d[2]:
        return (4 if d[2] < 0 else 5), 3 * at[d[1]] + at[d[0]]
    if d[1]:
        return (2 if d[1] < 0 else 3), at[d[0]]
    return (0 if d[0] < 0 else 1), 0


def lane_tables(rows):
    decode = np.zeros((72, len(rows)))
    where = np.zeros((8, len(rows)))
    away = np.zeros((8, len(rows)))
    for column, (d, kind, (qy, qz, qx), k) in enumerate(rows):
        message, group = told_by(d)
        first = 8 * group + (4 if kind == "inner" else 0)
        decode[first : first + 3, column] = (256, 16, 1)
        where[:, column] = 8 * message + k
        away[:, column] = code_number((5 * d[0] + qx, 5 * d[1] + qy, 5 * d[2] + qz))
    return decode, where, away


def code_number(place):
    return 256.0 * (place[0] + 5) + 16.0 * (place[1] + 5) + (place[2] + 5)


def laid(size, places):
    return [places.get(row) for row in range(size)]


def potential_blocks():
    off = [(a, b) for a in (1, 4) for b in (1, 4)]
    x_low = {0: (0, 0, 1), 1: (0, 0, 4), 2: (1, 0, 1), 3: (1, 0, 4), 6: (0, 0, 0), 7: (1, 0, 0)}
    x_low |= {9 + 3 * x + i: (x, a, 0) for x in range(2) for i, a in enumerate(VEDGE)}
    x_low |= {16 + 4 * x + i: (x, a, b) for x in range(2) for i, (a, b) in enumerate(off)}
    x_high = {0: (4, 0, 1), 6: (4, 0, 4), 7: (4, 0, 0)}
    x_high |= {1 + i: (4, a, b) for i, (a, b) in enumerate(off)}
    x_high |= {8 + i: (4, a, 0) for i, a in enumerate(VEDGE)}
    y_low = {2 * i + j: (a, 0, b) for i, a in enumerate(VEDGE) for j, b in enumerate((1, 4))}
    y_low |= {11 + i: (a, 0, 0) for i, a in enumerate(VEDGE)}
    z_low = {3 * i + j: (a, b, 0) for i, a in enumerate(VEDGE) for j, b in enumerate(VEDGE)}
    return laid(24, x_low), laid(16, x_high), laid(16, y_low), laid(16, z_low)


def merged(*blocks):
    if isinstance(blocks[0][1], list):
        ends = [first for first, _ in blocks[1:]] + [8]
        return sum((b[first:end] for (first, b), end in zip(blocks, ends)), [])
    row = lax.broadcasted_iota(jnp.int32, blocks[0][1].shape, 0)
    out = blocks[0][1]
    for first, block in blocks[1:]:
        out = jnp.where(row < first, out, block)
    return out


def y_potential(y_low, far_x, near_x):
    return [y_low[0:8], merged((0, near_x[0:8]), (3, y_low[8:16]), (6, near_x[0:8])), far_x[0:8]]


def z_potential(z_low, far_x, near_x, far_y):
    return [
        z_low[0:8],
        merged((0, z_low[8:16]), (1, far_x[8:16]), (7, far_y[8:16])),
        merged((0, near_x[8:16]), (3, far_y[8:16]), (6, far_y[16:24])),
    ]


def carried(block, axis, layer, step):
    return [
        None
        if p is None or (layer is not None and p[axis] != layer)
        else p[:axis] + (p[axis] + step,) + p[axis + 1 :]
        for p in block
    ]


@functools.cache
def tables():
    out = {}
    magic = np.zeros((16, 16))
    kinetic = np.zeros((16, 16))
    for r in range(16):
        for c in range(16):
            if 0 <= c - r + 8 < 16:
                magic[r, c] = MAGIC[c - r + 8]
            if abs(c - r) < 15:
                kinetic[r, c] = KINETIC[abs(c - r)]
    eye = np.eye(16)
    full = np.eye(256)
    row_of = np.array(
        [f * 16 + px * 8 + x8 for x8 in range(8) for px in range(2) for f in range(16)]
    )
    lane_of = np.array(
        [
            (py * 8 + y8) * 16 + pz * 8 + z8
            for py in range(2)
            for pz in range(2)
            for y8 in range(8)
            for z8 in range(8)
        ]
    )
    prow = full[row_of]
    pcol = full[:, lane_of]
    out["prow"], out["prow_t"] = prow, prow.T
    out["pcol"], out["pcol_t"] = pcol, pcol.T
    pair = np.kron(magic, magic)[np.ix_(lane_of, lane_of)] - full
    out["yz"], out["yz_t"] = pair.T, pair
    along = np.kron(eye, magic)[np.ix_(row_of, row_of)] - full
    out["x"], out["x_t"] = along, along.T
    second = (np.kron(kinetic, eye) + np.kron(eye, kinetic))[np.ix_(lane_of, lane_of)]
    out["kyz_h"], out["kyz_l"] = split_parts(-0.5 * second)
    along = np.kron(eye, kinetic)[np.ix_(row_of, row_of)]
    out["kx_h"], out["kx_l"] = split_parts(-0.5 * along)

    first, second = candidate_rows()
    names = [((0, 0, 0), "own", f) for f in range(16)]
    names += [((d, 0, 0), "border", k) for d in (-1, 1) for k in range(8)]
    columns = [((0, 0, 0), "own", c % 16) for c in range(128)]
    columns += [(d, kind, k) for d, kind, q, k in first]
    names += sorted(set(columns) - set(names))
    out["fold"] = np.zeros((len(columns), 256))
    for row, name in enumerate(columns):
        out["fold"][row, names.index(name)] = 1
    out["decode"], out["codes_where"], out["codes_away"] = lane_tables(first)
    out["decode_last"], out["codes_where_last"], out["codes_away_last"] = lane_tables(second)
    names = sorted({(d, kind, k) for d, kind, q, k in second})
    out["fold_last"] = np.zeros((len(second), 256))
    for row, (d, kind, q, k) in enumerate(second):
        out["fold_last"][row, names.index((d, kind, k))] = 1
    own = [None] * 200
    for z in range(5):
        for x in range(5):
            for y in range(5):
                own[z * 40 + x * 8 + y] = (x, y, z)
    x_low, x_high, y_low, z_low = potential_blocks()
    out["faces"] = np.zeros((32, 200))
    for row, place in enumerate(y_low + z_low):
        if place is not None:
            out["faces"][row, own.index(place)] = 1
    out["face_x"] = np.zeros((40, 72))
    for row, place in enumerate(x_low + x_high):
        if place is not None:
            x, y, z = place
            out["face_x"][row, VEDGE.index(z) * 24 + SLAB.index(x) * 8 + y] = 1
    far_x = carried(x_low, 0, None, 5)
    near_x = carried(x_high, 0, None, -5)
    far_y = carried(sum(y_potential(y_low, far_x, near_x), []), 1, 0, 5)
    far_z = carried(sum(z_potential(z_low, far_x, near_x, far_y), []), 2, 0, 5)
    codes = []
    for place in far_x + near_x + far_y + far_z:
        code = -1.0 if place is None else code_number(place)
        codes.append(-1.0 if code in codes else code)
    codes = np.broadcast_to(np.array(codes), (8, len(codes)))
    out["codes_beside"], out["codes_far"] = codes[:, :40], codes[:, 40:]
    codes = [-1.0 if p is None else code_number(p) for p in own]
    out["codes_own"] = np.broadcast_to(np.array(codes), (8, len(codes)))
    return {
        k: np.ascontiguousarray(
            v, dtype=np.float32 if k.startswith("codes") else ml_dtypes.bfloat16
        )
        for k, v in out.items()
    }


def dot(a, b):
    return lax.dot_general(a, b, (((1,), (0,)), ((), ())), preferred_element_type=F32)


def dot_nt(a, b):
    return lax.dot_general(a, b, (((1,), (1,)), ((), ())), preferred_element_type=F32)


def rolled(values):
    return pltpu.roll(values, 64, 1)


def iota(dims, axis):
    return lax.broadcasted_iota(jnp.int32, dims, axis)


def low_lanes(values):
    return iota(values.shape, 1) < 64


def to_octants(split, roll):
    rows = split.shape[0] // 8
    blocks = []
    for py in range(split.shape[1] // 128):
        here = split[:, py * 128 : (py + 1) * 128]
        other = roll(here)
        for pz in range(2):
            pieces = []
            for x8 in range(0, 8, 2):
                one = slice(x8 * rows, (x8 + 1) * rows)
                two = slice((x8 + 1) * rows, (x8 + 2) * rows)
                if pz == 0:
                    left, right = here[one], other[two]
                else:
                    left, right = other[one], here[two]
                pieces.append(jnp.where(low_lanes(left), left, right))
            blocks.append(jnp.concatenate(pieces, axis=1))
    return blocks


def to_octant(split, roll):
    return jnp.concatenate(to_octants(split, roll), axis=0)


def to_split(octant, roll):
    columns = []
    for py in range(2):
        first = octant[(2 * py) * 32 : (2 * py + 1) * 32]
        second = octant[(2 * py + 1) * 32 : (2 * py + 2) * 32]
        pieces = []
        for pair in range(4):
            lanes = slice(pair * 128, (pair + 1) * 128)
            one, two = first[:, lanes], second[:, lanes]
            pieces.append(jnp.where(low_lanes(one), one, roll(two)))
            pieces.append(jnp.where(low_lanes(one), roll(one), two))
        columns.append(jnp.concatenate(pieces, axis=0))
    return jnp.concatenate(columns, axis=1)


def octant_places(anchor):
    row = iota((8, 16), 0)
    base = jnp.zeros((8, 16), F32)
    for c in range(3):
        base = jnp.where(row % 4 == c, jnp.broadcast_to(anchor[c], (8, 16)), base)
    spread = (iota((16, 128), 0) == iota((16, 128), 1) % 16).astype(F32).astype(BF16)
    base = dot(base.astype(BF16), spread)
    turned = jnp.concatenate([base] * 16, axis=0).T
    row, lane = iota((128, 128), 0), iota((128, 128), 1)
    lane = lane % 4
    bit = jnp.where(lane == 0, row // 16, jnp.where(lane == 1, row // 64, row // 32)) % 2
    return jnp.where(lane < 3, turned + bit.astype(F32), 0.0), base


def lift_table(y8):
    row, lane = iota((40, 384), 0), iota((40, 384), 1)
    match = (lane // 64 == row // 8) & (lane % 8 == row % 8) & ((lane // 8) % 8 == y8)
    return match.astype(F32).astype(BF16)


def across(values):
    eye = (iota((8, 128), 0) == iota((8, 128), 1)).astype(F32).astype(BF16)
    return dot_nt(eye, values.astype(BF16))


def export_tables(base):
    edge = ((base == 0.0) | (base == 4.0)).astype(F32)
    edge = jnp.maximum(jnp.maximum(edge[0:1], edge[1:2]), edge[2:3])
    row, lane = iota((128, 128), 0), iota((128, 128), 1)
    before = (row < lane % 16).astype(F32).astype(BF16)
    before = jnp.where(row < 16, before, jnp.zeros_like(before))
    rank = dot(jnp.broadcast_to(edge, (8, 128)).astype(BF16), before)[0:1]
    row, lane = iota((64, 128), 0), iota((64, 128), 1)
    chosen = (rank == (row % 8).astype(F32)) & (edge > 0.5) & (row // 8 == lane // 16)
    row, lane = iota((16, 128), 0), iota((16, 128), 1)
    rank = (lane % 16).astype(F32) - rank
    inner = (
        (rank == (row % 8).astype(F32))
        & (edge < 0.5)
        & (row // 8 == (lane // 16) % 2)
        & ((lane // 64 == 1) == (base[1:2] == 3.0))
        & (((lane // 32) % 2 == 1) == (base[2:3] == 3.0))
    )
    return chosen.astype(F32).astype(BF16), inner.astype(F32).astype(BF16)


def same_function():
    return (iota((128, 128), 0) % 16 == iota((128, 128), 1) % 16).astype(F32)


def over_octants(values):
    total = values[0:16]
    for p in range(1, 8):
        total = total + values[16 * p : 16 * p + 16]
    return total


def summed(values, table):
    high = values.astype(BF16)
    low = (values - high.astype(F32)).astype(BF16)
    both = dot(jnp.concatenate([high, low], axis=0), table)
    return both[:16] + both[16:]


def repeated(values):
    return jnp.concatenate([values] * 8, axis=0)


def function_rows(boxes, anchor, t, roll):
    places, base = octant_places(anchor)
    table, inner = export_tables(base)
    split = dot(dot(t["prow"](), boxes).astype(BF16), t["pcol"]())
    octant = to_octant(split, roll).astype(BF16)
    return split.astype(BF16), octant, places, table, inner


def coordinate_rows(table, inner, places):
    border = dot(table, places.astype(BF16))[0:8]
    within = dot(inner, places.astype(BF16))
    use = iota((8, 128), 1) % 8 < 4
    rows = [jnp.where(use, border, within[8 * i : 8 * i + 8]) for i in range(2)]
    return [jnp.concatenate([r] * 4, axis=1) for r in rows]


def regroup_table(layers):
    row, lane = iota((8 * layers, 40 * layers), 0), iota((8 * layers, 40 * layers), 1)
    target = jnp.where(row % 8 < 5, row // 8 * 40 + row % 8, -400)
    blocks = [(lane == target + 5 * x8).astype(F32).astype(BF16) for x8 in range(8)]
    return jnp.concatenate(blocks, axis=0)


def lifted_rows(potential_rows):
    total = None
    for y8 in range(8):
        part = dot(potential_rows(y8).astype(BF16), lift_table(y8))
        total = part if total is None else total + part
    return total.astype(BF16)


PACK = ("prow", "pcol", "face_x")


def pack_body(boxes, anchor, slab_rows, t, roll=rolled):
    _, octant, places, table, inner = function_rows(boxes(), anchor(), t, roll)
    exported = dot(table, octant).astype(BF16)
    corners = dot(inner, octant)
    told = coordinate_rows(table, inner, places)
    by_z = to_octants(dot(regroup_table(3), lifted_rows(slab_rows)), roll)
    slab = jnp.concatenate([by_z[z] for z in VEDGE], axis=0).astype(BF16)
    face = dot(t["face_x"](), slab)
    low = jnp.concatenate([corners[0:8], told[0], face[0:24]], axis=0).astype(BF16)
    high = jnp.concatenate([corners[8:16], told[1], face[24:40]], axis=0).astype(BF16)
    return exported, low, high


LAYOUT = ("prow", "pcol", "faces")


def layout_body(boxes, anchor, potential_rows, t, roll=rolled):
    split, octant, places, table, inner = function_rows(boxes, anchor, t, roll)
    exported = dot(table, octant).astype(BF16)
    told = coordinate_rows(table, inner, places)[0].astype(BF16)
    by_z = to_octants(dot(regroup_table(5), lifted_rows(potential_rows)), roll)
    v_rows = jnp.concatenate(by_z[:5], axis=0).astype(BF16)
    v_faces = dot(t["faces"](), v_rows).astype(BF16)
    return exported, told, v_faces, split, octant, v_rows, places, table


def grid_values(split, t, roll):
    inner = split.astype(F32) + dot(split, t["yz"]())
    return to_octant(inner + dot(t["x"](), inner.astype(BF16)), roll)


def kinetic_values(split, t, roll):
    lanes = dot(split, t["kyz_h"]()) + dot(split, t["kyz_l"]())
    rows = dot(t["kx_h"](), split) + dot(t["kx_l"](), split)
    return to_octant(lanes + rows, roll)


def returned_values(weighted, t, roll):
    split = to_split(weighted, roll)
    inner = split + dot(split.astype(BF16), t["yz_t"]())
    return to_octant(inner + dot(t["x_t"](), inner.astype(BF16)), roll)


def own_weights(overlaps, applied_bf, octant, geometry):
    products = over_octants((dot_nt(applied_bf, octant) * CELL - overlaps) * geometry)
    same = same_function()
    coupling = summed(products, same.astype(BF16)) + PENALTY * same[:16]
    return (repeated(coupling) * geometry).astype(BF16)


OPERATE = ("yz", "x", "kyz_h", "kyz_l", "kx_h", "kx_l")


def row_codes(places):
    x, y, z = (places[:, c : c + 1] + 5.0 for c in range(3))
    return 256.0 * x + 16.0 * y + z


def lane_codes(places):
    lanes = across(places) + 5.0
    return 256.0 * lanes[0:1] + 16.0 * lanes[1:2] + lanes[2:3]


def near_codes(told, decode, where, away):
    codes = dot(told[:, :72], decode)
    row = iota(codes.shape, 0).astype(F32)
    return jnp.sum(jnp.where(row == where[0:1], codes, 0.0), axis=0, keepdims=True) + away[0:1]


def picked(code, codes, rows):
    return dot((code == codes[0:1]).astype(F32).astype(BF16), rows)


def beside(left, right):
    pieces = []
    for q in range(8):
        pieces += [left[8 * q : 8 * q + 8], right[8 * q : 8 * q + 8]]
    return jnp.concatenate(pieces, axis=0)


def ahead_body(split, octant, places, v_own, xm, xp, t, roll=rolled):
    left, right = xm.astype(F32), xp.astype(F32)
    side = beside(left[:64], right[:64])
    side_split = to_split(side, roll).astype(BF16)
    codes = []
    for qy in range(2):
        for qz in range(2):
            for qx in range(2):
                for d, rows in ((-5, left[72:80]), (5, right[72:80])):
                    code = 256.0 * rows[:, 0:1] + 16.0 * rows[:, 1:2] + rows[:, 2:3]
                    codes.append(code + code_number((qx + d, qy, qz)))
    code = jnp.concatenate([row_codes(places)] + codes, axis=0)
    v_beside = jnp.concatenate([right[80:], left[80:]], axis=0).astype(BF16)
    v_box = picked(code, t["codes_own"](), v_own) + picked(code, t["codes_beside"](), v_beside)
    v_box = v_box.astype(BF16)
    grid = [grid_values(r, t, roll) for r in (split, side_split)]
    kinetic = [kinetic_values(r, t, roll) for r in (split, side_split)]
    target = jnp.concatenate([octant, side.astype(BF16)], axis=0)
    code = jnp.broadcast_to(code, (256, 128))
    return jnp.concatenate(grid, axis=0), jnp.concatenate(kinetic, axis=0), v_box, target, code


FIRST = ("yz_t", "x_t", "fold", "decode", "codes_where", "codes_away", "codes_far")
AHEAD = OPERATE + ("codes_own", "codes_beside")


def first_body(
    target, code, places, table, grid, kinetic, v_box, cand, told, yp, zp, t, roll=rolled
):
    code = code[:, 0:1]
    v_far = jnp.concatenate([yp.astype(F32)[104:], zp.astype(F32)[200:]], axis=0).astype(BF16)
    v_box = v_box.astype(F32) + picked(code, t["codes_far"](), v_far)
    weighted = grid * v_box
    applied = [returned_values(weighted[r], t, roll) for r in (slice(0, 128), slice(128, 256))]
    applied = jnp.concatenate(applied, axis=0) + kinetic
    applied_bf = applied.astype(BF16)
    near = near_codes(told, t["decode"](), t["codes_where"](), t["codes_away"]())
    same_place = code == jnp.concatenate([lane_codes(places), near], axis=1)
    rows = jnp.concatenate([target[:128], cand], axis=0)
    products = dot_nt(applied_bf, rows) - PENALTY * dot_nt(target, rows)
    products = jnp.where(same_place, products * CELL, 0.0)
    products = jnp.concatenate(
        [over_octants(products[:128]), over_octants(products[128:])], axis=0
    )
    coupling = folded(products, t["fold"]())
    identity = (iota((32, 256), 0) == iota((32, 256), 1)).astype(F32)
    coupling = dot_nt((coupling + PENALTY * identity).astype(BF16), t["fold"]())
    coupling = jnp.concatenate([coupling[:16]] * 8 + [coupling[16:]] * 8, axis=0)
    weights = jnp.where(same_place, coupling, 0.0).astype(BF16)
    correction = dot(weights, rows)
    current = (target.astype(F32) - STEP * (applied - correction)).astype(BF16)
    sent = dot(table, current[:128]).astype(BF16)
    side = current[128:].astype(F32)
    facing = []
    for q in range(4):
        facing += [side[32 * q + 16 : 32 * q + 24], side[32 * q + 8 : 32 * q + 16]]
    facing = jnp.concatenate(facing, axis=0).astype(BF16)
    return current[:128], sent, facing, v_box[:128].astype(BF16)


def folded(values, table):
    count = values.shape[0]
    high = values.astype(BF16)
    low = (values - high.astype(F32)).astype(BF16)
    both = dot(jnp.concatenate([high, low], axis=0), table)
    return both[:count] + both[count:]


SECOND = OPERATE + ("yz_t", "x_t", "decode_last", "codes_where_last", "codes_away_last")


def second_body(octant, v_box, places, told, t, roll=rolled):
    split = to_split(octant.astype(F32), roll).astype(BF16)
    weighted = grid_values(split, t, roll) * v_box.astype(F32)
    applied = returned_values(weighted, t, roll) + kinetic_values(split, t, roll)
    applied_bf = applied.astype(BF16)
    code = row_codes(places)
    geometry = (code == lane_codes(places)).astype(F32)
    overlaps = dot_nt(octant, octant) * (CELL * PENALTY)
    own_w = own_weights(overlaps, applied_bf, octant, geometry)
    done = octant.astype(F32) - STEP * (applied - dot(own_w, octant))
    lanes = near_codes(
        told, t["decode_last"](), t["codes_where_last"](), t["codes_away_last"]()
    )
    near = (code == lanes).astype(F32)
    return done, applied_bf, near.astype(BF16)


LAST = ("fold_last", "prow_t", "pcol_t")


def last_body(done, applied_bf, octant, cand, near, t, roll=rolled):
    near = near.astype(F32)
    products = dot_nt(jnp.concatenate([applied_bf, octant], axis=0), cand)
    products = products[:128] - PENALTY * products[128:]
    coupling = folded(over_octants(products * CELL * near), t["fold_last"]())
    coupling = dot_nt(coupling.astype(BF16), t["fold_last"]())
    weights = (repeated(coupling) * near).astype(BF16)
    current = (done + STEP * dot(weights, cand)).astype(BF16)
    split = to_split(current.astype(F32), roll).astype(BF16)
    return dot(split, t["pcol_t"]()).astype(BF16)


def last_kernel(ins, t, outs):
    rows = last_body(*[r[...] for r in ins], t)
    target, held, semaphores = outs
    copies = []
    for half in range(2):
        part = pl.ds(128 * half, 128)
        held[part, :] = dot(t["prow_t"]()[128 * half : 128 * half + 128], rows).astype(BF16)
        copies.append(
            pltpu.make_async_copy(held.at[part], target.at[part], semaphores.at[half])
        )
        copies[-1].start()
    for copy in copies:
        copy.wait()


def shape(dims, dtype=BF16):
    return jax.ShapeDtypeStruct(dims, dtype)


class Fetched:
    def __init__(self, source, target, semaphore):
        self.copy = pltpu.make_async_copy(source, target, semaphore)
        self.target = target
        self.waiting = True
        self.copy.start()

    def ref(self):
        if self.waiting:
            self.copy.wait()
            self.waiting = False
        return self.target

    def __call__(self):
        return self.ref()[...]


def call(name, body, out_shape, inputs, consts, flops, space=pltpu.VMEM, scratch=()):
    arrays = list(inputs) + [jnp.asarray(tables()[k]) for k in consts]

    def kernel(*refs):
        t = {
            k: functools.partial(lambda ref: ref[...], r)
            for k, r in zip(consts, refs[len(inputs) : len(arrays)])
        }
        body(refs[: len(inputs)], t, refs[len(arrays) :])

    return pl.pallas_call(
        kernel,
        out_shape=out_shape,
        in_specs=[pl.BlockSpec(memory_space=pltpu.VMEM)] * len(arrays),
        out_specs=tuple(pl.BlockSpec(memory_space=space) for _ in out_shape),
        scratch_shapes=scratch,
        compiler_params=pltpu.CompilerParams(vmem_limit_bytes=24 << 20),
        cost_estimate=pl.CostEstimate(
            flops=flops, bytes_accessed=flops // 1000, transcendentals=0
        ),
        name=name,
    )(*arrays)


def pack_call(boxes, anchor, rows):
    arrays = [boxes, anchor, rows, rows] + [jnp.asarray(tables()[k]) for k in PACK]
    shapes = [(a.shape, a.dtype) for a in arrays]
    shapes[2:4] = [((960, 40), F32)]
    out_shape = (shape((104, 512)), shape((96, 512)))
    count = len(arrays)

    def kernel(*refs):
        sources = list(refs[:count])
        sources[2] = sources[2].at[pl.ds(0, 640)]
        sources[3] = sources[3].at[pl.ds(1280, 320)]
        targets = refs[count : count + 2]
        scratch = list(refs[count + 2 : -1])
        semaphores = refs[-1]
        low, high = scratch[-2:]
        slab = scratch[2]
        landing = scratch[:2] + [slab.at[pl.ds(0, 640)], slab.at[pl.ds(640, 320)]] + scratch[3:-2]
        fetched = [
            Fetched(a, b, semaphores.at[i]) for i, (a, b) in enumerate(zip(sources, landing))
        ]
        for piece in fetched:
            piece.ref()
        exported, low_rest, high_rest = pack_body(
            fetched[0],
            lambda: fetched[1]()[0, 0].astype(F32),
            lambda y8: slab[pl.ds(y8, 120, stride=8), :],
            dict(zip(PACK, fetched[4:])),
        )
        copies = []
        for i, (message, rest) in enumerate(((low, low_rest), (high, high_rest))):
            message[...] = jnp.concatenate([exported, rest], axis=0)
            copies.append(pltpu.make_async_copy(message, targets[i], semaphores.at[count + i]))
            copies[-1].start()
        for copy in copies:
            copy.wait()

    return pl.pallas_call(
        kernel,
        out_shape=out_shape,
        in_specs=[pl.BlockSpec(memory_space=pltpu.HBM)] * count,
        out_specs=tuple(pl.BlockSpec(memory_space=pltpu.HBM) for _ in out_shape),
        scratch_shapes=[pltpu.VMEM(*a) for a in shapes]
        + [pltpu.VMEM(o.shape, o.dtype) for o in out_shape]
        + [pltpu.SemaphoreType.DMA((count + 2,))],
        compiler_params=pltpu.CompilerParams(vmem_limit_bytes=56 << 20),
        cost_estimate=pl.CostEstimate(flops=10**8, bytes_accessed=10**6, transcendentals=0),
        name="pack",
    )(*arrays)


def layout_kernel(ins, t, outs):
    boxes, anchor, potential = ins
    got = layout_body(
        boxes[...],
        anchor[...][0, 0].astype(F32),
        lambda y8: potential[pl.ds(y8, 200, stride=8), :],
        t,
    )
    for ref, value in zip(outs, got):
        ref[...] = value


def whole_kernel(body):
    def run(ins, t, outs):
        got = body(*[r[...] for r in ins], t)
        for ref, value in zip(outs, got):
            ref[...] = value

    return run


def passed_along(value, axis, step):
    count = lax.axis_size(axis)
    return lax.ppermute(value, axis, [(i, (i + step) % count) for i in range(count)])


def y_messages(parts):
    return [[half_of(r, 32, keep) for r in parts] for keep in (0, 1)]


def z_messages(parts):
    return [[half_of(r, 16, keep) for r in parts] for keep in (0, 1)]


def sent_both(low, high, axis, send):
    below = send(jnp.concatenate(high, axis=0), axis, 1)
    return below, send(jnp.concatenate(low, axis=0), axis, -1)


def sent_in_pairs(low, high, axis, send):
    if send is not passed_along:
        return sent_both([low], [high], axis, send)
    count = lax.axis_size(axis)
    even = lax.axis_index(axis) % 2 == 0
    outside = [(i, (i + (1 if i % 2 else -1)) % count) for i in range(count)]
    inside = [(i, i + (-1 if i % 2 else 1)) for i in range(count)]
    far = lax.ppermute(jnp.where(even, low, high), axis, outside)
    near = lax.ppermute(jnp.where(even, high, low), axis, inside)
    return jnp.where(even, far, near), jnp.where(even, near, far)


def first_exchange(exported, told, xm, xp, v_faces, send=passed_along):
    v_far, v_near = xp[80:], xm[80:]
    group = lax.broadcasted_iota(jnp.int32, (8, 512), 1) // 8
    told_x = [xm[72:80], xp[72:80]]
    third = group % 3
    told_y = jnp.where(third == 0, told, jnp.where(third == 1, told_x[0], told_x[1]))
    parts = [exported, xm[:64], xp[:64]]
    low, high = y_messages(parts)
    ym, yp = sent_both(
        low + [told_y] + y_potential(v_faces[:16], v_far, v_near), high + [told_y], "gy", send
    )
    told_z = jnp.where(group < 3, told_y, jnp.where(group < 6, ym[96:], yp[96:104]))
    v_y = yp[104:]
    parts = parts + [ym[:96], yp[:96]]
    low, high = z_messages(parts)
    v_z = z_potential(v_faces[16:], v_far, v_near, v_y)
    zm, zp = sent_both(low + [told_z] + v_z, high + [told_z], "gz", send)
    rows = [xm[:64], xp[:64], xm[64:72], xp[64:72], ym[:96], yp[:96], zm[:192], zp[:192]]
    told = told_x + [ym[96:], yp[96:104], zm[192:], zp[192:200]]
    return jnp.concatenate(rows, axis=0), jnp.concatenate(told, axis=0), yp, zp


def second_exchange(exported, facing, send=passed_along):
    extra = [facing[:8]]
    low, high = y_messages([exported, facing])
    ym, yp = sent_both(low + extra, high, "gy", send)
    low, high = z_messages([exported, facing, ym, yp[:64]])
    low, high = jnp.concatenate(low, axis=0), jnp.concatenate(high, axis=0)
    zm, zp = sent_in_pairs(low, high, "gz", send)
    return jnp.concatenate([facing, ym, yp[:64], zm, zp], axis=0)


def local(boxes, anchors, potential):
    own = boxes.reshape(256, 256)
    anchor = jnp.transpose(anchors, (0, 1, 4, 2, 3))
    rows = potential.reshape(1600, 40)
    to_low, to_high = pack_call(own, anchor, rows)
    xm = passed_along(to_high, "gx", 1)
    xp = passed_along(to_low, "gx", -1)
    exported, told, v_faces, split, octant, v_own, places, table = call(
        "layout",
        layout_kernel,
        (
            shape((64, 512)),
            shape((8, 512)),
            shape((32, 512)),
            shape((256, 256)),
            shape((128, 512)),
            shape((200, 512)),
            shape((128, 128), F32),
            shape((64, 128)),
        ),
        (own, anchor, rows),
        LAYOUT,
        10**9,
    )
    cand, told, yp, zp = first_exchange(exported, told, xm, xp, v_faces)
    grid, kinetic, v_box, target, code = call(
        "ahead",
        whole_kernel(lambda *a: ahead_body(*a[:6], a[-1])),
        (
            shape((256, 512), F32),
            shape((256, 512), F32),
            shape((256, 512)),
            shape((256, 512)),
            shape((256, 128), F32),
        ),
        (split, octant, places, v_own, xm, xp, table),
        AHEAD + FIRST,
        10**9,
    )
    current, sent, facing, v_box = call(
        "first",
        whole_kernel(first_body),
        (shape((128, 512)), shape((64, 512)), shape((64, 512)), shape((128, 512))),
        (target, code, places, table, grid, kinetic, v_box, cand, told, yp, zp),
        FIRST,
        10**9,
    )
    near_rows = second_exchange(sent, facing)
    done, applied_bf, near = call(
        "second",
        whole_kernel(lambda *a: second_body(*a[:4], a[-1])),
        (shape((128, 512), F32), shape((128, 512)), shape((128, 448))),
        (current, v_box, places, told),
        SECOND + LAST,
        10**9,
    )
    (relaxed,) = call(
        "last",
        last_kernel,
        (shape((256, 256)),),
        (done, applied_bf, current, near_rows, near),
        LAST,
        10**9,
        pltpu.HBM,
        (pltpu.VMEM((256, 256), BF16), pltpu.SemaphoreType.DMA((2,))),
    )
    return relaxed.reshape(boxes.shape)


def solution(mesh):
    placed = (
        P("gx", "gy", "gz", None, None, None),
        P("gx", "gy", "gz", None, None),
        P("gx", "gy", "gz"),
    )
    return jax.shard_map(
        local,
        mesh=mesh,
        in_specs=placed,
        out_specs=P("gx", "gy", "gz", None, None, None),
        check_vma=False,
    )
```
